32 devices in a mesh: dp: 4 (over x, core), seq: 4 (over z), tensor: 2 (over y).
Axes of the slice: x: 2, y: 2, z: 4, core: 2. Of those that a mesh axis runs over, the one named last changes fastest.
Arguments:
- tokens: bfloat16 [4, 4096, 2048], P('dp', ('seq', 'tensor')), may hold values from -6 to 6
- doc_lengths: int32 [4, 8], P('dp'), may hold values from 1 to 2048, 4096 in all within a row
- w_query: bfloat16 [2048, 2048], P(None, 'tensor'), may hold values from -0.125 to 0.125
- w_key: bfloat16 [2048, 1024], P(None, 'tensor'), may hold values from -0.125 to 0.125
- w_value: bfloat16 [2048, 1024], P(None, 'tensor'), may hold values from -0.125 to 0.125
- w_out: bfloat16 [2048, 2048], P('tensor'), may hold values from -0.5 to 0.5
- w_gate: bfloat16 [2048, 6144], P(None, 'tensor'), may hold values from -0.125 to 0.125
- w_up: bfloat16 [2048, 6144], P(None, 'tensor'), may hold values from -0.125 to 0.125
- w_down: bfloat16 [6144, 2048], P('tensor'), may hold values from -0.078125 to 0.078125
- norm_attn: float32 [2048], replicated, may hold values from 0.25 to 1.75
- norm_mlp: float32 [2048], replicated, may hold values from 0.25 to 1.75
- query_norm: float32 [128], replicated, may hold values from 0.8 to 1.8
- key_norm: float32 [128], replicated, may hold values from 0.8 to 1.8
- cotangent: bfloat16 [4, 4096, 2048], P('dp', ('seq', 'tensor')), may hold values from -6 to 6
Outputs:
- output: bfloat16 [4, 4096, 2048], P('dp', ('seq', 'tensor'))
- grad_tokens: bfloat16 [4, 4096, 2048], P('dp', ('seq', 'tensor'))
- grad_w_query: float32 [2048, 2048], P(('dp', 'seq'), 'tensor')
- grad_w_key: float32 [2048, 1024], P(('dp', 'seq'), 'tensor')
- grad_w_value: float32 [2048, 1024], P(('dp', 'seq'), 'tensor')
- grad_w_out: float32 [2048, 2048], P('tensor', ('dp', 'seq'))
- grad_w_gate: float32 [2048, 6144], P(('dp', 'seq'), 'tensor')
- grad_w_up: float32 [2048, 6144], P(('dp', 'seq'), 'tensor')
- grad_w_down: float32 [6144, 2048], P('tensor', ('dp', 'seq'))
- grad_norm_attn: float32 [2048], replicated
- grad_norm_mlp: float32 [2048], replicated
- grad_query_norm: float32 [128], replicated
- grad_key_norm: float32 [128], replicated
The draws below stay inside these ranges and needn't reach their ends.
Inputs may be any that keep to these rules, and one draw needn't show every extreme that they name: `doc_lengths`: each row holds the lengths of the 8 documents of one sequence, in order; they sum to 4096, and the longest in each row is exactly 2048.
All inputs are finite; a program needn't handle non-finite values.
Results may differ from the reference program's by a relative error of at most 0.028.
Values may be sent and summed in bfloat16 or wider, within the bound.
A program may use at most 320 MiB of HBM per device.

```python
import math
from functools import partial
import jax
import jax.numpy as jnp
import numpy as np
from jax import lax

D = 2048
HQ = 16
HK = 8
HD = 128
FF = 6144
LEN = 4096
DOCS = 8
NSEQ = 4


def block_levels(rng, shape, pieces, smallest, top_value):
    def one(axis_at, parts):
        steps = jax.random.uniform(jax.random.fold_in(jax.random.fold_in(rng, 6), axis_at), (parts,), jnp.float32, smallest / len(pieces), top_value / len(pieces))
        return jnp.repeat(jnp.exp(steps), shape[axis_at] // parts).reshape((-1,) + (1,) * (len(shape) - axis_at - 1))

    factor_of = one(*pieces[0])
    for cut in pieces[1:]:
        factor_of = factor_of * one(*cut)
    return factor_of


def length_profile(count, total, reach, slope):
    portions = [(1 << 20) // math.isqrt(rank ** slope) + 1 for rank in range(2, count + 1)]
    surplus, holding = total - reach - (count - 1), [1] * (count - 1)
    while surplus > 0:
        candidates = [i for i in range(count - 1) if holding[i] < reach]
        whole, remaining = sum([portions[i] for i in candidates]), surplus
        for i in candidates:
            more = min(reach - holding[i], max(1, remaining * portions[i] // whole), surplus)
            holding[i] = holding[i] + more
            surplus = surplus - more
    return np.array([reach] + holding)


def uneven(own_key, number_of, total, bound, skew):
    if number_of == 2:
        one = jax.random.randint(own_key, (), max(1, total - bound), min(bound, total - 1) + 1)
        return jnp.stack([one, total - one])
    tallies = jnp.asarray(length_profile(number_of, total, bound, skew), jnp.int32)
    couples = (number_of - 1) // 2
    donor, receiver = tallies[1:1 + 2 * couples:2], tallies[2:2 + 2 * couples:2]
    margin = jnp.minimum(donor - 1, bound - receiver)
    shifted = jax.random.randint(jax.random.fold_in(own_key, 1), (couples,), 0, 1 << 20) % (margin + 1)
    tallies = tallies.at[1:1 + 2 * couples:2].set(donor - shifted).at[2:2 + 2 * couples:2].set(receiver + shifted)
    return tallies[jax.random.permutation(jax.random.fold_in(own_key, 2), number_of)]


def gaussian(own_key, extent, deviation, most, split=(), held_as=jnp.bfloat16):
    array = deviation * jax.random.normal(own_key, extent, jnp.float32)
    if split:
        array = array * block_levels(own_key, extent, split, -0.22, 0.18)
    return jnp.clip(array, -most, most).astype(held_as)


def setup_inputs(seed: int = 0) -> dict:
    streams_of = jax.random.split(jax.random.key(seed), 15)
    return {
        "tokens": gaussian(streams_of[0], (NSEQ, LEN, D), 1.0, 6.0, ((0, 4), (1, 8))),
        "doc_lengths": jax.vmap(lambda own: uneven(own, DOCS, LEN, LEN // 2, 2))(jax.random.split(streams_of[1], NSEQ)).reshape((NSEQ, DOCS)).astype(jnp.int32),
        "w_query": gaussian(streams_of[2], (D, HQ * HD), D ** -0.5, 0.125, ((1, 2),)),
        "w_key": gaussian(streams_of[3], (D, HK * HD), D ** -0.5, 0.125, ((1, 2),)),
        "w_value": gaussian(streams_of[4], (D, HK * HD), D ** -0.5, 0.125, ((1, 2),)),
        "w_out": gaussian(streams_of[5], (HQ * HD, D), (HQ * HD // 16) ** -0.5, 0.5, ((0, 2),)),
        "w_gate": gaussian(streams_of[6], (D, FF), D ** -0.5, 0.125, ((1, 2),)),
        "w_up": gaussian(streams_of[7], (D, FF), D ** -0.5, 0.125, ((1, 2),)),
        "w_down": gaussian(streams_of[8], (FF, D), FF ** -0.5, 0.078125, ((0, 2),)),
        "norm_attn": jnp.clip(1.0 + 0.15 * jax.random.normal(streams_of[9], (D,), jnp.float32), 0.25, 1.75),
        "norm_mlp": jnp.clip(1.0 + 0.15 * jax.random.normal(streams_of[10], (D,), jnp.float32), 0.25, 1.75),
        "query_norm": jnp.clip(jax.random.uniform(streams_of[11], (HD,), jnp.float32, 0.8, 1.8), 0.8, 1.8),
        "key_norm": jnp.clip(jax.random.uniform(streams_of[12], (HD,), jnp.float32, 0.8, 1.8), 0.8, 1.8),
        "cotangent": gaussian(streams_of[13], (NSEQ, LEN, D), 1.0, 6.0, ((0, 4), (1, 8))),
    }


@jax.custom_vjp
def low(v):
    return lax.optimization_barrier(v.astype(jnp.bfloat16)).astype(jnp.float32)

@jax.custom_vjp
def low_back(v):
    return v

def low_keep(v):
    return (low(v), None)

def low_pass(kept, grad):
    return (grad,)

def back_keep(v):
    return (v, None)

def back_low(kept, grad):
    return (low(grad),)
low.defvjp(low_keep, low_pass)
low_back.defvjp(back_keep, back_low)
eps_norm = 1e-06
rope_base = 1000000.0
mask_fill = -1e+30
highest = lax.Precision.HIGHEST

def doc_table(lengths, positions):
    doc_ends = jnp.cumsum(lengths).astype(jnp.int32)
    doc_ids = lax.optimization_barrier(jnp.sum((positions[:, None] >= doc_ends[None, :]).astype(jnp.int32), axis=1))
    starts = lax.optimization_barrier(jnp.max(jnp.where(doc_ends[None, :] <= positions[:, None], doc_ends[None, :], 0), axis=1))
    return (doc_ids, positions - starts)

def rope_tables(places):
    half_dim = HD // 2
    inverse = rope_base ** (-(jnp.arange(half_dim, dtype=jnp.float32) * 2.0 / HD))
    angles = places.astype(jnp.float32)[:, None] * inverse[None, :]
    angles = jnp.concatenate([angles, angles], axis=1)
    return (jnp.cos(angles), jnp.sin(angles))

def norm_rope(values, gain_vec, cosine, sine_rows):
    scaled = values * lax.rsqrt(lax.optimization_barrier(jnp.mean(values * values, axis=-1, keepdims=True)) + eps_norm) * gain_vec
    half_dim = scaled.shape[-1] // 2
    turned = jnp.concatenate([-scaled[..., half_dim:], scaled[..., :half_dim]], axis=-1)
    return scaled * cosine[:, None, :] + turned * sine_rows[:, None, :]

def rms_norm(values, gain_vec):
    return values * lax.rsqrt(lax.optimization_barrier(jnp.mean(values * values, axis=-1, keepdims=True)) + eps_norm) * gain_vec

def forward(tokens, w_query, w_key, w_value, w_out, w_gate, w_up, w_down, norm_attn, norm_mlp, query_norm, key_norm, doc_lengths):
    group_size = HQ // HK
    score_scale = HD ** (-0.5)
    block_rows = math.gcd(LEN, 512)
    block_count = LEN // block_rows

    def one_sequence(inputs):
        seq_tokens, seq_lengths = inputs
        positions = jnp.arange(LEN, dtype=jnp.int32)
        doc_ids, places = doc_table(seq_lengths, positions)
        cosine, sine_rows = rope_tables(places)
        attn_in = low(rms_norm(seq_tokens, norm_attn))
        q_raw = low_back(jnp.dot(attn_in, w_query, precision=highest)).reshape(LEN, HQ, HD)
        k_raw = low_back(jnp.dot(attn_in, w_key, precision=highest)).reshape(LEN, HK, HD)
        values = low(low_back(jnp.dot(attn_in, w_value, precision=highest))).reshape(LEN, HK, HD)
        queries = low(norm_rope(q_raw, query_norm, cosine, sine_rows)).reshape(LEN, HK, group_size, HD)
        key_rows = low(norm_rope(k_raw, key_norm, cosine, sine_rows))

        def attend(block_in):
            block_q, block_docs, block_pos = block_in
            scores = low_back(score_scale * jnp.einsum('qhgd,khd->hgqk', block_q, key_rows, precision=highest))
            allowed = (block_docs[:, None] == doc_ids[None, :]) & (positions[None, :] <= block_pos[:, None])
            scores = jnp.where(allowed, scores, mask_fill)
            maxima = lax.optimization_barrier(jnp.max(scores, axis=-1, keepdims=True))
            expo = jnp.exp(scores - maxima)
            weights = low(expo / lax.optimization_barrier(jnp.sum(expo, axis=-1, keepdims=True)))
            mixture = jnp.einsum('hgqk,khd->qhgd', weights, values, precision=highest)
            return mixture.reshape(block_rows, HQ * HD)
        attended = lax.map(jax.checkpoint(attend), (queries.reshape(block_count, block_rows, HK, group_size, HD), doc_ids.reshape(block_count, block_rows), positions.reshape(block_count, block_rows)))
        attended = low(low_back(attended.reshape(LEN, HQ * HD)))
        hidden_one = seq_tokens + low_back(jnp.dot(attended, w_out, precision=highest))
        mlp_in = low(rms_norm(hidden_one, norm_mlp))
        gate_vals = low_back(jnp.dot(mlp_in, w_gate, precision=highest))
        up_vals = low_back(jnp.dot(mlp_in, w_up, precision=highest))
        hidden = low(gate_vals * jax.nn.sigmoid(gate_vals) * up_vals)
        return hidden_one + low_back(jnp.dot(hidden, w_down, precision=highest))
    return lax.map(jax.checkpoint(one_sequence), (tokens, doc_lengths))

def reference(tokens, doc_lengths, w_query, w_key, w_value, w_out, w_gate, w_up, w_down, norm_attn, norm_mlp, query_norm, key_norm, cotangent):
    floats = (tokens.astype(jnp.float32), w_query.astype(jnp.float32), w_key.astype(jnp.float32), w_value.astype(jnp.float32), w_out.astype(jnp.float32), w_gate.astype(jnp.float32), w_up.astype(jnp.float32), w_down.astype(jnp.float32), norm_attn.astype(jnp.float32), norm_mlp.astype(jnp.float32), query_norm.astype(jnp.float32), key_norm.astype(jnp.float32))
    output, back_fn = jax.vjp(partial(forward, doc_lengths=doc_lengths), *floats)
    gradients = back_fn(cotangent.astype(jnp.float32))
    return (output.astype(jnp.bfloat16), gradients[0].astype(jnp.bfloat16), gradients[1], gradients[2], gradients[3], gradients[4], gradients[5], gradients[6], gradients[7], gradients[8], gradients[9], gradients[10], gradients[11])
```

```python
import functools
import math

import jax
import jax.numpy as jnp
from jax import lax
from jax.experimental import pallas as pl
from jax.experimental.pallas import tpu as pltpu
from jax.sharding import PartitionSpec as P

HD = 128
LONGEST = 2048
eps_norm = 1e-06
rope_base = 1000000.0
score_scale = HD ** (-0.5)
log2e = math.log2(math.e)
exp_scale = score_scale * log2e
BF = jnp.bfloat16
F32 = jnp.float32
MIB = 1 << 20


def params(limit=56, **kw):
    return pltpu.CompilerParams(vmem_limit_bytes=limit * MIB, **kw)


def cost(flops, bytes_accessed, transcendentals=0):
    return pl.CostEstimate(
        flops=int(flops), bytes_accessed=int(bytes_accessed), transcendentals=int(transcendentals)
    )


def dot(a, b, ca=1, cb=0):
    return lax.dot_general(a, b, (((ca,), (cb,)), ((), ())), preferred_element_type=F32)


def fixed(shape):
    zeros = (0,) * len(shape)
    return pl.BlockSpec(shape, lambda *_: zeros, pipeline_mode=pl.Buffered(1))


def grid_spec(scalars, grid, ins, outs, scratch=()):
    return pltpu.PrefetchScalarGridSpec(
        num_scalar_prefetch=scalars, grid=grid, in_specs=ins, out_specs=outs, scratch_shapes=scratch
    )


def sds(shape, dtype):
    return jax.ShapeDtypeStruct(shape, dtype)


def rms(x):
    return lax.rsqrt(jnp.mean(x * x, axis=-1, keepdims=True) + eps_norm)


def fold_rows(v):
    return jnp.sum(v.reshape(v.shape[0] // 8, 8, v.shape[1]), axis=0)


def kv_kernel(s_ref, x_ref, gain_ref, wk_ref, wv_ref, cos_ref, sin_ref, hg_ref, kv_ref, raw_ref):
    x = x_ref[...].astype(F32)
    a = (x * rms(x) * gain_ref[...]).astype(BF)
    k = dot(a, wk_ref[...])
    v = dot(a, wv_ref[...]).astype(BF)
    raw_ref[...] = k
    cosine, sine, hg = cos_ref[...], sin_ref[...], hg_ref[...]
    for h in range(k.shape[1] // HD):
        kh = k[:, h * HD : (h + 1) * HD]
        u = kh * rms(kh) * hg
        r = u * cosine + pltpu.roll(u, HD // 2, 1) * sine
        kv_ref[:, 2 * h * HD : (2 * h + 1) * HD] = r.astype(BF)
        kv_ref[:, (2 * h + 1) * HD : (2 * h + 2) * HD] = v[:, h * HD : (h + 1) * HD]


def project_kv(x, base_tile, gain, wk, wv, cosine, sine, hg, tm):
    rows, d = x.shape
    n = wk.shape[1]
    return pl.pallas_call(
        kv_kernel,
        grid_spec=grid_spec(
            1,
            (rows // tm,),
            [
                pl.BlockSpec((tm, d), lambda i, s: (i, 0)),
                fixed((1, d)),
                fixed((d, n)),
                fixed((d, n)),
                pl.BlockSpec((tm, HD), lambda i, s: (s[0] + i, 0)),
                pl.BlockSpec((tm, HD), lambda i, s: (s[0] + i, 0)),
                fixed((1, HD)),
            ],
            [
                pl.BlockSpec((tm, 2 * n), lambda i, s: (i, 0)),
                pl.BlockSpec((tm, n), lambda i, s: (i, 0)),
            ],
        ),
        out_shape=[sds((rows, 2 * n), BF), sds((rows, n), F32)],
        compiler_params=params(),
        cost_estimate=cost(4 * rows * d * n, 2 * rows * d + 4 * d * n + 8 * rows * n),
        name="project_kv",
    )(jnp.reshape(base_tile, (1,)), x, gain, wk, wv, cosine, sine, hg)


def q_kernel(
    s_ref, xa_ref, xb_ref, gain_ref, w_ref, cos_ref, sin_ref, hg_ref, x_ref, a_ref, q_ref, raw_ref,
    *, half,
):
    xin = jnp.where(pl.program_id(0) < half, xa_ref[...].astype(F32), xb_ref[...].astype(F32))
    x_ref[...] = xin.astype(BF)
    a = (xin * rms(xin) * gain_ref[...]).astype(BF)
    a_ref[...] = a
    q = dot(a, w_ref[...])
    raw_ref[...] = q
    cosine, sine, hg = cos_ref[...], sin_ref[...], hg_ref[...]
    for h in range(q.shape[1] // HD):
        qh = q[:, h * HD : (h + 1) * HD]
        u = qh * rms(qh) * hg
        r = u * cosine + pltpu.roll(u, HD // 2, 1) * sine
        q_ref[:, h * HD : (h + 1) * HD] = (r * exp_scale).astype(BF)


def project_q(xa, xb, bases, gain, w, cosine, sine, hg, tm):
    rows, d = xa.shape
    n = w.shape[1]
    half = rows // tm
    out_at = lambda i, s: (s[i // half] + i % half, 0)
    total = 2 * rows
    return pl.pallas_call(
        functools.partial(q_kernel, half=half),
        grid_spec=grid_spec(
            1,
            (2 * half,),
            [
                pl.BlockSpec((tm, d), lambda i, s: (jnp.minimum(i, half - 1), 0)),
                pl.BlockSpec((tm, d), lambda i, s: (jnp.maximum(i - half, 0), 0)),
                fixed((1, d)),
                fixed((d, n)),
                pl.BlockSpec((tm, HD), out_at),
                pl.BlockSpec((tm, HD), out_at),
                fixed((1, HD)),
            ],
            [
                pl.BlockSpec((tm, d), out_at),
                pl.BlockSpec((tm, d), out_at),
                pl.BlockSpec((tm, n), out_at),
                pl.BlockSpec((tm, n), out_at),
            ],
        ),
        out_shape=[
            sds((total, d), BF), sds((total, d), BF), sds((total, n), BF), sds((total, n), F32)
        ],
        compiler_params=params(),
        cost_estimate=cost(2 * total * d * n, 6 * total * d + 2 * d * n + 6 * total * n),
        name="project_q",
    )(bases, xa, xb, gain, w, cosine, sine, hg)


def fill_window(s_ref, at, segs, kwin, vwin):
    for n, seg in enumerate(segs):
        rows = seg.shape[0]
        base = pl.multiple_of(s_ref[at + n], math.gcd(rows, 256))
        kwin[pl.ds(base, rows), :HD] = seg[:, :HD]
        vwin[pl.ds(base, rows), :HD] = seg[:, HD:]


def flash_fwd_kernel(s_ref, q_ref, st_ref, *rest, nq, tq, tk, gs, row0, at_bases):
    segs, (o_ref, aug_ref, kwin, vwin, acc) = rest[:-5], rest[-5:]
    i = pl.program_id(1)

    @pl.when(i == 0)
    def _():
        fill_window(s_ref, at_bases, segs, kwin, vwin)
        vwin[:, HD:] = jnp.ones(vwin[:, HD:].shape, BF)

    q2 = jnp.concatenate([q_ref[:, g * HD : (g + 1) * HD] for g in range(gs)], axis=0)
    acc[...] = jnp.zeros_like(acc)
    lo, hi, flo, fhi = [s_ref[n * nq + i] for n in range(4)]

    def step(kt, masked):
        at = pl.multiple_of(kt * tk, tk)
        p = jnp.exp2(dot(q2, kwin[pl.ds(at, tk), :], 1, 1))
        if masked:
            st = st_ref[:, :1]
            j = at + lax.broadcasted_iota(jnp.int32, (tq, tk), 1)
            t = row0 + i * tq + lax.broadcasted_iota(jnp.int32, (tq, tk), 0)
            keep = (j >= st) & (j <= t)
            p = jnp.where(jnp.concatenate([keep] * gs, axis=0), p, 0.0)
        acc[...] += dot(p.astype(BF), vwin[pl.ds(at, tk), :])

    def body(kt, carry):
        inside = (kt >= flo) & (kt < fhi)

        @pl.when(inside)
        def _():
            step(kt, False)

        @pl.when(jnp.logical_not(inside))
        def _():
            step(kt, True)

        return carry

    lax.fori_loop(lo, hi, body, 0)
    total = acc[:, HD:]
    out = (acc[:, :HD] / total).astype(BF)
    neg = -jnp.log2(total)
    first = neg.astype(BF)
    rest_one = neg - first.astype(F32)
    second = rest_one.astype(BF)
    third = (rest_one - second.astype(F32)).astype(BF)
    lane = lax.broadcasted_iota(jnp.int32, total.shape, 1)
    aug = jnp.where(
        lane == 0,
        first.astype(F32),
        jnp.where(lane == 1, second.astype(F32), jnp.where(lane == 2, third.astype(F32), 0.0)),
    ).astype(BF)
    for g in range(gs):
        o_ref[:, g * HD : (g + 1) * HD] = out[g * tq : (g + 1) * tq]
        aug_ref[:, g * HD : (g + 1) * HD] = aug[g * tq : (g + 1) * tq]


def flash_fwd(scalars, q, starts_col, segs, window, chunk, rows, gs, tq, tk):
    width = gs * HD
    heads = q.shape[1] // width
    nq = rows // tq
    off = chunk * nq
    seg_specs = [pl.BlockSpec((seg.shape[0], 2 * HD), lambda h, i, s: (0, h)) for seg in segs]
    pairs = rows * (window // 2)
    return pl.pallas_call(
        functools.partial(
            flash_fwd_kernel, nq=nq, tq=tq, tk=tk, gs=gs,
            row0=window - q.shape[0] + chunk * rows, at_bases=4 * nq,
        ),
        grid_spec=grid_spec(
            1,
            (heads, nq),
            [
                pl.BlockSpec((tq, width), lambda h, i, s: (off + i, h)),
                pl.BlockSpec((tq, HD), lambda h, i, s: (off + i, 0)),
                *seg_specs,
            ],
            [
                pl.BlockSpec((tq, width), lambda h, i, s: (i, h)),
                pl.BlockSpec((tq, width), lambda h, i, s: (i, h)),
            ],
            [
                pltpu.VMEM((window, HD), BF),
                pltpu.VMEM((window, 2 * HD), BF),
                pltpu.VMEM((gs * tq, 2 * HD), F32),
            ],
        ),
        out_shape=[sds((rows, q.shape[1]), BF), sds((rows, q.shape[1]), BF)],
        compiler_params=params(),
        cost_estimate=cost(
            heads * gs * pairs * 8 * HD, 8 * q.size + sum(2 * x.size for x in segs),
            heads * gs * pairs,
        ),
        name="flash_fwd",
    )(scalars, q, starts_col, *segs)


def flash_bwd_kernel(s_ref, q_ref, st_ref, *rest, nc, ns, nb, nq, tq, tk, gs, row0, at_bases):
    das, outs, augs = rest[:nc], rest[nc : 2 * nc], rest[2 * nc : 3 * nc]
    segs = rest[3 * nc : 3 * nc + ns]
    dq_ref = rest[3 * nc + ns]
    dkvs = rest[3 * nc + ns + 1 : 3 * nc + ns + 1 + nb]
    kwin, vwin, dk, dv, dqs = rest[3 * nc + ns + 1 + nb :]
    span = dkvs[0].shape[0]

    fill_window(s_ref, at_bases, segs, kwin, vwin)
    lane = lax.broadcasted_iota(jnp.int32, (kwin.shape[0], HD), 1)
    marks = jnp.where(lane < 3, 1.0, 0.0).astype(BF)
    kwin[:, HD:] = marks
    vwin[:, HD:] = marks
    dk[...] = jnp.zeros_like(dk)
    dv[...] = jnp.zeros_like(dv)

    for i in range(nq):
        per = nq // nc
        c, r = i // per, i % per
        rows = slice(r * tq, (r + 1) * tq)
        heads = [slice(g * HD, (g + 1) * HD) for g in range(gs)]
        pile = lambda ref, rr: jnp.concatenate([ref[rr, hh] for hh in heads], axis=0)
        q2 = pile(q_ref, slice(i * tq, (i + 1) * tq))
        qa = jnp.concatenate([q2, pile(augs[c], rows)], axis=1)
        do2 = pile(das[c], rows)
        neg = -jnp.sum(
            do2.astype(F32) * pile(outs[c], rows).astype(F32), axis=1, keepdims=True
        )
        first = neg.astype(BF).astype(F32)
        second = (neg - first).astype(BF).astype(F32)
        third = neg - first - second
        ln = lax.broadcasted_iota(jnp.int32, (gs * tq, HD), 1)
        daug = jnp.where(
            ln == 0, first, jnp.where(ln == 1, second, jnp.where(ln == 2, third, 0.0))
        ).astype(BF)
        da = jnp.concatenate([do2, daug], axis=1)
        dqs[...] = jnp.zeros_like(dqs)
        lo, hi, flo, fhi = [s_ref[n * nq + i] for n in range(4)]

        def step(kt, masked, i=i, q2=q2, qa=qa, do2=do2, da=da):
            at = pl.multiple_of(kt * tk, tk)
            ka = kwin[pl.ds(at, tk), :]
            p = jnp.exp2(dot(ka, qa, 1, 1))
            if masked:
                st = st_ref[:1, i * tq : (i + 1) * tq]
                j = at + lax.broadcasted_iota(jnp.int32, (tk, tq), 0)
                t = row0 + i * tq + lax.broadcasted_iota(jnp.int32, (tk, tq), 1)
                keep = (j >= st) & (j <= t)
                p = jnp.where(jnp.concatenate([keep] * gs, axis=1), p, 0.0)
            grad = (p * dot(vwin[pl.ds(at, tk), :], da, 1, 1)).astype(BF)
            dv[pl.ds(at, tk), :] += dot(p.astype(BF), do2)
            dk[pl.ds(at, tk), :] += dot(grad, q2)
            dqs[...] += dot(grad, ka[:, :HD], 0, 0)

        def body(kt, carry, step=step, flo=flo, fhi=fhi):
            inside = (kt >= flo) & (kt < fhi)

            @pl.when(inside)
            def _():
                step(kt, False)

            @pl.when(jnp.logical_not(inside))
            def _():
                step(kt, True)

            return carry

        lax.fori_loop(lo, hi, body, 0)
        for g in range(gs):
            dq_ref[i * tq : (i + 1) * tq, heads[g]] = dqs[g * tq : (g + 1) * tq] * score_scale

    for b in range(nb):
        part = slice(b * span, (b + 1) * span)
        dkvs[b][:, :HD] = (dk[part, :] * (1.0 / log2e)).astype(BF)
        dkvs[b][:, HD:] = dv[part, :].astype(BF)


def flash_bwd(scalars, q, starts_row, das, outs, augs, segs, window, gs, tq, tk):
    span, total = q.shape
    width = gs * HD
    heads = total // width
    nc, nb, nq = len(das), window // span, span // tq
    rows = das[0].shape[0]
    chunk = pl.BlockSpec((rows, width), lambda h, s: (0, h))
    seg_specs = [pl.BlockSpec((seg.shape[0], 2 * HD), lambda h, s: (0, h)) for seg in segs]
    pairs = span * (window // 2)
    return pl.pallas_call(
        functools.partial(
            flash_bwd_kernel, nc=nc, ns=len(segs), nb=nb, nq=nq, tq=tq, tk=tk, gs=gs,
            row0=window - span, at_bases=4 * nq,
        ),
        grid_spec=grid_spec(
            1,
            (heads,),
            [
                pl.BlockSpec((span, width), lambda h, s: (0, h)),
                pl.BlockSpec((8, span), lambda h, s: (0, 0)),
                *([chunk] * (3 * nc)),
                *seg_specs,
            ],
            [
                pl.BlockSpec((span, width), lambda h, s: (0, h)),
                *([pl.BlockSpec((span, 2 * HD), lambda h, s: (0, h))] * nb),
            ],
            [
                pltpu.VMEM((window, 2 * HD), BF),
                pltpu.VMEM((window, 2 * HD), BF),
                pltpu.VMEM((window, HD), F32),
                pltpu.VMEM((window, HD), F32),
                pltpu.VMEM((gs * tq, HD), F32),
            ],
        ),
        out_shape=[sds((span, total), F32)] + [sds((span, heads * 2 * HD), BF)] * nb,
        compiler_params=params(),
        cost_estimate=cost(
            heads * gs * pairs * 14 * HD, 20 * q.size + sum(2 * x.size for x in segs),
            heads * gs * pairs,
        ),
        name="flash_bwd",
    )(scalars, q, starts_row, *das, *outs, *augs, *segs)


def mlp_kernel(*refs, np_):
    x_ref, parts = refs[0], refs[1 : 1 + np_]
    (gain_ref, cot_ref, wg_ref, wu_ref, wd_ref, m_ref, h_ref, dg_ref, du_ref, gm_ref, acc) = refs[
        1 + np_ :
    ]
    j = pl.program_id(0)

    @pl.when(j == 0)
    def _():
        rows = x_ref.shape[0]
        for r in range(0, rows, 128):
            at = slice(r, r + 128)
            h1 = x_ref[at, :].astype(F32)
            for part in parts:
                h1 = h1 + part[at, :].astype(F32)
            m_ref[at, :] = (h1 * rms(h1) * gain_ref[...]).astype(BF)

    m = m_ref[...]
    gate = dot(m, wg_ref[...])
    up = dot(m, wu_ref[...])
    gh = dot(cot_ref[...], wd_ref[...], 1, 1)
    sig = jax.nn.sigmoid(gate)
    silu = gate * sig
    h_ref[...] = (silu * up).astype(BF)
    dg = (gh * up * sig * (1.0 + gate * (1.0 - sig))).astype(BF)
    du = (gh * silu).astype(BF)
    dg_ref[...] = dg
    du_ref[...] = du
    add = dot(dg, wg_ref[...], 1, 1) + dot(du, wu_ref[...], 1, 1)

    @pl.when(j == 0)
    def _():
        acc[...] = add

    @pl.when(j > 0)
    def _():
        acc[...] += add

    @pl.when(j == pl.num_programs(0) - 1)
    def _():
        gm_ref[...] = acc[...].astype(BF)


def mlp(x, parts, cot, gain, wg, wu, wd, chunk, tf):
    rows, d = parts[0].shape
    ff = wg.shape[1]
    once = pl.Buffered(1)
    at_chunk = pl.BlockSpec((rows, d), lambda j: (chunk, 0), pipeline_mode=once)
    whole = pl.BlockSpec((rows, d), lambda j: (0, 0), pipeline_mode=once)
    tile = pl.BlockSpec((rows, tf), lambda j: (0, j))
    return pl.pallas_call(
        functools.partial(mlp_kernel, np_=len(parts)),
        grid=(ff // tf,),
        in_specs=[
            at_chunk,
            *([whole] * len(parts)),
            pl.BlockSpec((1, d), lambda j: (0, 0)),
            at_chunk,
            pl.BlockSpec((d, tf), lambda j: (0, j)),
            pl.BlockSpec((d, tf), lambda j: (0, j)),
            pl.BlockSpec((tf, d), lambda j: (j, 0)),
        ],
        out_specs=[
            pl.BlockSpec((rows, d), lambda j: (0, 0)), tile, tile, tile,
            pl.BlockSpec((rows, d), lambda j: (0, 0)),
        ],
        scratch_shapes=[pltpu.VMEM((rows, d), F32)],
        out_shape=[
            sds((rows, d), BF), sds((rows, ff), BF), sds((rows, ff), BF), sds((rows, ff), BF),
            sds((rows, d), BF),
        ],
        compiler_params=params(),
        cost_estimate=cost(10 * rows * d * ff, 6 * d * ff + 6 * rows * ff + 10 * rows * d),
        name="mlp",
    )(x, *parts, gain, cot, wg, wu, wd)


def mid_kernel(*refs, np_, ng):
    x_ref, parts, grads = refs[0], refs[1 : 1 + np_], refs[1 + np_ : 1 + np_ + ng]
    gain_ref, cot_ref, w_ref, gh_ref, ga_ref, gn_ref = refs[1 + np_ + ng :]
    h1 = x_ref[...].astype(F32)
    for part in parts:
        h1 = h1 + part[...].astype(F32)
    inv = rms(h1)
    n2 = h1 * inv
    gm = grads[0][...].astype(F32)
    for grad in grads[1:]:
        gm = gm + grad[...].astype(F32)
    g2 = gm * gain_ref[...]
    gh = cot_ref[...].astype(F32) + inv * (g2 - n2 * jnp.mean(g2 * n2, axis=1, keepdims=True))
    low = gh.astype(BF)
    gh_ref[...] = low
    ga_ref[...] = dot(low, w_ref[...], 1, 1).astype(BF)
    add = fold_rows(gm * n2)

    @pl.when(pl.program_id(0) == 0)
    def _():
        gn_ref[...] = add

    @pl.when(pl.program_id(0) > 0)
    def _():
        gn_ref[...] += add


def mid_backward(x, parts, grads, cot, gain, w_out, chunk, tm):
    rows, d = parts[0].shape
    n = w_out.shape[0]
    tiles = rows // tm
    at_chunk = pl.BlockSpec((tm, d), lambda i: (chunk * tiles + i, 0))
    tile = pl.BlockSpec((tm, d), lambda i: (i, 0))
    return pl.pallas_call(
        functools.partial(mid_kernel, np_=len(parts), ng=len(grads)),
        grid=(tiles,),
        in_specs=[
            at_chunk, *([tile] * (len(parts) + len(grads))), fixed((1, d)), at_chunk, fixed((n, d))
        ],
        out_specs=[tile, pl.BlockSpec((tm, n), lambda i: (i, 0)), pl.BlockSpec((8, d), lambda i: (0, 0))],
        out_shape=[sds((rows, d), BF), sds((rows, n), BF), sds((8, d), F32)],
        compiler_params=params(),
        cost_estimate=cost(2 * rows * d * n, 14 * rows * d + 2 * d * n),
        name="mid_backward",
    )(x, *parts, *grads, gain, cot, w_out)


def head_back(grad, raw, hg, cosine, sine):
    inv = rms(raw)
    n = raw * inv
    du = grad * cosine + pltpu.roll(grad * sine, HD // 2, 1)
    dn = du * hg
    return inv * (dn - n * jnp.mean(dn * n, axis=1, keepdims=True)), fold_rows(du * n)


def add_out(ref, value):
    @pl.when(pl.program_id(0) == 0)
    def _():
        ref[...] = value

    @pl.when(pl.program_id(0) > 0)
    def _():
        ref[...] += value


def q_back_kernel(dq_ref, raw_ref, cos_ref, sin_ref, hg_ref, low_ref, gain_ref):
    total = jnp.zeros(gain_ref.shape, F32)
    for h in range(dq_ref.shape[1] // HD):
        at = slice(h * HD, (h + 1) * HD)
        back, part = head_back(dq_ref[:, at], raw_ref[:, at], hg_ref[...], cos_ref[...], sin_ref[...])
        low_ref[:, at] = back.astype(BF)
        total = total + part
    add_out(gain_ref, total)


def q_back(dq, raw, cosine, sine, hg, tm):
    rows, n = dq.shape
    tile = pl.BlockSpec((tm, n), lambda i: (i, 0))
    table = pl.BlockSpec((tm, HD), lambda i: (i, 0))
    return pl.pallas_call(
        q_back_kernel,
        grid=(rows // tm,),
        in_specs=[tile, tile, table, table, fixed((1, HD))],
        out_specs=[tile, pl.BlockSpec((8, HD), lambda i: (0, 0))],
        out_shape=[sds((rows, n), BF), sds((8, HD), F32)],
        compiler_params=params(),
        cost_estimate=cost(30 * rows * n, 10 * rows * n),
        name="q_back",
    )(dq, raw, cosine, sine, hg)


def in_kernel(s_ref, *refs, nk):
    dkvs = refs[:nk]
    (raw_ref, dq_ref, x_ref, cos_ref, sin_ref, hg_ref, wq_ref, wk_ref, wv_ref,
     low_ref, ga_ref, gain_ref, gn_ref) = refs[nk:]
    heads = raw_ref.shape[1] // HD
    total = jnp.zeros(gain_ref.shape, F32)
    for h in range(heads):
        dk = dkvs[0][:, 2 * h * HD : (2 * h + 1) * HD].astype(F32)
        dv = dkvs[0][:, (2 * h + 1) * HD : (2 * h + 2) * HD].astype(F32)
        for ref in dkvs[1:]:
            dk = dk + ref[:, 2 * h * HD : (2 * h + 1) * HD].astype(F32)
            dv = dv + ref[:, (2 * h + 1) * HD : (2 * h + 2) * HD].astype(F32)
        at = slice(h * HD, (h + 1) * HD)
        back, part = head_back(dk, raw_ref[:, at], hg_ref[...], cos_ref[...], sin_ref[...])
        low_ref[:, at] = back.astype(BF)
        low_ref[:, (heads + h) * HD : (heads + h + 1) * HD] = dv.astype(BF)
        total = total + part
    add_out(gain_ref, total)
    low = low_ref[...]
    ga = (
        dot(dq_ref[...], wq_ref[...], 1, 1)
        + dot(low[:, : heads * HD], wk_ref[...], 1, 1)
        + dot(low[:, heads * HD :], wv_ref[...], 1, 1)
    )
    ga_ref[...] = ga.astype(BF)
    x = x_ref[...].astype(F32)
    add_out(gn_ref, fold_rows(ga * (x * rms(x))))


def in_back(dkvs, raw, dq_low, x, base_tile, cosine, sine, hg, wq, wk, wv, tm):
    rows, n = raw.shape
    d = x.shape[1]
    nq = wq.shape[1]
    moved = lambda width: pl.BlockSpec((tm, width), lambda i, s: (s[0] + i, 0))
    tile = lambda width: pl.BlockSpec((tm, width), lambda i, s: (i, 0))
    return pl.pallas_call(
        functools.partial(in_kernel, nk=len(dkvs)),
        grid_spec=grid_spec(
            1,
            (rows // tm,),
            [
                *([moved(2 * n)] * len(dkvs)), tile(n), moved(nq), moved(d), moved(HD), moved(HD),
                fixed((1, HD)), fixed((d, nq)), fixed((d, n)), fixed((d, n)),
            ],
            [
                tile(2 * n), tile(d),
                pl.BlockSpec((8, HD), lambda i, s: (0, 0)), pl.BlockSpec((8, d), lambda i, s: (0, 0)),
            ],
        ),
        out_shape=[sds((rows, 2 * n), BF), sds((rows, d), BF), sds((8, HD), F32), sds((8, d), F32)],
        compiler_params=params(),
        cost_estimate=cost(
            2 * rows * d * (nq + 2 * n), 4 * rows * d + 2 * d * (nq + 2 * n) + 12 * rows * n
        ),
        name="in_back",
    )(jnp.reshape(base_tile, (1,)), *dkvs, raw, dq_low, x, cosine, sine, hg, wq, wk, wv)


def wgrad_kernel(s_ref, *refs, nt, na, row_type, ns):
    out_ref, aside = refs[2 * nt + na], refs[2 * nt + na + 1 :]
    if row_type:
        turned = aside[0]

        @pl.when(pl.program_id(1) == 0)
        def _():
            for n in range(nt):
                turned[n] = refs[2 * n][...].T

        total = dot(turned[0], refs[1][...])
        for n in range(1, nt):
            total = total + dot(turned[n], refs[2 * n + 1][...])
    else:
        total = dot(refs[0][...], refs[1][...], 0, 0)
        for n in range(1, nt):
            total = total + dot(refs[2 * n][...], refs[2 * n + 1][...], 0, 0)
    for n in range(ns):
        if row_type:
            size = total.shape[0] // ns
            piece = total[n * size : (n + 1) * size]
        else:
            size = total.shape[1] // ns
            piece = total[:, n * size : (n + 1) * size]
        for add in refs[2 * nt : 2 * nt + na]:
            piece = piece + add[0, n].astype(F32)
        out_ref[0, n] = piece.astype(BF)


def wgrad(terms, blocks, addends, row_type, nd, ns, rows):
    nb, nt = len(blocks), len(terms)
    scalars = jnp.stack(
        [jnp.asarray(v, jnp.int32) for v in blocks]
        + [jnp.asarray(v, jnp.int32) for t in terms for v in (t[1], t[3])]
    )
    left, right = terms[0][0].shape[1], terms[0][2].shape[1]
    ins = []
    if row_type:
        bw = left // nd
        tile = min(512, right)
        steps = right // tile
        for n in range(nt):
            ins.append(pl.BlockSpec((rows, bw), lambda b, t, s, n=n: (s[nb + 2 * n], s[b])))
            ins.append(pl.BlockSpec((rows, tile), lambda b, t, s, n=n: (s[nb + 2 * n + 1], t)))
        out_dims = (ns, bw // ns, right)
        block = (1, ns, bw // ns, tile)
        at = lambda b, t, s: (b, 0, 0, t)
        add_at = lambda k: lambda b, t, s: (k, 0, 0, t)
        scratch = [pltpu.VMEM((nt, bw, rows), BF)]
        flops = 2 * nb * nt * rows * bw * right
    else:
        bw = right // nd
        tile = min(512, left)
        steps = left // tile
        for n in range(nt):
            ins.append(pl.BlockSpec((rows, tile), lambda b, t, s, n=n: (s[nb + 2 * n], t)))
            ins.append(pl.BlockSpec((rows, bw), lambda b, t, s, n=n: (s[nb + 2 * n + 1], s[b])))
        out_dims = (ns, left, bw // ns)
        block = (1, ns, tile, bw // ns)
        at = lambda b, t, s: (b, 0, t, 0)
        add_at = lambda k: lambda b, t, s: (k, 0, t, 0)
        scratch = []
        flops = 2 * nb * nt * rows * bw * left
    operands = [v for t in terms for v in (t[0], t[2])]
    for arr, k in addends:
        ins.append(pl.BlockSpec(block, add_at(k)))
        operands.append(arr)
    size = nb * math.prod(out_dims)
    return pl.pallas_call(
        functools.partial(wgrad_kernel, nt=nt, na=len(addends), row_type=row_type, ns=ns),
        grid_spec=grid_spec(1, (nb, steps), ins, pl.BlockSpec(block, at), scratch),
        out_shape=sds((nb, *out_dims), BF),
        compiler_params=params(),
        cost_estimate=cost(
            flops, 2 * size * (1 + len(addends)) + 2 * nt * rows * (left + right)
        ),
        name="wgrad",
    )(scalars, *operands)


def reduce_weights(terms, row_type, nd, ns, rows, z):
    d = lax.axis_index("dp")
    make = lambda blocks, adds: wgrad(terms, blocks, adds, row_type, nd, ns, rows)
    side = [(k, k ^ 1) for k in range(nd)]
    across = [(k, k ^ 2) for k in range(nd)]
    got = lax.ppermute(make([d ^ 1, d ^ 3], []), "dp", side)
    far = make([d ^ 2], [(got, 1)])
    near = make([d], [(got, 0)])
    come = lax.ppermute(far, "dp", across)

    def piece(j):
        j = jnp.clip(j, 0, ns - 1)
        take = lambda v: lax.dynamic_index_in_dim(v[0], j, 0, keepdims=False).astype(F32)
        return take(near) + take(come)

    total, right, left = piece(z), None, None
    for s in range(1, ns):
        send_right, send_left = piece(ns - s + z), piece(z + s - ns)
        if right is not None:
            send_right, send_left = send_right + right.astype(F32), send_left + left.astype(F32)
        right = lax.ppermute(send_right.astype(BF), "seq", [(k, k + 1) for k in range(s)])
        left = lax.ppermute(
            send_left.astype(BF), "seq", [(ns - 1 - k, ns - 2 - k) for k in range(s)]
        )
    return total + right.astype(F32) + left.astype(F32)


def final_kernel(x_ref, ga_ref, gb_ref, h0_ref, h1_ref, gain_ref, s_ref, out_ref):
    x = x_ref[...].astype(F32)
    inv = rms(x)
    n1 = x * inv
    g1 = (ga_ref[...].astype(F32) + gb_ref[...].astype(F32)) * gain_ref[...]
    gh = jnp.where(s_ref[0] == 0, h0_ref[...].astype(F32), h1_ref[...].astype(F32))
    out_ref[...] = (gh + inv * (g1 - n1 * jnp.mean(g1 * n1, axis=1, keepdims=True))).astype(BF)


def final(x, ga, gb, h0, h1, gain, y, tm):
    rows, d = x.shape
    tile = pl.BlockSpec((tm, d), lambda i: (i, 0))
    return pl.pallas_call(
        final_kernel,
        grid=(rows // tm,),
        in_specs=[tile] * 5 + [fixed((1, d)), pl.BlockSpec(memory_space=pltpu.SMEM)],
        out_specs=tile,
        out_shape=sds((rows, d), BF),
        compiler_params=params(),
        cost_estimate=cost(20 * rows * d, 12 * rows * d),
        name="final",
    )(x, ga, gb, h0, h1, gain, jnp.reshape(y, (1,)))


def per_device(
    tokens, doc_lengths, w_query, w_key, w_value, w_out, w_gate, w_up, w_down,
    norm_attn, norm_mlp, query_norm, key_norm, cotangent, *, nd, ns, nt,
):
    tokens, cotangent = tokens[0], cotangent[0]
    own_rows, d = tokens.shape
    span = own_rows * nt
    rows = span // 2
    heads_kv = w_key.shape[1] // HD
    gs = w_query.shape[1] // w_key.shape[1]
    z, y = lax.axis_index("seq"), lax.axis_index("tensor")
    row = lambda v: v[None, :]
    tm = 256
    tq, tk = 256, 512
    swap = lambda v: lax.ppermute(v, "tensor", [(0, 1), (1, 0)])
    pick = lambda a, b: jnp.where(y == 0, a, b)

    back = min(ns - 1, -(-(LONGEST - 1) // span))
    window = (back + 1) * span
    ends = jnp.cumsum(doc_lengths[0])
    positions = z * span + jnp.arange(span, dtype=jnp.int32)
    starts = jnp.max(jnp.where(ends[None, :] <= positions[:, None], ends[None, :], 0), axis=1)
    half = HD // 2
    inverse = rope_base ** (-(jnp.arange(half, dtype=F32) * 2.0 / HD))
    angles = (positions - starts).astype(F32)[:, None] * inverse[None, :]
    cosine = jnp.tile(jnp.cos(angles), (1, 2))
    sine = jnp.sin(angles)
    sine = jnp.concatenate([-sine, sine], axis=1)
    rel = jnp.clip(starts - (z - back) * span, 0, window - 1)
    starts_col = jnp.broadcast_to(rel[:, None], (span, HD))
    starts_row = jnp.broadcast_to(rel[None, :], (8, span))

    def bounds(first_row, count):
        heads = rel[first_row : first_row + count : tq]
        tails = rel[first_row + tq - 1 : first_row + count : tq]
        at = window - span + first_row + tq * jnp.arange(count // tq, dtype=jnp.int32)
        return [heads // tk, (at + tq - 1) // tk + 1, (tails + tk - 1) // tk, (at + 1) // tk]

    if nt == 2:
        other = swap(tokens)
        cot_in, other = lax.optimization_barrier((cotangent, other))
        cot_other = swap(cot_in)
        pieces, bases = [tokens, other], [y * rows, (1 - y) * rows]
        cot = jnp.concatenate([pick(cotangent, cot_other), pick(cot_other, cotangent)], axis=0)
    else:
        everything = lax.all_gather(tokens, "tensor", axis=0, tiled=True)
        cot = lax.all_gather(cotangent, "tensor", axis=0, tiled=True)
        pieces, bases = [everything[:rows], everything[rows:]], [0, rows]
    bases = [jnp.asarray(b, jnp.int32) for b in bases]
    base_tiles = [b // tm for b in bases]

    hops, raws, seg_bases = [], [], []
    ahead = [(k, k + 1) for k in range(ns - 1)]
    for x_piece, base, base_tile in zip(pieces, bases, base_tiles):
        kv, raw = project_kv(
            x_piece, base_tile, row(norm_attn), w_key, w_value, cosine, sine, row(key_norm), tm
        )
        raws.append(raw)
        for hop in range(back + 1):
            hops.append(kv)
            seg_bases.append((back - hop) * span + base)
            if hop < back:
                kv = lax.ppermute(kv, "seq", ahead)
    x_all, attn_in, query, q_raw = project_q(
        pieces[0], pieces[1], jnp.stack(base_tiles), row(norm_attn), w_query, cosine, sine,
        row(query_norm), tm,
    )

    outs, augs, parts = [], [], []
    for c in range(2):
        scalars = jnp.concatenate([*bounds(c * rows, rows), jnp.stack(seg_bases)])
        out, aug = flash_fwd(scalars, query, starts_col, hops, window, c, rows, gs, tq, tk)
        outs.append(out)
        augs.append(aug)
        partial = dot(out, w_out).astype(BF)
        parts.append([partial, swap(partial)] if nt == 2 else [lax.psum(partial, "tensor")])

    low_mlp, hidden, d_gate, d_up, grads = [], [], [], [], []
    tf = min(256, w_gate.shape[1])
    for c in range(2):
        m, h, dg, du, gm = mlp(x_all, parts[c], cot, row(norm_mlp), w_gate, w_up, w_down, c, tf)
        low_mlp.append(m)
        hidden.append(h)
        d_gate.append(dg)
        d_up.append(du)
        grads.append([gm, swap(gm)] if nt == 2 else [lax.psum(gm, "tensor")])
    shrink = functools.partial(reduce_weights, nd=nd, ns=ns, rows=rows, z=z)
    g_down = shrink([(hidden[c], 0, cot, c) for c in range(2)], False)
    g_gate = shrink([(low_mlp[c], 0, d_gate[c], 0) for c in range(2)], True)
    g_up = shrink([(low_mlp[c], 0, d_up[c], 0) for c in range(2)], True)

    gh, g_att, g_norm_two = [], [], []
    for c in range(2):
        low, ga, gn = mid_backward(x_all, parts[c], grads[c], cot, row(norm_mlp), w_out, c, tm)
        gh.append(low)
        g_att.append(ga)
        g_norm_two.append(gn)
    g_out = shrink([(outs[c], 0, gh[c], 0) for c in range(2)], False)
    scalars = jnp.concatenate([*bounds(0, span), jnp.stack(seg_bases)])
    dq, *dkvs = flash_bwd(
        scalars, query, starts_row, g_att, outs, augs, hops, window, gs, tq, tk
    )
    behind = [(k + 1, k) for k in range(ns - 1)]
    come = None
    for b in range(back):
        send = dkvs[b]
        if come is not None:
            send = (send.astype(F32) + come.astype(F32)).astype(BF)
        come = lax.ppermute(send, "seq", behind)
    dkv = [dkvs[back]] + ([come] if come is not None else [])

    dq_low, g_qn = q_back(dq, q_raw, cosine, sine, row(query_norm), tm)
    g_query = shrink([(attn_in, c, dq_low, c) for c in range(2)], True)
    lows, gas, g_kn, g_norm_one = [None] * 2, [None] * 2, [], []
    for n in (1, 0):
        lows[n], gas[n], gain_part, norm_part = in_back(
            dkv, raws[n], dq_low, x_all, base_tiles[n], cosine, sine, row(key_norm),
            w_query, w_key, w_value, tm,
        )
        g_kn.append(gain_part)
        g_norm_one.append(norm_part)
    kv_cut = heads_kv * HD
    g_kv = shrink([(attn_in, bases[n] // rows, lows[n], 0) for n in range(2)], True)

    downs = [dot(hidden[c], w_down).astype(BF) for c in range(2)]
    up32 = lambda v: v.astype(F32)
    if nt == 2:
        come_down = swap(pick(downs[1], downs[0]))
        result = up32(tokens) + up32(pick(downs[0], downs[1])) + up32(come_down)
        for n in range(2):
            result = result + up32(pick(parts[0][n], parts[1][n]))
        grad_tokens = final(tokens, gas[0], swap(gas[1]), gh[0], gh[1], row(norm_attn), y, tm)
    else:
        scatter = lambda v: lax.psum_scatter(v, "tensor", scatter_dimension=0, tiled=True)
        mine = lambda pair: lax.dynamic_slice_in_dim(
            jnp.concatenate(pair, axis=0), y * own_rows, own_rows
        )
        result = up32(tokens) + up32(scatter(jnp.concatenate(downs, axis=0)))
        result = result + up32(mine([parts[0][0], parts[1][0]]))
        x32 = up32(tokens)
        inv = rms(x32)
        n1 = x32 * inv
        g1 = up32(scatter(jnp.concatenate(gas, axis=0))) * row(norm_attn)
        moved = inv * (g1 - n1 * jnp.mean(g1 * n1, axis=1, keepdims=True))
        grad_tokens = (up32(mine(gh)) + moved).astype(BF)

    share = 1.0 / nt
    fold = lambda pair: jnp.sum(pair[0] + pair[1], axis=0)
    packed = jnp.concatenate(
        [fold(g_norm_one), fold(g_norm_two) * share, jnp.sum(g_qn, axis=0), fold(g_kn)]
    )
    packed = lax.psum(packed, ("dp", "seq", "tensor"))
    return (
        result.astype(BF)[None], grad_tokens[None], g_query, g_kv[:, :kv_cut], g_kv[:, kv_cut:],
        g_out, g_gate, g_up, g_down,
        packed[:d], packed[d : 2 * d], packed[2 * d : 2 * d + HD], packed[2 * d + HD :],
    )


def solution(mesh):
    sizes = dict(nd=mesh.shape["dp"], ns=mesh.shape["seq"], nt=mesh.shape["tensor"])
    rows, cols, both = P("dp", ("seq", "tensor"), None), P(None, "tensor"), ("dp", "seq")
    return jax.shard_map(
        functools.partial(per_device, **sizes),
        mesh=mesh,
        in_specs=(
            rows, P("dp", None), cols, cols, cols, P("tensor", None), cols, cols, P("tensor", None),
            P(), P(), P(), P(), rows,
        ),
        out_specs=(
            rows, rows, P(both, "tensor"), P(both, "tensor"), P(both, "tensor"), P("tensor", both),
            P(both, "tensor"), P(both, "tensor"), P("tensor", both), P(), P(), P(), P(),
        ),
        check_vma=False,
    )
```

```python
import functools
import math

import jax
import jax.numpy as jnp
from jax import lax
from jax.experimental import pallas as pl
from jax.experimental.pallas import tpu as pltpu
from jax.sharding import PartitionSpec as P

HD = 128
LONGEST = 2048
eps_norm = 1e-06
rope_base = 1000000.0
score_scale = HD ** (-0.5)
log2e = math.log2(math.e)
exp_scale = score_scale * log2e
BF = jnp.bfloat16
F32 = jnp.float32
MIB = 1 << 20
cost_scale = 0.4


def params(limit=56, **kw):
    return pltpu.CompilerParams(vmem_limit_bytes=limit * MIB, **kw)


def cost(us):
    return pl.CostEstimate(flops=int(us * cost_scale * 1e9), bytes_accessed=0, transcendentals=0)


def dot(a, b, ca=1, cb=0):
    return lax.dot_general(a, b, (((ca,), (cb,)), ((), ())), preferred_element_type=F32)


def fixed(shape):
    zeros = (0,) * len(shape)
    return pl.BlockSpec(shape, lambda *_: zeros, pipeline_mode=pl.Buffered(1))


def grid_spec(scalars, grid, ins, outs, scratch=()):
    return pltpu.PrefetchScalarGridSpec(
        num_scalar_prefetch=scalars, grid=grid, in_specs=ins, out_specs=outs, scratch_shapes=scratch
    )


def sds(shape, dtype):
    return jax.ShapeDtypeStruct(shape, dtype)


def rms(x):
    return lax.rsqrt(jnp.mean(x * x, axis=-1, keepdims=True) + eps_norm)


def fold_rows(v):
    return jnp.sum(v.reshape(v.shape[0] // 8, 8, v.shape[1]), axis=0)


def kv_kernel(s_ref, x_ref, gain_ref, wk_ref, wv_ref, cos_ref, sin_ref, hg_ref, kv_ref, raw_ref):
    x = x_ref[...].astype(F32)
    a = (x * rms(x) * gain_ref[...]).astype(BF)
    k = dot(a, wk_ref[...])
    v = dot(a, wv_ref[...]).astype(BF)
    raw_ref[...] = k
    cosine, sine, hg = cos_ref[...], sin_ref[...], hg_ref[...]
    for h in range(k.shape[1] // HD):
        kh = k[:, h * HD : (h + 1) * HD]
        u = kh * rms(kh) * hg
        r = u * cosine + pltpu.roll(u, HD // 2, 1) * sine
        kv_ref[:, 2 * h * HD : (2 * h + 1) * HD] = r.astype(BF)
        kv_ref[:, (2 * h + 1) * HD : (2 * h + 2) * HD] = v[:, h * HD : (h + 1) * HD]


def project_kv(x, base_tile, gain, wk, wv, cosine, sine, hg, tm):
    rows, d = x.shape
    n = wk.shape[1]
    return pl.pallas_call(
        kv_kernel,
        grid_spec=grid_spec(
            1,
            (rows // tm,),
            [
                pl.BlockSpec((tm, d), lambda i, s: (i, 0)),
                fixed((1, d)),
                fixed((d, n)),
                fixed((d, n)),
                pl.BlockSpec((tm, HD), lambda i, s: (s[0] + i, 0)),
                pl.BlockSpec((tm, HD), lambda i, s: (s[0] + i, 0)),
                fixed((1, HD)),
            ],
            [
                pl.BlockSpec((tm, 2 * n), lambda i, s: (i, 0)),
                pl.BlockSpec((tm, n), lambda i, s: (i, 0)),
            ],
        ),
        out_shape=[sds((rows, 2 * n), BF), sds((rows, n), F32)],
        compiler_params=params(),
        cost_estimate=cost(6.5),
        name="project_kv",
    )(jnp.reshape(base_tile, (1,)), x, gain, wk, wv, cosine, sine, hg)


def q_kernel(
    s_ref, xa_ref, xb_ref, gain_ref, w_ref, cos_ref, sin_ref, hg_ref, x_ref, a_ref, q_ref, raw_ref,
    *, half,
):
    xin = jnp.where(pl.program_id(0) < half, xa_ref[...].astype(F32), xb_ref[...].astype(F32))
    x_ref[...] = xin.astype(BF)
    a = (xin * rms(xin) * gain_ref[...]).astype(BF)
    a_ref[...] = a
    q = dot(a, w_ref[...])
    raw_ref[...] = q
    cosine, sine, hg = cos_ref[...], sin_ref[...], hg_ref[...]
    for h in range(q.shape[1] // HD):
        qh = q[:, h * HD : (h + 1) * HD]
        u = qh * rms(qh) * hg
        r = u * cosine + pltpu.roll(u, HD // 2, 1) * sine
        q_ref[:, h * HD : (h + 1) * HD] = (r * exp_scale).astype(BF)


def project_q(xa, xb, bases, gain, w, cosine, sine, hg, tm):
    rows, d = xa.shape
    n = w.shape[1]
    half = rows // tm
    out_at = lambda i, s: (s[i // half] + i % half, 0)
    total = 2 * rows
    return pl.pallas_call(
        functools.partial(q_kernel, half=half),
        grid_spec=grid_spec(
            1,
            (2 * half,),
            [
                pl.BlockSpec((tm, d), lambda i, s: (jnp.minimum(i, half - 1), 0)),
                pl.BlockSpec((tm, d), lambda i, s: (jnp.maximum(i - half, 0), 0)),
                fixed((1, d)),
                fixed((d, n)),
                pl.BlockSpec((tm, HD), out_at),
                pl.BlockSpec((tm, HD), out_at),
                fixed((1, HD)),
            ],
            [
                pl.BlockSpec((tm, d), out_at),
                pl.BlockSpec((tm, d), out_at),
                pl.BlockSpec((tm, n), out_at),
                pl.BlockSpec((tm, n), out_at),
            ],
        ),
        out_shape=[
            sds((total, d), BF), sds((total, d), BF), sds((total, n), BF), sds((total, n), F32)
        ],
        compiler_params=params(),
        cost_estimate=cost(13),
        name="project_q",
    )(bases, xa, xb, gain, w, cosine, sine, hg)


def fill_window(s_ref, at, segs, kwin, vwin):
    for n, seg in enumerate(segs):
        rows = seg.shape[0]
        base = pl.multiple_of(s_ref[at + n], math.gcd(rows, 256))
        kwin[pl.ds(base, rows), :HD] = seg[:, :HD]
        vwin[pl.ds(base, rows), :HD] = seg[:, HD:]


def spread(value, gs, tq):
    step = HD // gs
    return jnp.concatenate([value[:, g * step : g * step + 1] for g in range(gs)], axis=0)


def flash_fwd_kernel(s_ref, q_ref, st_ref, *rest, nseg, prior, last, nq, tq, tk, gs, w0, row0):
    segs, rest = rest[:nseg], rest[nseg:]
    acc_in, rest = rest[: 2 * prior], rest[2 * prior :]
    o_ref, l_ref, kwin, vwin, acc = rest
    i = pl.program_id(1)

    @pl.when(i == 0)
    def _():
        fill_window(s_ref, 4 * nq, segs, kwin, vwin)
        vwin[:, HD:] = jnp.ones(vwin[:, HD:].shape, BF)

    heads = [slice(g * HD, (g + 1) * HD) for g in range(gs)]
    q2 = jnp.concatenate([q_ref[:, hh] for hh in heads], axis=0)
    if prior:
        acc[:, :HD] = jnp.concatenate([acc_in[0][:, hh] for hh in heads], axis=0)
        acc[:, HD:] = jnp.broadcast_to(spread(acc_in[1], gs, tq), (gs * tq, HD))
    else:
        acc[...] = jnp.zeros_like(acc)
    lo, hi, flo, fhi = [s_ref[n * nq + i] for n in range(4)]

    def step(kt, masked):
        at = pl.multiple_of(kt * tk, tk)
        p = jnp.exp2(dot(q2, kwin[pl.ds(at, tk), :], 1, 1))
        if masked:
            st = st_ref[:, :1]
            j = w0 + at + lax.broadcasted_iota(jnp.int32, (tq, tk), 1)
            t = row0 + i * tq + lax.broadcasted_iota(jnp.int32, (tq, tk), 0)
            keep = (j >= st) & (j <= t)
            p = jnp.where(jnp.concatenate([keep] * gs, axis=0), p, 0.0)
        acc[...] += dot(p.astype(BF), vwin[pl.ds(at, tk), :])

    def body(kt, carry):
        inside = (kt >= flo) & (kt < fhi)

        @pl.when(inside)
        def _():
            step(kt, False)

        @pl.when(jnp.logical_not(inside))
        def _():
            step(kt, True)

        return carry

    lax.fori_loop(lo, hi, body, 0)
    total, out = acc[:, HD:], acc[:, :HD]
    if last:
        total = 1.0 / total
        out = (out * total).astype(BF)
    lane = lax.broadcasted_iota(jnp.int32, (tq, HD), 1)
    packed = total[:tq]
    for g in range(gs):
        o_ref[:, heads[g]] = out[g * tq : (g + 1) * tq]
        packed = jnp.where(lane >= g * (HD // gs), total[g * tq : (g + 1) * tq], packed)
    l_ref[...] = packed


def flash_fwd(bounds, bases, q, starts_col, segs, prior, window, part, row_at, rows, last, gs, tq, tk):
    width = gs * HD
    heads = q.shape[1] // width
    nq = rows // tq
    off = row_at // tq
    w0, w1 = part
    scalars = jnp.concatenate([*bounds(row_at, rows, w0, w1), jnp.stack([b - w0 for b in bases])])
    seg_specs = [pl.BlockSpec((seg.shape[0], 2 * HD), lambda h, i, s: (0, h)) for seg in segs]
    pairs = rows * (w1 - w0) // 2
    moved = lambda w: pl.BlockSpec((tq, w), lambda h, i, s: (off + i, h))
    tile = lambda w: pl.BlockSpec((tq, w), lambda h, i, s: (i, h))
    return pl.pallas_call(
        functools.partial(
            flash_fwd_kernel, nseg=len(segs), prior=len(prior) // 2, last=last, nq=nq, tq=tq,
            tk=tk, gs=gs, w0=w0, row0=window - q.shape[0] + row_at,
        ),
        grid_spec=grid_spec(
            1,
            (heads, nq),
            [
                moved(width),
                pl.BlockSpec((tq, HD), lambda h, i, s: (off + i, 0)),
                *seg_specs,
                *([moved(width), moved(HD)] if prior else []),
            ],
            [tile(width), tile(HD)],
            [
                pltpu.VMEM((w1 - w0, HD), BF),
                pltpu.VMEM((w1 - w0, 2 * HD), BF),
                pltpu.VMEM((gs * tq, 2 * HD), F32),
            ],
        ),
        out_shape=[sds((rows, q.shape[1]), BF if last else F32), sds((rows, heads * HD), F32)],
        compiler_params=params(),
        cost_estimate=cost(12 * last + 22 * (1 - last)),
        name="flash_fwd",
    )(scalars, q, starts_col, *segs, *prior)


def flash_bwd_kernel(s_ref, q_ref, st_ref, *rest, nc, ns, nb, nq, tq, tk, gs, row0):
    das, outs, sums = rest[:nc], rest[nc : 2 * nc], rest[2 * nc : 3 * nc]
    segs = rest[3 * nc : 3 * nc + ns]
    dq_ref = rest[3 * nc + ns]
    dkvs = rest[3 * nc + ns + 1 : 3 * nc + ns + 1 + nb]
    kwin, vwin, dk, dv, dqs = rest[3 * nc + ns + 1 + nb :]
    span = dkvs[0].shape[0]

    fill_window(s_ref, 4 * nq, segs, kwin, vwin)
    lane = lax.broadcasted_iota(jnp.int32, (vwin.shape[0], HD), 1)
    vwin[:, HD:] = jnp.where(lane < 2, 1.0, 0.0).astype(BF)
    dk[...] = jnp.zeros_like(dk)
    dv[...] = jnp.zeros_like(dv)

    for i in range(nq):
        per = nq // nc
        c, r = i // per, i % per
        rows = slice(r * tq, (r + 1) * tq)
        heads = [slice(g * HD, (g + 1) * HD) for g in range(gs)]
        pile = lambda ref, rr: jnp.concatenate([ref[rr, hh] for hh in heads], axis=0)
        q2 = pile(q_ref, slice(i * tq, (i + 1) * tq))
        scaled = pile(das[c], rows).astype(F32) * spread(sums[c][rows, :], gs, tq)
        neg = -jnp.sum(scaled * pile(outs[c], rows).astype(F32), axis=1, keepdims=True)
        do2 = scaled.astype(BF)
        first = neg.astype(BF).astype(F32)
        ln = lax.broadcasted_iota(jnp.int32, (gs * tq, HD), 1)
        daug = jnp.where(ln == 0, first, jnp.where(ln == 1, neg - first, 0.0)).astype(BF)
        da = jnp.concatenate([do2, daug], axis=1)
        dqs[...] = jnp.zeros_like(dqs)
        lo, hi, flo, fhi = [s_ref[n * nq + i] for n in range(4)]

        def step(kt, masked, i=i, q2=q2, do2=do2, da=da):
            at = pl.multiple_of(kt * tk, tk)
            ka = kwin[pl.ds(at, tk), :]
            p = jnp.exp2(dot(ka, q2, 1, 1))
            if masked:
                st = st_ref[:1, i * tq : (i + 1) * tq]
                j = at + lax.broadcasted_iota(jnp.int32, (tk, tq), 0)
                t = row0 + i * tq + lax.broadcasted_iota(jnp.int32, (tk, tq), 1)
                keep = (j >= st) & (j <= t)
                p = jnp.where(jnp.concatenate([keep] * gs, axis=1), p, 0.0)
            grad = (p * dot(vwin[pl.ds(at, tk), :], da, 1, 1)).astype(BF)
            dv[pl.ds(at, tk), :] += dot(p.astype(BF), do2)
            dk[pl.ds(at, tk), :] += dot(grad, q2)
            dqs[...] += dot(grad, ka, 0, 0)

        def body(kt, carry, step=step, flo=flo, fhi=fhi):
            inside = (kt >= flo) & (kt < fhi)

            @pl.when(inside)
            def _():
                step(kt, False)

            @pl.when(jnp.logical_not(inside))
            def _():
                step(kt, True)

            return carry

        lax.fori_loop(lo, hi, body, 0)
        for g in range(gs):
            dq_ref[i * tq : (i + 1) * tq, heads[g]] = dqs[g * tq : (g + 1) * tq] * score_scale

    for b in range(nb):
        part = slice(b * span, (b + 1) * span)
        dkvs[b][:, :HD] = (dk[part, :] * (1.0 / log2e)).astype(BF)
        dkvs[b][:, HD:] = dv[part, :].astype(BF)


def flash_bwd(scalars, q, starts_row, das, outs, sums, segs, window, gs, tq, tk, heads):
    span, total = q.shape
    width = gs * HD
    h0, count = heads
    nc, nb, nq = len(das), window // span, span // tq
    rows = das[0].shape[0]
    chunk = lambda w: pl.BlockSpec((rows, w), lambda h, s: (0, h0 + h))
    seg_specs = [pl.BlockSpec((seg.shape[0], 2 * HD), lambda h, s: (0, h0 + h)) for seg in segs]
    pairs = span * (window // 2)
    return pl.pallas_call(
        functools.partial(
            flash_bwd_kernel, nc=nc, ns=len(segs), nb=nb, nq=nq, tq=tq, tk=tk, gs=gs,
            row0=window - span,
        ),
        grid_spec=grid_spec(
            1,
            (count,),
            [
                pl.BlockSpec((span, width), lambda h, s: (0, h0 + h)),
                pl.BlockSpec((8, span), lambda h, s: (0, 0)),
                *([chunk(width)] * (2 * nc)),
                *([chunk(HD)] * nc),
                *seg_specs,
            ],
            [
                pl.BlockSpec((span, width), lambda h, s: (0, h)),
                *([pl.BlockSpec((span, 2 * HD), lambda h, s: (0, h))] * nb),
            ],
            [
                pltpu.VMEM((window, HD), BF),
                pltpu.VMEM((window, 2 * HD), BF),
                pltpu.VMEM((window, HD), F32),
                pltpu.VMEM((window, HD), F32),
                pltpu.VMEM((gs * tq, HD), F32),
            ],
        ),
        out_shape=[sds((span, count * width), F32)] + [sds((span, count * 2 * HD), BF)] * nb,
        compiler_params=params(),
        cost_estimate=cost(80 * count * width // total),
        name="flash_bwd",
    )(scalars, q, starts_row, *das, *outs, *sums, *segs)


def mlp_kernel(*refs, np_):
    x_ref, parts = refs[0], refs[1 : 1 + np_]
    (gain_ref, cot_ref, wg_ref, wu_ref, wd_ref, m_ref, h_ref, dg_ref, du_ref, gm_ref, acc) = refs[
        1 + np_ :
    ]
    j = pl.program_id(0)

    @pl.when(j == 0)
    def _():
        rows = x_ref.shape[0]
        for r in range(0, rows, 128):
            at = slice(r, r + 128)
            h1 = x_ref[at, :].astype(F32)
            for part in parts:
                h1 = h1 + part[at, :].astype(F32)
            m_ref[at, :] = (h1 * rms(h1) * gain_ref[...]).astype(BF)

    m = m_ref[...]
    gate = dot(m, wg_ref[...])
    up = dot(m, wu_ref[...])
    gh = dot(cot_ref[...], wd_ref[...], 1, 1)
    sig = jax.nn.sigmoid(gate)
    silu = gate * sig
    h_ref[...] = (silu * up).astype(BF)
    dg = (gh * up * sig * (1.0 + gate * (1.0 - sig))).astype(BF)
    du = (gh * silu).astype(BF)
    dg_ref[...] = dg
    du_ref[...] = du
    add = dot(dg, wg_ref[...], 1, 1) + dot(du, wu_ref[...], 1, 1)

    @pl.when(j == 0)
    def _():
        acc[...] = add

    @pl.when(j > 0)
    def _():
        acc[...] += add

    @pl.when(j == pl.num_programs(0) - 1)
    def _():
        gm_ref[...] = acc[...].astype(BF)


def mlp(x, parts, cot, gain, wg, wu, wd, chunk, tf):
    rows, d = parts[0].shape
    ff = wg.shape[1]
    once = pl.Buffered(1)
    at_chunk = pl.BlockSpec((rows, d), lambda j: (chunk, 0), pipeline_mode=once)
    whole = pl.BlockSpec((rows, d), lambda j: (0, 0), pipeline_mode=once)
    tile = pl.BlockSpec((rows, tf), lambda j: (0, j))
    return pl.pallas_call(
        functools.partial(mlp_kernel, np_=len(parts)),
        grid=(ff // tf,),
        in_specs=[
            at_chunk,
            *([whole] * len(parts)),
            pl.BlockSpec((1, d), lambda j: (0, 0)),
            at_chunk,
            pl.BlockSpec((d, tf), lambda j: (0, j)),
            pl.BlockSpec((d, tf), lambda j: (0, j)),
            pl.BlockSpec((tf, d), lambda j: (j, 0)),
        ],
        out_specs=[
            pl.BlockSpec((rows, d), lambda j: (0, 0)), tile, tile, tile,
            pl.BlockSpec((rows, d), lambda j: (0, 0)),
        ],
        scratch_shapes=[pltpu.VMEM((rows, d), F32)],
        out_shape=[
            sds((rows, d), BF), sds((rows, ff), BF), sds((rows, ff), BF), sds((rows, ff), BF),
            sds((rows, d), BF),
        ],
        compiler_params=params(),
        cost_estimate=cost(47),
        name="mlp",
    )(x, *parts, gain, cot, wg, wu, wd)


def mid_kernel(*refs, np_, ng):
    x_ref, parts, grads = refs[0], refs[1 : 1 + np_], refs[1 + np_ : 1 + np_ + ng]
    gain_ref, cot_ref, w_ref, gh_ref, ga_ref, gn_ref = refs[1 + np_ + ng :]
    h1 = x_ref[...].astype(F32)
    for part in parts:
        h1 = h1 + part[...].astype(F32)
    inv = rms(h1)
    n2 = h1 * inv
    gm = grads[0][...].astype(F32)
    for grad in grads[1:]:
        gm = gm + grad[...].astype(F32)
    g2 = gm * gain_ref[...]
    gh = cot_ref[...].astype(F32) + inv * (g2 - n2 * jnp.mean(g2 * n2, axis=1, keepdims=True))
    low = gh.astype(BF)
    gh_ref[...] = low
    ga_ref[...] = dot(low, w_ref[...], 1, 1).astype(BF)
    add = fold_rows(gm * n2)

    @pl.when(pl.program_id(0) == 0)
    def _():
        gn_ref[...] = add

    @pl.when(pl.program_id(0) > 0)
    def _():
        gn_ref[...] += add


def mid_backward(x, parts, grads, cot, gain, w_out, chunk, tm):
    rows, d = parts[0].shape
    n = w_out.shape[0]
    tiles = rows // tm
    at_chunk = pl.BlockSpec((tm, d), lambda i: (chunk * tiles + i, 0))
    tile = pl.BlockSpec((tm, d), lambda i: (i, 0))
    return pl.pallas_call(
        functools.partial(mid_kernel, np_=len(parts), ng=len(grads)),
        grid=(tiles,),
        in_specs=[
            at_chunk, *([tile] * (len(parts) + len(grads))), fixed((1, d)), at_chunk, fixed((n, d))
        ],
        out_specs=[tile, pl.BlockSpec((tm, n), lambda i: (i, 0)), pl.BlockSpec((8, d), lambda i: (0, 0))],
        out_shape=[sds((rows, d), BF), sds((rows, n), BF), sds((8, d), F32)],
        compiler_params=params(),
        cost_estimate=cost(11),
        name="mid_backward",
    )(x, *parts, *grads, gain, cot, w_out)


def head_back(grad, raw, hg, cosine, sine):
    inv = rms(raw)
    n = raw * inv
    du = grad * cosine + pltpu.roll(grad * sine, HD // 2, 1)
    dn = du * hg
    return inv * (dn - n * jnp.mean(dn * n, axis=1, keepdims=True)), fold_rows(du * n)


def add_out(ref, value):
    @pl.when(pl.program_id(0) == 0)
    def _():
        ref[...] = value

    @pl.when(pl.program_id(0) > 0)
    def _():
        ref[...] += value


def q_back_kernel(*refs, ng):
    dqs = refs[:ng]
    raw_ref, cos_ref, sin_ref, hg_ref, low_ref, gain_ref = refs[ng:]
    total = jnp.zeros(gain_ref.shape, F32)
    per = dqs[0].shape[1] // HD
    for h in range(raw_ref.shape[1] // HD):
        at, sub = slice(h * HD, (h + 1) * HD), slice(h % per * HD, (h % per + 1) * HD)
        back, part = head_back(
            dqs[h // per][:, sub], raw_ref[:, at], hg_ref[...], cos_ref[...], sin_ref[...]
        )
        low_ref[:, at] = back.astype(BF)
        total = total + part
    add_out(gain_ref, total)


def q_back(dqs, raw, cosine, sine, hg, tm):
    rows, n = raw.shape
    tile = pl.BlockSpec((tm, n), lambda i: (i, 0))
    part = pl.BlockSpec((tm, n // len(dqs)), lambda i: (i, 0))
    table = pl.BlockSpec((tm, HD), lambda i: (i, 0))
    return pl.pallas_call(
        functools.partial(q_back_kernel, ng=len(dqs)),
        grid=(rows // tm,),
        in_specs=[*([part] * len(dqs)), tile, table, table, fixed((1, HD))],
        out_specs=[tile, pl.BlockSpec((8, HD), lambda i: (0, 0))],
        out_shape=[sds((rows, n), BF), sds((8, HD), F32)],
        compiler_params=params(),
        cost_estimate=cost(8.5),
        name="q_back",
    )(*dqs, raw, cosine, sine, hg)


def in_kernel(s_ref, *refs, ng, nk):
    groups = [refs[g * nk : (g + 1) * nk] for g in range(ng)]
    (raw_ref, dq_ref, x_ref, cos_ref, sin_ref, hg_ref, wq_ref, wk_ref, wv_ref,
     low_ref, ga_ref, gain_ref, gn_ref) = refs[ng * nk :]
    heads = raw_ref.shape[1] // HD
    per = heads // ng
    total = jnp.zeros(gain_ref.shape, F32)
    for h in range(heads):
        k_at = slice(2 * (h % per) * HD, (2 * (h % per) + 1) * HD)
        v_at = slice((2 * (h % per) + 1) * HD, (2 * (h % per) + 2) * HD)
        dk, dv = 0.0, 0.0
        for ref in groups[h // per]:
            dk = dk + ref[:, k_at].astype(F32)
            dv = dv + ref[:, v_at].astype(F32)
        at = slice(h * HD, (h + 1) * HD)
        back, part = head_back(dk, raw_ref[:, at], hg_ref[...], cos_ref[...], sin_ref[...])
        low_ref[:, at] = back.astype(BF)
        low_ref[:, (heads + h) * HD : (heads + h + 1) * HD] = dv.astype(BF)
        total = total + part
    add_out(gain_ref, total)
    low = low_ref[...]
    ga = (
        dot(dq_ref[...], wq_ref[...], 1, 1)
        + dot(low[:, : heads * HD], wk_ref[...], 1, 1)
        + dot(low[:, heads * HD :], wv_ref[...], 1, 1)
    )
    ga_ref[...] = ga.astype(BF)
    x = x_ref[...].astype(F32)
    add_out(gn_ref, fold_rows(ga * (x * rms(x))))


def in_back(groups, raw, dq_low, x, base_tile, cosine, sine, hg, wq, wk, wv, tm):
    rows, n = raw.shape
    d = x.shape[1]
    nq = wq.shape[1]
    ng, nk = len(groups), len(groups[0])
    moved = lambda width: pl.BlockSpec((tm, width), lambda i, s: (s[0] + i, 0))
    tile = lambda width: pl.BlockSpec((tm, width), lambda i, s: (i, 0))
    return pl.pallas_call(
        functools.partial(in_kernel, ng=ng, nk=nk),
        grid_spec=grid_spec(
            1,
            (rows // tm,),
            [
                *([moved(2 * n // ng)] * (ng * nk)),
                tile(n), moved(nq), moved(d), moved(HD), moved(HD),
                fixed((1, HD)), fixed((d, nq)), fixed((d, n)), fixed((d, n)),
            ],
            [
                tile(2 * n), tile(d),
                pl.BlockSpec((8, HD), lambda i, s: (0, 0)), pl.BlockSpec((8, d), lambda i, s: (0, 0)),
            ],
        ),
        out_shape=[sds((rows, 2 * n), BF), sds((rows, d), BF), sds((8, HD), F32), sds((8, d), F32)],
        compiler_params=params(),
        cost_estimate=cost(12.5),
        name="in_back",
    )(
        jnp.reshape(base_tile, (1,)), *[v for g in groups for v in g], raw, dq_low, x, cosine,
        sine, hg, wq, wk, wv,
    )


def wgrad_kernel(s_ref, *refs, nt, na, cut, row_type, ns):
    outs, aside = refs[2 * nt + na : 2 * nt + na + cut], refs[2 * nt + na + cut :]
    if row_type:
        turned = aside[0]

        @pl.when(pl.program_id(1) == 0)
        def _():
            for n in range(nt):
                turned[n] = refs[2 * n][...].T

        total = dot(turned[0], refs[1][...])
        for n in range(1, nt):
            total = total + dot(turned[n], refs[2 * n + 1][...])
    else:
        total = dot(refs[0][...], refs[1][...], 0, 0)
        for n in range(1, nt):
            total = total + dot(refs[2 * n][...], refs[2 * n + 1][...], 0, 0)
    for n in range(ns):
        if row_type:
            size = total.shape[0] // ns
            piece = total[n * size : (n + 1) * size]
        else:
            size = total.shape[1] // ns
            piece = total[:, n * size : (n + 1) * size]
        adds, n_at = [], n
        for add in refs[2 * nt : 2 * nt + na]:
            if 0 <= n_at < add.shape[1]:
                adds.append(add[0, n_at])
            n_at = n if add.shape[1] == ns else n_at - add.shape[1]
        for add in adds:
            piece = piece + add.astype(F32)
        outs[n * cut // ns][0, n % (ns // cut)] = piece.astype(BF)


def after(value, *others):
    return lax.optimization_barrier((value, *others))[0]


def nought(value):
    return jnp.minimum(jnp.abs(value[:1, :1].astype(F32)), 0.0)


def wgrad(terms, blocks, addends, row_type, nd, ns, rows, behind, cut=1, done=()):
    nb, nt = len(blocks), len(terms)
    scalars = jnp.stack(
        [jnp.asarray(v, jnp.int32) for v in blocks]
        + [jnp.asarray(v(), jnp.int32) for t in terms for v in (t[1], t[3])]
    )
    scalars = after(scalars, *behind)
    for value in done:
        scalars = scalars + nought(value)[0].astype(jnp.int32)
    left, right = terms[0][0].shape[1], terms[0][2].shape[1]
    ins = []
    if row_type:
        bw = left // nd
        tile = min(512, right)
        steps = right // tile
        for n in range(nt):
            ins.append(pl.BlockSpec((rows, bw), lambda b, t, s, n=n: (s[nb + 2 * n], s[b])))
            ins.append(pl.BlockSpec((rows, tile), lambda b, t, s, n=n: (s[nb + 2 * n + 1], t)))
        out_dims = (ns, bw // ns, right)
        block = lambda n: (1, n, bw // ns, tile)
        at = lambda b, t, s: (b, 0, 0, t)
        add_at = lambda k: lambda b, t, s: (k, 0, 0, t)
        scratch = [pltpu.VMEM((nt, bw, rows), BF)]
    else:
        bw = right // nd
        tile = min(512, left)
        steps = left // tile
        for n in range(nt):
            ins.append(pl.BlockSpec((rows, tile), lambda b, t, s, n=n: (s[nb + 2 * n], t)))
            ins.append(pl.BlockSpec((rows, bw), lambda b, t, s, n=n: (s[nb + 2 * n + 1], s[b])))
        out_dims = (ns, left, bw // ns)
        block = lambda n: (1, n, tile, bw // ns)
        at = lambda b, t, s: (b, 0, t, 0)
        add_at = lambda k: lambda b, t, s: (k, 0, t, 0)
        scratch = []
    work = 2e-9 * nt * rows * left * right / nd
    operands = [v for t in terms for v in (t[0], t[2])]
    for arr, k in addends:
        ins.append(pl.BlockSpec(block(arr.shape[1]), add_at(k)))
        operands.append(arr)
    size = nb * math.prod(out_dims)
    return pl.pallas_call(
        functools.partial(wgrad_kernel, nt=nt, na=len(addends), cut=cut, row_type=row_type, ns=ns),
        grid_spec=grid_spec(
            1, (nb, steps), ins, [pl.BlockSpec(block(ns // cut), at)] * cut, scratch
        ),
        out_shape=[sds((nb, ns // cut, *out_dims[1:]), BF)] * cut,
        compiler_params=params(),
        cost_estimate=cost(1 + 3 * work),
        name="wgrad",
    )(scalars, *operands)


def flip(d, bits):
    return {1: d + 1 - 2 * (d % 2), 2: d + 2 - 4 * (d // 2), 3: 3 - d}[bits]


def wgrad_send_kernel(*refs, nt, row_type, ns, steps, tile):
    ins, out_ref = refs[: 2 * nt], refs[2 * nt]
    slots, send_sem, recv_sem = refs[2 * nt + 1 : 2 * nt + 4]
    b, t = pl.program_id(0), pl.program_id(1)
    k = b * steps + t
    last = 2 * steps - 1
    partner = {"dp": flip(lax.axis_index("dp"), 1)}

    @pl.when(k == 0)
    def _():
        barrier = pltpu.get_barrier_semaphore()
        pl.semaphore_signal(
            barrier, inc=1, device_id=partner, device_id_type=pl.DeviceIdType.MESH
        )
        pl.semaphore_wait(barrier, 1)

    def copy(src, dst, slot):
        return pltpu.make_async_remote_copy(
            src_ref=src, dst_ref=dst, send_sem=send_sem.at[slot], recv_sem=recv_sem,
            device_id=partner, device_id_type=pl.DeviceIdType.MESH,
        )

    def place(b, t):
        at = pl.ds(pl.multiple_of(t * tile, tile), tile)
        return out_ref.at[b, :, :, at] if row_type else out_ref.at[b, :, at, :]

    slot = k % 2

    @pl.when(k >= 2)
    def _():
        copy(slots.at[slot], place(b, t), slot).wait_send()

    if row_type:
        turned = refs[2 * nt + 4]

        @pl.when(t == 0)
        def _():
            for n in range(nt):
                turned[n] = ins[2 * n][...].T

        total = dot(turned[0], ins[1][...])
        for n in range(1, nt):
            total = total + dot(turned[n], ins[2 * n + 1][...])
    else:
        total = dot(ins[0][...], ins[1][...], 0, 0)
        for n in range(1, nt):
            total = total + dot(ins[2 * n][...], ins[2 * n + 1][...], 0, 0)
    size = total.shape[0 if row_type else 1] // ns
    for n in range(ns):
        piece = total[n * size : (n + 1) * size] if row_type else total[:, n * size : (n + 1) * size]
        slots[slot, n] = piece.astype(BF)
    copy(slots.at[slot], place(b, t), slot).start()

    @pl.when(k == last)
    def _():
        copy(slots.at[1 - slot], place(b, t), 1 - slot).wait_send()
        copy(slots.at[slot], place(b, t), slot).wait_send()
        copy(out_ref, out_ref, slot).wait_recv()


def wgrad_send(terms, row_type, nd, ns, rows, ident, behind):
    nt = len(terms)
    left, right = terms[0][0].shape[1], terms[0][2].shape[1]
    block = lambda b: jnp.where(
        b == 0, flip(lax.axis_index("dp"), 1), flip(lax.axis_index("dp"), 3)
    )
    ins = []
    if row_type:
        bw = left // nd
        tile = min(512, right)
        steps = right // tile
        for t in terms:
            ins.append(pl.BlockSpec((rows, bw), lambda b, s, r=t[1]: (r(), block(b))))
            ins.append(pl.BlockSpec((rows, tile), lambda b, s, r=t[3]: (r(), s)))
        out_dims, slot = (ns, bw // ns, right), (ns, bw // ns, tile)
        scratch = [pltpu.VMEM((nt, bw, rows), BF)]
    else:
        bw = right // nd
        tile = min(512, left)
        steps = left // tile
        for t in terms:
            ins.append(pl.BlockSpec((rows, tile), lambda b, s, r=t[1]: (r(), s)))
            ins.append(pl.BlockSpec((rows, bw), lambda b, s, r=t[3]: (r(), block(b))))
        out_dims, slot = (ns, left, bw // ns), (ns, tile, bw // ns)
        scratch = []
    work = 2e-9 * nt * rows * left * right / nd
    operands = [v for t in terms for v in (t[0], t[2])]
    operands[0] = after(operands[0], *behind)
    return pl.pallas_call(
        functools.partial(
            wgrad_send_kernel, nt=nt, row_type=row_type, ns=ns, steps=steps, tile=tile
        ),
        grid=(2, steps),
        in_specs=ins,
        out_specs=pl.BlockSpec(memory_space=pl.ANY),
        scratch_shapes=[
            pltpu.VMEM((2, *slot), BF), pltpu.SemaphoreType.DMA((2,)), pltpu.SemaphoreType.DMA,
            *scratch,
        ],
        out_shape=sds((2, *out_dims), BF),
        compiler_params=params(collective_id=ident, has_side_effects=True),
        cost_estimate=cost(2 + 4.4 * work),
        name="wgrad_send",
    )(*operands)


class Shrink:
    def __init__(self, terms, row_type, ahead=None, small=False, *, nd, ns, rows):
        self.small = small
        self.args, self.nd = (terms, row_type), nd
        self.ahead = ahead
        self.ident = ahead.ident + 1 if ahead else 0
        self.sizes = (nd, ns, rows)
        self.d = lax.axis_index("dp")

    def make(self, blocks, adds, behind, **more):
        terms, row_type = self.args
        return wgrad(terms, blocks, adds, row_type, *self.sizes, behind, **more)

    def send(self, *behind):
        terms, row_type = self.args
        self.got = wgrad_send(terms, row_type, *self.sizes, self.ident, behind)
        return self.got

    def far(self, *behind, done=()):
        out = self.make([self.d ^ 2], [(self.got, 1)], behind, done=done)[0]
        first = [self.ahead.ahead.come] if self.ahead and self.ahead.ahead else []
        self.come = lax.ppermute(
            after(out, *first), "dp", [(k, k ^ 2) for k in range(self.nd)]
        )
        return out

    def near(self, *behind):
        self.here = self.make([self.d], [(self.got, 0), (self.come, 0)], behind)[0]
        if not self.small:
            self.share = lax.psum_scatter(self.here[0], "seq", scatter_dimension=0)
        return self.here

    def finish(self):
        if not self.small:
            return self.share.astype(F32)
        z, ns = lax.axis_index("seq"), self.sizes[1]
        piece = lambda j: lax.dynamic_index_in_dim(self.here[0], j, 0, keepdims=False)
        first = jnp.stack([piece(z ^ 1), piece(z ^ 3)])
        first = lax.ppermute(first, "seq", [(k, k ^ 1) for k in range(ns)]).astype(F32)
        second = (piece(z ^ 2).astype(F32) + first[1]).astype(BF)
        second = lax.ppermute(second, "seq", [(k, k ^ 2) for k in range(ns)])
        return piece(z).astype(F32) + first[0] + second.astype(F32)


def final_kernel(x_ref, ga_ref, gb_ref, h0_ref, h1_ref, gain_ref, s_ref, out_ref):
    x = x_ref[...].astype(F32)
    inv = rms(x)
    n1 = x * inv
    g1 = (ga_ref[...].astype(F32) + gb_ref[...].astype(F32)) * gain_ref[...]
    gh = jnp.where(s_ref[0] == 0, h0_ref[...].astype(F32), h1_ref[...].astype(F32))
    out_ref[...] = (gh + inv * (g1 - n1 * jnp.mean(g1 * n1, axis=1, keepdims=True))).astype(BF)


def final(x, ga, gb, h0, h1, gain, y, tm):
    rows, d = x.shape
    tile = pl.BlockSpec((tm, d), lambda i: (i, 0))
    return pl.pallas_call(
        final_kernel,
        grid=(rows // tm,),
        in_specs=[tile] * 5 + [fixed((1, d)), pl.BlockSpec(memory_space=pltpu.SMEM)],
        out_specs=tile,
        out_shape=sds((rows, d), BF),
        compiler_params=params(),
        cost_estimate=cost(8),
        name="final",
    )(x, ga, gb, h0, h1, gain, jnp.reshape(y, (1,)))


def per_device(
    tokens, doc_lengths, w_query, w_key, w_value, w_out, w_gate, w_up, w_down,
    norm_attn, norm_mlp, query_norm, key_norm, cotangent, *, nd, ns, nt,
):
    tokens, cotangent = tokens[0], cotangent[0]
    own_rows, d = tokens.shape
    span = own_rows * nt
    rows = span // 2
    heads_kv = w_key.shape[1] // HD
    gs = w_query.shape[1] // w_key.shape[1]
    z, y = lax.axis_index("seq"), lax.axis_index("tensor")
    row = lambda v: v[None, :]
    tm = 256
    tq, tk = 256, 512
    swap = lambda v: lax.ppermute(v, "tensor", [(0, 1), (1, 0)])
    pick = lambda a, b: jnp.where(y == 0, a, b)

    back = min(ns - 1, -(-(LONGEST - 1) // span))
    window = (back + 1) * span
    ends = jnp.cumsum(doc_lengths[0])
    positions = z * span + jnp.arange(span, dtype=jnp.int32)
    starts = jnp.max(jnp.where(ends[None, :] <= positions[:, None], ends[None, :], 0), axis=1)
    half = HD // 2
    inverse = rope_base ** (-(jnp.arange(half, dtype=F32) * 2.0 / HD))
    angles = (positions - starts).astype(F32)[:, None] * inverse[None, :]
    cosine = jnp.tile(jnp.cos(angles), (1, 2))
    sine = jnp.sin(angles)
    sine = jnp.concatenate([-sine, sine], axis=1)
    rel = jnp.clip(starts - (z - back) * span, 0, window - 1)
    starts_col = jnp.broadcast_to(rel[:, None], (span, HD))
    starts_row = jnp.broadcast_to(rel[None, :], (8, span))

    def bounds(first_row, count, w0, w1):
        heads = rel[first_row : first_row + count : tq]
        tails = rel[first_row + tq - 1 : first_row + count : tq]
        at = window - span + first_row + tq * jnp.arange(count // tq, dtype=jnp.int32)
        inside = lambda v: jnp.clip(v - w0, 0, w1 - w0)
        up = lambda v: (v + tk - 1) // tk
        return [inside(heads) // tk, up(inside(at + tq)), up(inside(tails)), inside(at + 1) // tk]

    if nt == 2:
        other = swap(tokens)
        cot_in, other = lax.optimization_barrier((cotangent, other))
        cot_other = swap(cot_in)
        pieces, bases = [tokens, other], [y * rows, (1 - y) * rows]
        cot = jnp.concatenate([pick(cotangent, cot_other), pick(cot_other, cotangent)], axis=0)
    else:
        everything = lax.all_gather(tokens, "tensor", axis=0, tiled=True)
        cot = lax.all_gather(cotangent, "tensor", axis=0, tiled=True)
        pieces, bases = [everything[:rows], everything[rows:]], [0, rows]
    bases = [jnp.asarray(b, jnp.int32) for b in bases]
    base_tiles = [b // tm for b in bases]

    segs, seg_bases = [[] for _ in range(back + 1)], [[] for _ in range(back + 1)]
    raws = []
    ahead = [(k, k + 1) for k in range(ns - 1)]
    for x_piece, base, base_tile in zip(pieces, bases, base_tiles):
        kv, raw = project_kv(
            x_piece, base_tile, row(norm_attn), w_key, w_value, cosine, sine, row(key_norm), tm
        )
        raws.append(raw)
        for hop in range(back + 1):
            segs[hop].append(kv)
            seg_bases[hop].append((back - hop) * span + base)
            if hop < back:
                kv = lax.ppermute(kv, "seq", ahead)
    x_all, attn_in, query, q_raw = project_q(
        pieces[0], pieces[1], jnp.stack(base_tiles), row(norm_attn), w_query, cosine, sine,
        row(query_norm), tm,
    )

    attend = functools.partial(flash_fwd, bounds, gs=gs, tq=tq, tk=tk, window=window)
    prior = []
    for hop in range(back):
        part = ((back - hop) * span, (back - hop + 1) * span)
        prior = attend(
            seg_bases[hop], query, starts_col, segs[hop], prior, part=part, row_at=0, rows=span,
            last=False,
        )
    outs, sums, parts = [], [], []
    for c in range(2):
        out, total = attend(
            seg_bases[back], query, after(starts_col, *outs), segs[back], prior, part=(0, span),
            row_at=c * rows, rows=rows, last=True,
        )
        outs.append(out)
        sums.append(total)
        partial = dot(out, w_out).astype(BF)
        parts.append([partial, swap(partial)] if nt == 2 else [lax.psum(partial, "tensor")])

    low_mlp, hidden, d_gate, d_up, grads = [], [], [], [], []
    tf = min(512, w_gate.shape[1] // 2)
    for c in range(2):
        m, h, dg, du, gm = mlp(
            x_all, parts[c], cot, after(row(norm_mlp), *low_mlp), w_gate, w_up, w_down, c, tf
        )
        low_mlp.append(m)
        hidden.append(h)
        d_gate.append(dg)
        d_up.append(du)
        grads.append([gm, swap(gm)] if nt == 2 else [lax.psum(gm, "tensor")])

    shrink = functools.partial(Shrink, nd=nd, ns=ns, rows=rows)
    zero = lambda: 0
    chunk = lambda c: lambda: c
    down = shrink([(hidden[c], zero, cot, chunk(c)) for c in range(2)], False)
    gate = shrink([(low_mlp[c], zero, d_gate[c], zero) for c in range(2)], True, down)
    up = shrink([(low_mlp[c], zero, d_up[c], zero) for c in range(2)], True, gate)
    gh, g_att, g_norm_two = [], [], []

    def middle(c, *behind):
        low, ga, gn = mid_backward(
            x_all, parts[c], grads[c], cot, after(row(norm_mlp), *behind), w_out, c, tm
        )
        gh.append(low)
        g_att.append(ga)
        g_norm_two.append(gn)
        return low

    down.send()
    middle(0)
    middle(1, gh[0], gate.send(down.far()))
    t = []
    hop_segs = [v for seg in segs for v in seg]
    hop_bases = jnp.stack([v for b in seg_bases for v in b])
    scalars = jnp.concatenate([*bounds(0, span, 0, window), hop_bases])
    halves = [(0, heads_kv)] if heads_kv == 1 else [(0, heads_kv // 2), (heads_kv // 2, heads_kv // 2)]
    behind = [(k + 1, k) for k in range(ns - 1)]
    dqs, dkvs = [], []
    for part, heads in enumerate(halves):
        dq, *dkv = flash_bwd(
            after(scalars, *t), query, starts_row, g_att, outs, sums, hop_segs, window, gs, tq, tk,
            heads,
        )
        come = None
        for b in range(back):
            send = dkv[b]
            if come is not None:
                send = (send.astype(F32) + come.astype(F32)).astype(BF)
            come = lax.ppermute(send, "seq", behind)
        dqs.append(dq)
        dkvs.append([dkv[back]] + ([come] if come is not None else []))
        if part == 0:
            t = [gate.far(gh[1]), down.near(dq)]
    out_w = shrink([(outs[c], zero, gh[c], zero) for c in range(2)], False, up, True)
    t = up.far(gate.near(up.send(*dqs)))
    dq_low, g_qn = q_back(dqs, q_raw, cosine, sine, after(row(query_norm), t), tm)
    query_w = shrink([(attn_in, chunk(c), dq_low, chunk(c)) for c in range(2)], True, out_w, True)
    t = out_w.far(out_w.send(dq_low))
    t = query_w.far(query_w.send(t))
    w_down_later = after(w_down, dq_low)
    downs = [dot(hidden[c], w_down_later).astype(BF) for c in range(2)]
    t = [t, *downs]

    lows, gas, g_kn, g_norm_one = [None] * 2, [None] * 2, [], []
    for n in (1, 0):
        lows[n], gas[n], gain_part, norm_part = in_back(
            dkvs, raws[n], dq_low, x_all, base_tiles[n], cosine, sine, after(row(key_norm) + nought(down.share), *t),
            w_query, w_key, w_value, tm,
        )
        g_kn.append(gain_part)
        g_norm_one.append(norm_part)
    kv_cut = heads_kv * HD
    own_half = lambda: lax.axis_index("tensor")
    half_of = lambda n: chunk(n) if nt != 2 else own_half if n == 0 else lambda: 1 - own_half()
    kv_w = shrink([(attn_in, half_of(n), lows[n], zero) for n in range(2)], True, query_w, True)
    kv_w.send()
    t = up.near(kv_w.far(done=[gate.share]))
    t = query_w.near(out_w.near(t))
    kv_w.near(t)
    g_down, g_gate, g_up, g_out, g_query, g_kv = [
        v.finish() for v in (down, gate, up, out_w, query_w, kv_w)
    ]

    up32 = lambda v: v.astype(F32)
    if nt == 2:
        come_down = swap(pick(downs[1], downs[0]))
        result = up32(tokens) + up32(pick(downs[0], downs[1])) + up32(come_down)
        for n in range(2):
            result = result + up32(pick(parts[0][n], parts[1][n]))
        grad_tokens = final(tokens, gas[0], swap(gas[1]), gh[0], gh[1], row(norm_attn), y, tm)
    else:
        scatter = lambda v: lax.psum_scatter(v, "tensor", scatter_dimension=0, tiled=True)
        mine = lambda pair: lax.dynamic_slice_in_dim(
            jnp.concatenate(pair, axis=0), y * own_rows, own_rows
        )
        result = up32(tokens) + up32(scatter(jnp.concatenate(downs, axis=0)))
        result = result + up32(mine([parts[0][0], parts[1][0]]))
        x32 = up32(tokens)
        inv = rms(x32)
        n1 = x32 * inv
        g1 = up32(scatter(jnp.concatenate(gas, axis=0))) * row(norm_attn)
        moved = inv * (g1 - n1 * jnp.mean(g1 * n1, axis=1, keepdims=True))
        grad_tokens = (up32(mine(gh)) + moved).astype(BF)

    share = 1.0 / nt
    fold = lambda pair: jnp.sum(pair[0] + pair[1], axis=0)
    axes = (("dp", nd), ("seq", ns), ("tensor", nt))
    packed = jnp.concatenate(
        [fold(g_norm_one), fold(g_norm_two) * share, jnp.sum(g_qn, axis=0), fold(g_kn)]
    )
    packed = total_sum(packed, axes)
    return (
        result.astype(BF)[None], grad_tokens[None], g_query, g_kv[:, :kv_cut], g_kv[:, kv_cut:],
        g_out, g_gate, g_up, g_down,
        packed[:d], packed[d : 2 * d], packed[2 * d : 2 * d + HD], packed[2 * d + HD :],
    )


def total_sum(v, sizes):
    for name, size in sizes:
        step = 1
        while step < size:
            v = v + lax.ppermute(v, name, [(k, k ^ step) for k in range(size)])
            step *= 2
    return v


def solution(mesh):
    sizes = dict(nd=mesh.shape["dp"], ns=mesh.shape["seq"], nt=mesh.shape["tensor"])
    rows, cols, both = P("dp", ("seq", "tensor"), None), P(None, "tensor"), ("dp", "seq")
    return jax.shard_map(
        functools.partial(per_device, **sizes),
        mesh=mesh,
        in_specs=(
            rows, P("dp", None), cols, cols, cols, P("tensor", None), cols, cols, P("tensor", None),
            P(), P(), P(), P(), rows,
        ),
        out_specs=(
            rows, rows, P(both, "tensor"), P(both, "tensor"), P(both, "tensor"), P("tensor", both),
            P(both, "tensor"), P(both, "tensor"), P("tensor", both), P(), P(), P(), P(),
        ),
        check_vma=False,
    )
```

```python
import functools
import math

import jax
import jax.numpy as jnp
from jax import lax
from jax.experimental import pallas as pl
from jax.experimental.pallas import tpu as pltpu
from jax.sharding import PartitionSpec as P

HD = 128
LONGEST = 2048
eps_norm = 1e-06
rope_base = 1000000.0
score_scale = HD ** (-0.5)
log2e = math.log2(math.e)
exp_scale = score_scale * log2e
BF = jnp.bfloat16
F32 = jnp.float32
MIB = 1 << 20
PLAN = {
    "c_mid": 1.0,
    "e_dn_d0": 1,
    "e_dp_q": 1,
    "e_fb0_gf": 1,
    "e_fb1_gf": 1,
    "e_fb1_uf": 1,
    "e_fin_qn": 1,
    "e_gn_d1": 1,
    "e_in_cd": 1,
    "e_in_dp": 1,
    "e_in_qf": 1,
    "e_in_un": 1,
    "e_kf_un": 1,
    "e_m1_gf": 1,
    "e_m1_m0": 1,
    "e_on_kf": 1,
    "e_pk_fin": 1,
    "e_pk_kc": 1,
    "e_pk_kn": 1,
    "e_qb_gn": 1,
    "e_qb_uf": 1,
    "e_qf_of": 1,
    "e_qn_on": 1,
    "scale": 0.7,
    "serial": 1,
}


def O(key, default=0):
    return PLAN.get(key, default)


cost_scale = O("scale", 0.4)


def params(limit=56, **kw):
    return pltpu.CompilerParams(vmem_limit_bytes=limit * MIB, **kw)


def cost(us):
    return pl.CostEstimate(flops=int(us * cost_scale * 1e9), bytes_accessed=0, transcendentals=0)


def dot(a, b, ca=1, cb=0):
    return lax.dot_general(a, b, (((ca,), (cb,)), ((), ())), preferred_element_type=F32)


def fixed(shape):
    zeros = (0,) * len(shape)
    return pl.BlockSpec(shape, lambda *_: zeros, pipeline_mode=pl.Buffered(1))


def grid_spec(scalars, grid, ins, outs, scratch=()):
    return pltpu.PrefetchScalarGridSpec(
        num_scalar_prefetch=scalars, grid=grid, in_specs=ins, out_specs=outs, scratch_shapes=scratch
    )


def sds(shape, dtype):
    return jax.ShapeDtypeStruct(shape, dtype)


def rms(x):
    return lax.rsqrt(jnp.mean(x * x, axis=-1, keepdims=True) + eps_norm)


def fold_rows(v):
    return jnp.sum(v.reshape(v.shape[0] // 8, 8, v.shape[1]), axis=0)


def kv_kernel(s_ref, x_ref, gain_ref, wk_ref, wv_ref, cos_ref, sin_ref, hg_ref, kv_ref, raw_ref):
    x = x_ref[...].astype(F32)
    a = (x * rms(x) * gain_ref[...]).astype(BF)
    k = dot(a, wk_ref[...])
    v = dot(a, wv_ref[...]).astype(BF)
    raw_ref[...] = k
    cosine, sine, hg = cos_ref[...], sin_ref[...], hg_ref[...]
    for h in range(k.shape[1] // HD):
        kh = k[:, h * HD : (h + 1) * HD]
        u = kh * rms(kh) * hg
        r = u * cosine + pltpu.roll(u, HD // 2, 1) * sine
        kv_ref[:, 2 * h * HD : (2 * h + 1) * HD] = r.astype(BF)
        kv_ref[:, (2 * h + 1) * HD : (2 * h + 2) * HD] = v[:, h * HD : (h + 1) * HD]


def project_kv(x, base_tile, gain, wk, wv, cosine, sine, hg, tm):
    rows, d = x.shape
    n = wk.shape[1]
    return pl.pallas_call(
        kv_kernel,
        grid_spec=grid_spec(
            1,
            (rows // tm,),
            [
                pl.BlockSpec((tm, d), lambda i, s: (i, 0)),
                fixed((1, d)),
                fixed((d, n)),
                fixed((d, n)),
                pl.BlockSpec((tm, HD), lambda i, s: (s[0] + i, 0)),
                pl.BlockSpec((tm, HD), lambda i, s: (s[0] + i, 0)),
                fixed((1, HD)),
            ],
            [
                pl.BlockSpec((tm, 2 * n), lambda i, s: (i, 0)),
                pl.BlockSpec((tm, n), lambda i, s: (i, 0)),
            ],
        ),
        out_shape=[sds((rows, 2 * n), BF), sds((rows, n), F32)],
        compiler_params=params(),
        cost_estimate=cost(6.5),
        name="project_kv",
    )(jnp.reshape(base_tile, (1,)), x, gain, wk, wv, cosine, sine, hg)


def q_kernel(
    s_ref, xa_ref, xb_ref, gain_ref, w_ref, cos_ref, sin_ref, hg_ref, x_ref, a_ref, q_ref, raw_ref,
    *, half,
):
    xin = jnp.where(pl.program_id(0) < half, xa_ref[...].astype(F32), xb_ref[...].astype(F32))
    x_ref[...] = xin.astype(BF)
    a = (xin * rms(xin) * gain_ref[...]).astype(BF)
    a_ref[...] = a
    q = dot(a, w_ref[...])
    raw_ref[...] = q
    cosine, sine, hg = cos_ref[...], sin_ref[...], hg_ref[...]
    for h in range(q.shape[1] // HD):
        qh = q[:, h * HD : (h + 1) * HD]
        u = qh * rms(qh) * hg
        r = u * cosine + pltpu.roll(u, HD // 2, 1) * sine
        q_ref[:, h * HD : (h + 1) * HD] = (r * exp_scale).astype(BF)


def project_q(xa, xb, bases, gain, w, cosine, sine, hg, tm):
    rows, d = xa.shape
    n = w.shape[1]
    half = rows // tm
    out_at = lambda i, s: (s[i // half] + i % half, 0)
    total = 2 * rows
    return pl.pallas_call(
        functools.partial(q_kernel, half=half),
        grid_spec=grid_spec(
            1,
            (2 * half,),
            [
                pl.BlockSpec((tm, d), lambda i, s: (jnp.minimum(i, half - 1), 0)),
                pl.BlockSpec((tm, d), lambda i, s: (jnp.maximum(i - half, 0), 0)),
                fixed((1, d)),
                fixed((d, n)),
                pl.BlockSpec((tm, HD), out_at),
                pl.BlockSpec((tm, HD), out_at),
                fixed((1, HD)),
            ],
            [
                pl.BlockSpec((tm, d), out_at),
                pl.BlockSpec((tm, d), out_at),
                pl.BlockSpec((tm, n), out_at),
                pl.BlockSpec((tm, n), out_at),
            ],
        ),
        out_shape=[
            sds((total, d), BF), sds((total, d), BF), sds((total, n), BF), sds((total, n), F32)
        ],
        compiler_params=params(),
        cost_estimate=cost(13),
        name="project_q",
    )(bases, xa, xb, gain, w, cosine, sine, hg)


def fill_window(s_ref, at, segs, kwin, vwin):
    for n, seg in enumerate(segs):
        rows = seg.shape[0]
        base = pl.multiple_of(s_ref[at + n], math.gcd(rows, 256))
        kwin[pl.ds(base, rows), :HD] = seg[:, :HD]
        vwin[pl.ds(base, rows), :HD] = seg[:, HD:]


def spread(value, gs, tq):
    step = HD // gs
    return jnp.concatenate([value[:, g * step : g * step + 1] for g in range(gs)], axis=0)


def flash_fwd_kernel(s_ref, q_ref, st_ref, *rest, nseg, prior, last, nq, tq, tk, gs, w0, row0):
    segs, rest = rest[:nseg], rest[nseg:]
    acc_in, rest = rest[: 2 * prior], rest[2 * prior :]
    o_ref, l_ref, kwin, vwin, acc = rest
    i = pl.program_id(1)

    @pl.when(i == 0)
    def _():
        fill_window(s_ref, 4 * nq, segs, kwin, vwin)
        vwin[:, HD:] = jnp.ones(vwin[:, HD:].shape, BF)

    heads = [slice(g * HD, (g + 1) * HD) for g in range(gs)]
    q2 = jnp.concatenate([q_ref[:, hh] for hh in heads], axis=0)
    if prior:
        acc[:, :HD] = jnp.concatenate([acc_in[0][:, hh] for hh in heads], axis=0)
        acc[:, HD:] = jnp.broadcast_to(spread(acc_in[1], gs, tq), (gs * tq, HD))
    else:
        acc[...] = jnp.zeros_like(acc)
    lo, hi, flo, fhi = [s_ref[n * nq + i] for n in range(4)]

    def step(kt, masked):
        at = pl.multiple_of(kt * tk, tk)
        p = jnp.exp2(dot(q2, kwin[pl.ds(at, tk), :], 1, 1))
        if masked:
            st = st_ref[:, :1]
            j = w0 + at + lax.broadcasted_iota(jnp.int32, (tq, tk), 1)
            t = row0 + i * tq + lax.broadcasted_iota(jnp.int32, (tq, tk), 0)
            keep = (j >= st) & (j <= t)
            p = jnp.where(jnp.concatenate([keep] * gs, axis=0), p, 0.0)
        acc[...] += dot(p.astype(BF), vwin[pl.ds(at, tk), :])

    def body(kt, carry):
        inside = (kt >= flo) & (kt < fhi)

        @pl.when(inside)
        def _():
            step(kt, False)

        @pl.when(jnp.logical_not(inside))
        def _():
            step(kt, True)

        return carry

    lax.fori_loop(lo, hi, body, 0)
    total, out = acc[:, HD:], acc[:, :HD]
    if last:
        total = 1.0 / total
        out = (out * total).astype(BF)
    lane = lax.broadcasted_iota(jnp.int32, (tq, HD), 1)
    packed = total[:tq]
    for g in range(gs):
        o_ref[:, heads[g]] = out[g * tq : (g + 1) * tq]
        packed = jnp.where(lane >= g * (HD // gs), total[g * tq : (g + 1) * tq], packed)
    l_ref[...] = packed


def flash_fwd(bounds, bases, q, starts_col, segs, prior, window, part, row_at, rows, last, gs, tq, tk):
    width = gs * HD
    heads = q.shape[1] // width
    nq = rows // tq
    off = row_at // tq
    w0, w1 = part
    scalars = jnp.concatenate([*bounds(row_at, rows, w0, w1), jnp.stack([b - w0 for b in bases])])
    seg_specs = [pl.BlockSpec((seg.shape[0], 2 * HD), lambda h, i, s: (0, h)) for seg in segs]
    pairs = rows * (w1 - w0) // 2
    moved = lambda w: pl.BlockSpec((tq, w), lambda h, i, s: (off + i, h))
    tile = lambda w: pl.BlockSpec((tq, w), lambda h, i, s: (i, h))
    return pl.pallas_call(
        functools.partial(
            flash_fwd_kernel, nseg=len(segs), prior=len(prior) // 2, last=last, nq=nq, tq=tq,
            tk=tk, gs=gs, w0=w0, row0=window - q.shape[0] + row_at,
        ),
        grid_spec=grid_spec(
            1,
            (heads, nq),
            [
                moved(width),
                pl.BlockSpec((tq, HD), lambda h, i, s: (off + i, 0)),
                *seg_specs,
                *([moved(width), moved(HD)] if prior else []),
            ],
            [tile(width), tile(HD)],
            [
                pltpu.VMEM((w1 - w0, HD), BF),
                pltpu.VMEM((w1 - w0, 2 * HD), BF),
                pltpu.VMEM((gs * tq, 2 * HD), F32),
            ],
        ),
        out_shape=[sds((rows, q.shape[1]), BF if last else F32), sds((rows, heads * HD), F32)],
        compiler_params=params(),
        cost_estimate=cost(7 * last + 19 * (1 - last)),
        name="flash_fwd",
    )(scalars, q, starts_col, *segs, *prior)


def flash_bwd_kernel(s_ref, q_ref, st_ref, *rest, nc, ns, nb, nq, tq, tk, gs, row0):
    das, outs, sums = rest[:nc], rest[nc : 2 * nc], rest[2 * nc : 3 * nc]
    segs = rest[3 * nc : 3 * nc + ns]
    dq_ref = rest[3 * nc + ns]
    dkvs = rest[3 * nc + ns + 1 : 3 * nc + ns + 1 + nb]
    kwin, vwin, dk, dv, dqs = rest[3 * nc + ns + 1 + nb :]
    span = dkvs[0].shape[0]

    fill_window(s_ref, 4 * nq, segs, kwin, vwin)
    lane = lax.broadcasted_iota(jnp.int32, (vwin.shape[0], HD), 1)
    vwin[:, HD:] = jnp.where(lane < 2, 1.0, 0.0).astype(BF)
    dk[...] = jnp.zeros_like(dk)
    dv[...] = jnp.zeros_like(dv)

    for i in range(nq):
        per = nq // nc
        c, r = i // per, i % per
        rows = slice(r * tq, (r + 1) * tq)
        heads = [slice(g * HD, (g + 1) * HD) for g in range(gs)]
        pile = lambda ref, rr: jnp.concatenate([ref[rr, hh] for hh in heads], axis=0)
        q2 = pile(q_ref, slice(i * tq, (i + 1) * tq))
        scaled = pile(das[c], rows).astype(F32) * spread(sums[c][rows, :], gs, tq)
        neg = -jnp.sum(scaled * pile(outs[c], rows).astype(F32), axis=1, keepdims=True)
        do2 = scaled.astype(BF)
        first = neg.astype(BF).astype(F32)
        ln = lax.broadcasted_iota(jnp.int32, (gs * tq, HD), 1)
        daug = jnp.where(ln == 0, first, jnp.where(ln == 1, neg - first, 0.0)).astype(BF)
        da = jnp.concatenate([do2, daug], axis=1)
        dqs[...] = jnp.zeros_like(dqs)
        lo, hi, flo, fhi = [s_ref[n * nq + i] for n in range(4)]

        def step(kt, masked, i=i, q2=q2, do2=do2, da=da):
            at = pl.multiple_of(kt * tk, tk)
            ka = kwin[pl.ds(at, tk), :]
            p = jnp.exp2(dot(ka, q2, 1, 1))
            if masked:
                st = st_ref[:1, i * tq : (i + 1) * tq]
                j = at + lax.broadcasted_iota(jnp.int32, (tk, tq), 0)
                t = row0 + i * tq + lax.broadcasted_iota(jnp.int32, (tk, tq), 1)
                keep = (j >= st) & (j <= t)
                p = jnp.where(jnp.concatenate([keep] * gs, axis=1), p, 0.0)
            grad = (p * dot(vwin[pl.ds(at, tk), :], da, 1, 1)).astype(BF)
            dv[pl.ds(at, tk), :] += dot(p.astype(BF), do2)
            dk[pl.ds(at, tk), :] += dot(grad, q2)
            dqs[...] += dot(grad, ka, 0, 0)

        def body(kt, carry, step=step, flo=flo, fhi=fhi):
            inside = (kt >= flo) & (kt < fhi)

            @pl.when(inside)
            def _():
                step(kt, False)

            @pl.when(jnp.logical_not(inside))
            def _():
                step(kt, True)

            return carry

        lax.fori_loop(lo, hi, body, 0)
        for g in range(gs):
            dq_ref[i * tq : (i + 1) * tq, heads[g]] = dqs[g * tq : (g + 1) * tq] * score_scale

    for b in range(nb):
        part = slice(b * span, (b + 1) * span)
        dkvs[b][:, :HD] = (dk[part, :] * (1.0 / log2e)).astype(BF)
        dkvs[b][:, HD:] = dv[part, :].astype(BF)


def flash_bwd(scalars, q, starts_row, das, outs, sums, segs, window, gs, tq, tk, heads):
    span, total = q.shape
    width = gs * HD
    h0, count = heads
    nc, nb, nq = len(das), window // span, span // tq
    rows = das[0].shape[0]
    chunk = lambda w: pl.BlockSpec((rows, w), lambda h, s: (0, h0 + h))
    seg_specs = [pl.BlockSpec((seg.shape[0], 2 * HD), lambda h, s: (0, h0 + h)) for seg in segs]
    pairs = span * (window // 2)
    return pl.pallas_call(
        functools.partial(
            flash_bwd_kernel, nc=nc, ns=len(segs), nb=nb, nq=nq, tq=tq, tk=tk, gs=gs,
            row0=window - span,
        ),
        grid_spec=grid_spec(
            1,
            (count,),
            [
                pl.BlockSpec((span, width), lambda h, s: (0, h0 + h)),
                pl.BlockSpec((8, span), lambda h, s: (0, 0)),
                *([chunk(width)] * (2 * nc)),
                *([chunk(HD)] * nc),
                *seg_specs,
            ],
            [
                pl.BlockSpec((span, width), lambda h, s: (0, h)),
                *([pl.BlockSpec((span, 2 * HD), lambda h, s: (0, h))] * nb),
            ],
            [
                pltpu.VMEM((window, HD), BF),
                pltpu.VMEM((window, 2 * HD), BF),
                pltpu.VMEM((window, HD), F32),
                pltpu.VMEM((window, HD), F32),
                pltpu.VMEM((gs * tq, HD), F32),
            ],
        ),
        out_shape=[sds((span, count * width), F32)] + [sds((span, count * 2 * HD), BF)] * nb,
        compiler_params=params(),
        cost_estimate=cost(O('c_fb', 1.0) * 72 * count * width // total),
        name="flash_bwd",
    )(scalars, q, starts_row, *das, *outs, *sums, *segs)


def mlp_kernel(*refs, np_):
    x_ref, parts = refs[0], refs[1 : 1 + np_]
    gain_ref, gh_ref, wg_ref, wu_ref, m_ref, h_ref, dg_ref, du_ref, gm_ref, acc = refs[1 + np_ :]
    j = pl.program_id(0)

    @pl.when(j == 0)
    def _():
        rows = x_ref.shape[0]
        for r in range(0, rows, 128):
            at = slice(r, r + 128)
            h1 = x_ref[at, :].astype(F32)
            for part in parts:
                h1 = h1 + part[at, :].astype(F32)
            m_ref[at, :] = (h1 * rms(h1) * gain_ref[...]).astype(BF)
        acc[...] = jnp.zeros_like(acc)

    m = m_ref[...]
    gate = dot(m, wg_ref[...])
    up = dot(m, wu_ref[...])
    gh = gh_ref[...].astype(F32)
    sig = jax.nn.sigmoid(gate)
    silu = gate * sig
    h_ref[...] = (silu * up).astype(BF)
    dg = (gh * up * (sig * (1.0 + gate * (1.0 - sig)))).astype(BF)
    du = (gh * silu).astype(BF)
    dg_ref[...] = dg
    du_ref[...] = du
    acc[...] += dot(dg, wg_ref[...], 1, 1) + dot(du, wu_ref[...], 1, 1)

    @pl.when(j == pl.num_programs(0) - 1)
    def _():
        gm_ref[...] = acc[...].astype(BF)


def mlp(x, parts, gh, gain, wg, wu, chunk, tf):
    rows, d = parts[0].shape
    ff = wg.shape[1]
    once = pl.Buffered(1)
    at_chunk = pl.BlockSpec((rows, d), lambda j: (chunk, 0), pipeline_mode=once)
    whole = pl.BlockSpec((rows, d), lambda j: (0, 0), pipeline_mode=once)
    tile = pl.BlockSpec((rows, tf), lambda j: (0, j))
    return pl.pallas_call(
        functools.partial(mlp_kernel, np_=len(parts)),
        grid=(ff // tf,),
        in_specs=[
            at_chunk,
            *([whole] * len(parts)),
            pl.BlockSpec((1, d), lambda j: (0, 0)),
            pl.BlockSpec((rows, tf), lambda j: (chunk, j)),
            pl.BlockSpec((d, tf), lambda j: (0, j)),
            pl.BlockSpec((d, tf), lambda j: (0, j)),
        ],
        out_specs=[
            pl.BlockSpec((rows, d), lambda j: (0, 0)), tile, tile, tile,
            pl.BlockSpec((rows, d), lambda j: (0, 0)),
        ],
        scratch_shapes=[pltpu.VMEM((rows, d), F32)],
        out_shape=[
            sds((rows, d), BF), sds((rows, ff), BF), sds((rows, ff), BF), sds((rows, ff), BF),
            sds((rows, d), BF),
        ],
        compiler_params=params(),
        cost_estimate=cost(O('c_mlp', 1.0) * 38),
        name="mlp",
    )(x, *parts, gain, gh, wg, wu)


def mid_kernel(*refs, np_, ng):
    x_ref, parts, grads = refs[0], refs[1 : 1 + np_], refs[1 + np_ : 1 + np_ + ng]
    gain_ref, cot_ref, w_ref, gh_ref, ga_ref, gn_ref = refs[1 + np_ + ng :]
    h1 = x_ref[...].astype(F32)
    for part in parts:
        h1 = h1 + part[...].astype(F32)
    inv = rms(h1)
    n2 = h1 * inv
    gm = grads[0][...].astype(F32)
    for grad in grads[1:]:
        gm = gm + grad[...].astype(F32)
    g2 = gm * gain_ref[...]
    gh = cot_ref[...].astype(F32) + inv * (g2 - n2 * jnp.mean(g2 * n2, axis=1, keepdims=True))
    low = gh.astype(BF)
    gh_ref[...] = low
    ga_ref[...] = dot(low, w_ref[...], 1, 1).astype(BF)
    add = fold_rows(gm * n2)

    @pl.when(pl.program_id(0) == 0)
    def _():
        gn_ref[...] = add

    @pl.when(pl.program_id(0) > 0)
    def _():
        gn_ref[...] += add


def mid_backward(x, parts, grads, cot, gain, w_out, chunk, tm):
    rows, d = parts[0].shape
    n = w_out.shape[0]
    tiles = rows // tm
    at_chunk = pl.BlockSpec((tm, d), lambda i: (chunk * tiles + i, 0))
    tile = pl.BlockSpec((tm, d), lambda i: (i, 0))
    return pl.pallas_call(
        functools.partial(mid_kernel, np_=len(parts), ng=len(grads)),
        grid=(tiles,),
        in_specs=[
            at_chunk, *([tile] * (len(parts) + len(grads))), fixed((1, d)), at_chunk, fixed((n, d))
        ],
        out_specs=[tile, pl.BlockSpec((tm, n), lambda i: (i, 0)), pl.BlockSpec((8, d), lambda i: (0, 0))],
        out_shape=[sds((rows, d), BF), sds((rows, n), BF), sds((8, d), F32)],
        compiler_params=params(),
        cost_estimate=cost(O('c_mid', 1.0) * 11),
        name="mid_backward",
    )(x, *parts, *grads, gain, cot, w_out)


def head_back(grad, raw, hg, cosine, sine):
    inv = rms(raw)
    n = raw * inv
    du = grad * cosine + pltpu.roll(grad * sine, HD // 2, 1)
    dn = du * hg
    return inv * (dn - n * jnp.mean(dn * n, axis=1, keepdims=True)), fold_rows(du * n)


def add_out(ref, value):
    @pl.when(pl.program_id(0) == 0)
    def _():
        ref[...] = value

    @pl.when(pl.program_id(0) > 0)
    def _():
        ref[...] += value


def q_back_kernel(*refs, ng):
    dqs = refs[:ng]
    raw_ref, cos_ref, sin_ref, hg_ref, low_ref, gain_ref = refs[ng:]
    total = jnp.zeros(gain_ref.shape, F32)
    per = dqs[0].shape[1] // HD
    for h in range(raw_ref.shape[1] // HD):
        at, sub = slice(h * HD, (h + 1) * HD), slice(h % per * HD, (h % per + 1) * HD)
        back, part = head_back(
            dqs[h // per][:, sub], raw_ref[:, at], hg_ref[...], cos_ref[...], sin_ref[...]
        )
        low_ref[:, at] = back.astype(BF)
        total = total + part
    add_out(gain_ref, total)


def q_back(dqs, raw, cosine, sine, hg, tm):
    rows, n = raw.shape
    tile = pl.BlockSpec((tm, n), lambda i: (i, 0))
    part = pl.BlockSpec((tm, n // len(dqs)), lambda i: (i, 0))
    table = pl.BlockSpec((tm, HD), lambda i: (i, 0))
    return pl.pallas_call(
        functools.partial(q_back_kernel, ng=len(dqs)),
        grid=(rows // tm,),
        in_specs=[*([part] * len(dqs)), tile, table, table, fixed((1, HD))],
        out_specs=[tile, pl.BlockSpec((8, HD), lambda i: (0, 0))],
        out_shape=[sds((rows, n), BF), sds((8, HD), F32)],
        compiler_params=params(),
        cost_estimate=cost(O('c_qb', 1.0) * 8.5),
        name="q_back",
    )(*dqs, raw, cosine, sine, hg)


def in_kernel(s_ref, *refs, ng, nk):
    groups = [refs[g * nk : (g + 1) * nk] for g in range(ng)]
    (raw_ref, dq_ref, x_ref, cos_ref, sin_ref, hg_ref, wq_ref, wk_ref, wv_ref,
     low_ref, ga_ref, gain_ref, gn_ref) = refs[ng * nk :]
    heads = raw_ref.shape[1] // HD
    per = heads // ng
    total = jnp.zeros(gain_ref.shape, F32)
    for h in range(heads):
        k_at = slice(2 * (h % per) * HD, (2 * (h % per) + 1) * HD)
        v_at = slice((2 * (h % per) + 1) * HD, (2 * (h % per) + 2) * HD)
        dk, dv = 0.0, 0.0
        for ref in groups[h // per]:
            dk = dk + ref[:, k_at].astype(F32)
            dv = dv + ref[:, v_at].astype(F32)
        at = slice(h * HD, (h + 1) * HD)
        back, part = head_back(dk, raw_ref[:, at], hg_ref[...], cos_ref[...], sin_ref[...])
        low_ref[:, at] = back.astype(BF)
        low_ref[:, (heads + h) * HD : (heads + h + 1) * HD] = dv.astype(BF)
        total = total + part
    add_out(gain_ref, total)
    low = low_ref[...]
    ga = (
        dot(dq_ref[...], wq_ref[...], 1, 1)
        + dot(low[:, : heads * HD], wk_ref[...], 1, 1)
        + dot(low[:, heads * HD :], wv_ref[...], 1, 1)
    )
    ga_ref[...] = ga.astype(BF)
    x = x_ref[...].astype(F32)
    add_out(gn_ref, fold_rows(ga * (x * rms(x))))


def in_back(groups, raw, dq_low, x, base_tile, cosine, sine, hg, wq, wk, wv, tm):
    rows, n = raw.shape
    d = x.shape[1]
    nq = wq.shape[1]
    ng, nk = len(groups), len(groups[0])
    moved = lambda width: pl.BlockSpec((tm, width), lambda i, s: (s[0] + i, 0))
    tile = lambda width: pl.BlockSpec((tm, width), lambda i, s: (i, 0))
    return pl.pallas_call(
        functools.partial(in_kernel, ng=ng, nk=nk),
        grid_spec=grid_spec(
            1,
            (rows // tm,),
            [
                *([moved(2 * n // ng)] * (ng * nk)),
                tile(n), moved(nq), moved(d), moved(HD), moved(HD),
                fixed((1, HD)), fixed((d, nq)), fixed((d, n)), fixed((d, n)),
            ],
            [
                tile(2 * n), tile(d),
                pl.BlockSpec((8, HD), lambda i, s: (0, 0)), pl.BlockSpec((8, d), lambda i, s: (0, 0)),
            ],
        ),
        out_shape=[sds((rows, 2 * n), BF), sds((rows, d), BF), sds((8, HD), F32), sds((8, d), F32)],
        compiler_params=params(),
        cost_estimate=cost(O('c_in', 1.0) * 12.5),
        name="in_back",
    )(
        jnp.reshape(base_tile, (1,)), *[v for g in groups for v in g], raw, dq_low, x, cosine,
        sine, hg, wq, wk, wv,
    )


def pick_tile(n):
    for tile in (1536, 1024, 768, 512, 384, 256, 128):
        if n % tile == 0 and n > tile:
            return tile
    return n


def product(refs, nt):
    stack = lambda ks: jnp.concatenate([refs[k][...] for k in ks], axis=0)
    return dot(stack(range(0, 2 * nt, 2)), stack(range(1, 2 * nt, 2)), 0, 0)


def pieces_of(total, row_type, ns):
    size = total.shape[0 if row_type else 1] // ns
    for n in range(ns):
        yield total[n * size : (n + 1) * size] if row_type else total[:, n * size : (n + 1) * size]


def wgrad_kernel(s_ref, *refs, nt, na, row_type, ns, seq_first):
    adds, out_ref = refs[2 * nt : 2 * nt + na], refs[2 * nt + na]
    for n, piece in enumerate(pieces_of(product(refs, nt), row_type, ns)):
        for add in adds:
            piece = piece + add[0, n].astype(F32)
        out_ref[(n, 0) if seq_first else (0, n)] = piece.astype(BF)


def after(value, *others):
    return lax.optimization_barrier((value, *others))[0]


def nought(value):
    return jnp.minimum(jnp.abs(value[:1, :1].astype(F32)), 0.0)


def wgrad(terms, blocks, addends, row_type, nd, ns, rows, behind, seq_first=False):
    nb, nt = len(blocks), len(terms)
    scalars = jnp.stack(
        [jnp.asarray(v, jnp.int32) for v in blocks]
        + [jnp.asarray(v(), jnp.int32) for t in terms for v in (t[1], t[3])]
    )
    scalars = after(scalars, *behind)
    left, right = terms[0][0].shape[1], terms[0][2].shape[1]
    ins = []
    if row_type:
        bw = left // nd
        tile = pick_tile(right)
        steps = right // tile
        for n in range(nt):
            ins.append(pl.BlockSpec((rows, bw), lambda b, t, s, n=n: (s[nb + 2 * n], s[b])))
            ins.append(pl.BlockSpec((rows, tile), lambda b, t, s, n=n: (s[nb + 2 * n + 1], t)))
        out_dims = (ns, bw // ns, right)
        block = (1, ns, bw // ns, tile)
        at = lambda b, t, s: (b, 0, 0, t)
        add_at = lambda k: lambda b, t, s: (k, 0, 0, t)
    else:
        bw = right // nd
        tile = pick_tile(left)
        steps = left // tile
        for n in range(nt):
            ins.append(pl.BlockSpec((rows, tile), lambda b, t, s, n=n: (s[nb + 2 * n], t)))
            ins.append(pl.BlockSpec((rows, bw), lambda b, t, s, n=n: (s[nb + 2 * n + 1], s[b])))
        out_dims = (ns, left, bw // ns)
        block = (1, ns, tile, bw // ns)
        at = lambda b, t, s: (b, 0, t, 0)
        add_at = lambda k: lambda b, t, s: (k, 0, t, 0)
    work = 2e-9 * nt * rows * left * right / nd
    operands = [v for t in terms for v in (t[0], t[2])]
    for arr, k in addends:
        ins.append(pl.BlockSpec(block, at if k is None else add_at(k)))
        operands.append(arr)
    out_dims = (ns, nb, *out_dims[1:]) if seq_first else (nb, *out_dims)
    out_block, out_at = block, at
    if seq_first:
        out_block = (block[1], 1, *block[2:])
        out_at = lambda *a: (0, at(*a)[0], *at(*a)[2:])
    return pl.pallas_call(
        functools.partial(
            wgrad_kernel, nt=nt, na=len(addends), row_type=row_type, ns=ns, seq_first=seq_first
        ),
        grid_spec=grid_spec(1, (nb, steps), ins, pl.BlockSpec(out_block, out_at)),
        out_shape=sds(out_dims, BF),
        compiler_params=params(),
        cost_estimate=cost(O('c_wg', 1.0) * (1 + 2.3 * work * nb)),
        name="wgrad",
    )(scalars, *operands)


def flip(d, bits):
    return {1: d + 1 - 2 * (d % 2), 2: d + 2 - 4 * (d // 2), 3: 3 - d}[bits]


def wgrad_send_kernel(*refs, nt, row_type, ns, steps, tile):
    ins, out_ref = refs[: 2 * nt], refs[2 * nt]
    slots, send_sem, recv_sem = refs[2 * nt + 1 : 2 * nt + 4]
    b, t = pl.program_id(0), pl.program_id(1)
    k = b * steps + t
    last = 2 * steps - 1
    partner = {"dp": flip(lax.axis_index("dp"), 1)}

    @pl.when(k == 0)
    def _():
        barrier = pltpu.get_barrier_semaphore()
        pl.semaphore_signal(
            barrier, inc=1, device_id=partner, device_id_type=pl.DeviceIdType.MESH
        )
        pl.semaphore_wait(barrier, 1)

    def copy(src, dst, slot):
        return pltpu.make_async_remote_copy(
            src_ref=src, dst_ref=dst, send_sem=send_sem.at[slot], recv_sem=recv_sem,
            device_id=partner, device_id_type=pl.DeviceIdType.MESH,
        )

    def place(b, t):
        at = pl.ds(pl.multiple_of(t * tile, tile), tile)
        return out_ref.at[b, :, :, at] if row_type else out_ref.at[b, :, at, :]

    slot = k % 2

    @pl.when(k >= 2)
    def _():
        copy(slots.at[slot], place(b, t), slot).wait_send()

    for n, piece in enumerate(pieces_of(product(ins, nt), row_type, ns)):
        slots[slot, n] = piece.astype(BF)
    copy(slots.at[slot], place(b, t), slot).start()

    @pl.when(k == last)
    def _():
        copy(slots.at[1 - slot], place(b, t), 1 - slot).wait_send()
        copy(slots.at[slot], place(b, t), slot).wait_send()
        copy(out_ref, out_ref, slot).wait_recv()


def wgrad_send(terms, row_type, nd, ns, rows, ident, behind):
    nt = len(terms)
    left, right = terms[0][0].shape[1], terms[0][2].shape[1]
    block = lambda b: jnp.where(
        b == 0, flip(lax.axis_index("dp"), 1), flip(lax.axis_index("dp"), 3)
    )
    ins = []
    if row_type:
        bw = left // nd
        tile = pick_tile(right)
        steps = right // tile
        for t in terms:
            ins.append(pl.BlockSpec((rows, bw), lambda b, s, r=t[1]: (r(), block(b))))
            ins.append(pl.BlockSpec((rows, tile), lambda b, s, r=t[3]: (r(), s)))
        out_dims, slot = (ns, bw // ns, right), (ns, bw // ns, tile)
    else:
        bw = right // nd
        tile = pick_tile(left)
        steps = left // tile
        for t in terms:
            ins.append(pl.BlockSpec((rows, tile), lambda b, s, r=t[1]: (r(), s)))
            ins.append(pl.BlockSpec((rows, bw), lambda b, s, r=t[3]: (r(), block(b))))
        out_dims, slot = (ns, left, bw // ns), (ns, tile, bw // ns)
    work = 2e-9 * nt * rows * left * right / nd
    operands = [v for t in terms for v in (t[0], t[2])]
    operands[0] = after(operands[0], *behind)
    return pl.pallas_call(
        functools.partial(
            wgrad_send_kernel, nt=nt, row_type=row_type, ns=ns, steps=steps, tile=tile
        ),
        grid=(2, steps),
        in_specs=ins,
        out_specs=pl.BlockSpec(memory_space=pl.ANY),
        scratch_shapes=[
            pltpu.VMEM((2, *slot), BF), pltpu.SemaphoreType.DMA((2,)), pltpu.SemaphoreType.DMA,
        ],
        out_shape=sds((2, *out_dims), BF),
        compiler_params=params(collective_id=ident, has_side_effects=True),
        cost_estimate=cost(O('c_ws', 1.0) * (2 + 3.4 * work)),
        name="wgrad_send",
    )(*operands)


class Shrink:
    def __init__(self, terms, row_type, ahead=None, small=False, *, nd, ns, rows):
        self.small, self.pair = small, None
        self.args, self.nd = (terms, row_type), nd
        self.ahead = ahead
        self.ident = ahead.ident + 1 if ahead else 0
        self.sizes = (nd, ns, rows)
        self.d = lax.axis_index("dp")

    def make(self, blocks, adds, behind, **more):
        terms, row_type = self.args
        return wgrad(terms, blocks, adds, row_type, *self.sizes, behind, **more)

    def send(self, *behind):
        terms, row_type = self.args
        self.got = wgrad_send(terms, row_type, *self.sizes, self.ident, behind)
        return self.got

    def far(self, *behind):
        out = self.make([self.d ^ 2], [(self.got, 1)], behind)
        first = self.ahead
        for _ in range(O('serial', 1)):
            first = first.ahead if first else None
        first = [first.come] if first and first.pair is None and O('serial', 1) < 3 else []
        self.come = lax.ppermute(
            after(out, *first), "dp", [(k, k ^ 2) for k in range(self.nd)]
        )
        return out

    def both(self, *behind):
        out = self.make([self.d, self.d ^ 2], [(self.got, None)], behind, seq_first=True)
        self.pair = lax.psum_scatter(out, "seq", scatter_dimension=0)
        return out

    def near(self, *behind):
        self.here = self.make([self.d], [(self.got, 0), (self.come, 0)], behind)
        if not self.small:
            self.share = lax.psum_scatter(self.here[0], "seq", scatter_dimension=0)
        return self.here

    def finish(self):
        if self.pair is not None:
            come = lax.ppermute(self.pair[1], "dp", [(k, k ^ 2) for k in range(self.nd)])
            return self.pair[0].astype(F32) + come.astype(F32)
        if not self.small:
            return self.share.astype(F32)
        z, ns = lax.axis_index("seq"), self.sizes[1]
        piece = lambda j: lax.dynamic_index_in_dim(self.here[0], j, 0, keepdims=False)
        first = jnp.stack([piece(z ^ 1), piece(z ^ 3)])
        first = lax.ppermute(first, "seq", [(k, k ^ 1) for k in range(ns)]).astype(F32)
        second = (piece(z ^ 2).astype(F32) + first[1]).astype(BF)
        second = lax.ppermute(second, "seq", [(k, k ^ 2) for k in range(ns)])
        return piece(z).astype(F32) + first[0] + second.astype(F32)


def final_kernel(x_ref, ga_ref, gb_ref, h0_ref, h1_ref, gain_ref, s_ref, out_ref):
    x = x_ref[...].astype(F32)
    inv = rms(x)
    n1 = x * inv
    g1 = (ga_ref[...].astype(F32) + gb_ref[...].astype(F32)) * gain_ref[...]
    gh = jnp.where(s_ref[0] == 0, h0_ref[...].astype(F32), h1_ref[...].astype(F32))
    out_ref[...] = (gh + inv * (g1 - n1 * jnp.mean(g1 * n1, axis=1, keepdims=True))).astype(BF)


def final(x, ga, gb, h0, h1, gain, y, tm):
    rows, d = x.shape
    tile = pl.BlockSpec((tm, d), lambda i: (i, 0))
    return pl.pallas_call(
        final_kernel,
        grid=(rows // tm,),
        in_specs=[tile] * 5 + [fixed((1, d)), pl.BlockSpec(memory_space=pltpu.SMEM)],
        out_specs=tile,
        out_shape=sds((rows, d), BF),
        compiler_params=params(),
        cost_estimate=cost(O('c_fin', 1.0) * 8),
        name="final",
    )(x, ga, gb, h0, h1, gain, jnp.reshape(y, (1,)))


def per_device(
    tokens, doc_lengths, w_query, w_key, w_value, w_out, w_gate, w_up, w_down,
    norm_attn, norm_mlp, query_norm, key_norm, cotangent, *, nd, ns, nt,
):
    tokens, cotangent = tokens[0], cotangent[0]
    own_rows, d = tokens.shape
    span = own_rows * nt
    rows = span // 2
    heads_kv = w_key.shape[1] // HD
    gs = w_query.shape[1] // w_key.shape[1]
    z, y = lax.axis_index("seq"), lax.axis_index("tensor")
    row = lambda v: v[None, :]
    tm = 256
    tq = tk = 512
    swap = lambda v: lax.ppermute(v, "tensor", [(0, 1), (1, 0)])
    pick = lambda a, b: jnp.where(y == 0, a, b)

    back = min(ns - 1, -(-(LONGEST - 1) // span))
    window = (back + 1) * span
    ends = jnp.cumsum(doc_lengths[0])
    positions = z * span + jnp.arange(span, dtype=jnp.int32)
    starts = jnp.max(jnp.where(ends[None, :] <= positions[:, None], ends[None, :], 0), axis=1)
    half = HD // 2
    inverse = rope_base ** (-(jnp.arange(half, dtype=F32) * 2.0 / HD))
    angles = (positions - starts).astype(F32)[:, None] * inverse[None, :]
    cosine = jnp.tile(jnp.cos(angles), (1, 2))
    sine = jnp.sin(angles)
    sine = jnp.concatenate([-sine, sine], axis=1)
    rel = jnp.clip(starts - (z - back) * span, 0, window - 1)
    starts_col = jnp.broadcast_to(rel[:, None], (span, HD))
    starts_row = jnp.broadcast_to(rel[None, :], (8, span))

    def bounds(first_row, count, w0, w1):
        heads = rel[first_row : first_row + count : tq]
        tails = rel[first_row + tq - 1 : first_row + count : tq]
        at = window - span + first_row + tq * jnp.arange(count // tq, dtype=jnp.int32)
        inside = lambda v: jnp.clip(v - w0, 0, w1 - w0)
        up = lambda v: (v + tk - 1) // tk
        return [inside(heads) // tk, up(inside(at + tq)), up(inside(tails)), inside(at + 1) // tk]

    if nt == 2:
        other = swap(tokens)
        cot_in, other = lax.optimization_barrier((cotangent, other))
        cot_other = swap(cot_in)
        pieces, bases = [tokens, other], [y * rows, (1 - y) * rows]
        cot = jnp.concatenate([pick(cotangent, cot_other), pick(cot_other, cotangent)], axis=0)
    else:
        everything = lax.all_gather(tokens, "tensor", axis=0, tiled=True)
        cot = lax.all_gather(cotangent, "tensor", axis=0, tiled=True)
        pieces, bases = [everything[:rows], everything[rows:]], [0, rows]
    bases = [jnp.asarray(b, jnp.int32) for b in bases]
    base_tiles = [b // tm for b in bases]

    segs, seg_bases = [[] for _ in range(back + 1)], [[] for _ in range(back + 1)]
    raws = []
    ahead = [(k, k + 1) for k in range(ns - 1)]
    for x_piece, base, base_tile in zip(pieces, bases, base_tiles):
        if raws and O('e_kv_hop'):
            base_tile = after(base_tile, segs[1][0])
        kv, raw = project_kv(
            x_piece, base_tile, row(norm_attn), w_key, w_value, cosine, sine, row(key_norm), tm
        )
        raws.append(raw)
        for hop in range(back + 1):
            segs[hop].append(kv)
            seg_bases[hop].append((back - hop) * span + base)
            if hop < back:
                kv = lax.ppermute(kv, "seq", ahead)
    x_all, attn_in, query, q_raw = project_q(
        pieces[0], pieces[1], jnp.stack(base_tiles), row(norm_attn), w_query, cosine, sine,
        row(query_norm), tm,
    )

    attend = functools.partial(flash_fwd, bounds, gs=gs, tq=tq, tk=tk, window=window)
    prior = []
    for hop in range(back):
        part = ((back - hop) * span, (back - hop + 1) * span)
        prior = attend(
            seg_bases[hop], query, starts_col, segs[hop], prior, part=part, row_at=0, rows=span,
            last=False,
        )
    outs, sums, parts = [], [], []
    for c in range(2):
        out, total = attend(
            seg_bases[back], query, after(starts_col, *[v[0] for v in parts]), segs[back], prior, part=(0, span),
            row_at=c * rows, rows=rows, last=True,
        )
        outs.append(out)
        sums.append(total)
        partial = dot(out, w_out).astype(BF)
        parts.append([partial, swap(partial)] if nt == 2 else [lax.psum(partial, "tensor")])

    grad_hidden = dot(after(cot, partial), w_down, 1, 1).astype(BF)
    low_mlp, hidden, d_gate, d_up, grads = [], [], [], [], []
    tf = min(512, w_gate.shape[1] // 2)
    for c in range(2):
        m, h, dg, du, gm = mlp(
            x_all, parts[c], grad_hidden, after(row(norm_mlp), *low_mlp), w_gate, w_up, c, tf
        )
        low_mlp.append(m)
        hidden.append(h)
        d_gate.append(dg)
        d_up.append(du)
        grads.append([gm, swap(gm)] if nt == 2 else [lax.psum(gm, "tensor")])

    shrink = functools.partial(Shrink, nd=nd, ns=ns, rows=rows)
    zero = lambda: 0
    chunk = lambda c: lambda: c
    down = shrink([(hidden[c], zero, cot, chunk(c)) for c in range(2)], False, None, bool(O('p_down')))
    gate = shrink([(low_mlp[c], zero, d_gate[c], zero) for c in range(2)], True, down, bool(O('p_gate')))
    up = shrink([(low_mlp[c], zero, d_up[c], zero) for c in range(2)], True, gate, bool(O('p_up')))
    gh, g_att, g_norm_two = [], [], []

    def middle(c, *behind):
        low, ga, gn = mid_backward(
            x_all, parts[c], grads[c], cot, after(row(norm_mlp), *behind), w_out, c, tm
        )
        gh.append(low)
        g_att.append(ga)
        g_norm_two.append(gn)
        return low

    opt = lambda k, *v: list(v) if O(k) else []
    down.send()
    middle(0, *opt('e_m0_ds', down.got))
    zf = bool(O('zf'))
    df = down.both(*opt('e_df_m0', gh[0])) if zf else down.far(*opt('e_df_m0', gh[0]))
    gs_out = gate.send(*opt('e_gs_df', df), *opt('e_gs_m0', gh[0]))
    gf = gate.far() if O('e_gf_early') else None
    middle(1, *opt('e_m1_m0', gh[0]), *opt('e_m1_gs', gs_out), *opt('e_m1_gf', *([gf] if gf is not None else [])))
    if gf is None:
        gf = gate.far(gh[1])
    t = opt('e_fb0_gf', gf)
    hop_segs = [v for seg in segs for v in seg]
    hop_bases = jnp.stack([v for b in seg_bases for v in b])
    scalars = jnp.concatenate([*bounds(0, span, 0, window), hop_bases])
    halves = [(0, heads_kv)] if heads_kv == 1 else [(0, heads_kv // 2), (heads_kv // 2, heads_kv // 2)]
    behind = [(k + 1, k) for k in range(ns - 1)]
    dqs, dkvs, first_hops = [], [], []
    for part, heads in enumerate(halves):
        dq, *dkv = flash_bwd(
            after(scalars, *t), query, starts_row, g_att, outs, sums, hop_segs, window, gs, tq, tk,
            heads,
        )
        come = None
        for b in range(back):
            send = dkv[b]
            if come is not None:
                send = (send.astype(F32) + come.astype(F32)).astype(BF)
            come = lax.ppermute(send, "seq", behind)
            first_hops += [come] if b == 0 else []
        dqs.append(dq)
        dkvs.append([dkv[back]] + ([come] if come is not None else []))
        if part == 0:
            dn = dq if zf else down.near(*opt('e_dn_d0', dq))
            us = up.send(dq)
            t = opt('e_fb1_dn', dn) + opt('e_fb1_us', us) + opt('e_fb1_gf', gf)
            if O('e_fb1_uf'):
                uf = up.far()
                t += [uf]
    out_w = shrink([(outs[c], zero, gh[c], zero) for c in range(2)], False, up, bool(O('p_out',1)))
    if not O('e_fb1_uf'):
        uf = up.far(dqs[-1])
    gn_ = gate.near(*opt('e_gn_d1', dqs[-1]), *opt('e_gn_uf', uf), *opt('e_gn_hop', *first_hops))
    dq_low, g_qn = q_back(
        dqs, q_raw, cosine, sine,
        after(row(query_norm), *opt('e_qb_uf', uf), *opt('e_qb_gn', gn_), *opt('e_qb_hop', *first_hops)), tm,
    )
    query_w = shrink([(attn_in, chunk(c), dq_low, chunk(c)) for c in range(2)], True, out_w, bool(O('p_q',1)))
    os_ = out_w.send(dq_low)
    qs_ = query_w.send(*opt('e_qs_os', os_))
    of_ = out_w.far(*opt('e_of_qs', qs_))
    qf_ = query_w.far(*opt('e_qf_of', of_))
    w_down_later = after(w_down, dq_low) if O('e_dp_q') else after(w_down, gh[1]) if O('e_dp_m') else w_down
    downs = [dot(hidden[c], w_down_later).astype(BF) for c in range(2)]
    come_down = swap(pick(downs[1], downs[0])) if nt == 2 else downs[0]
    un = up.near(*opt('e_un_qf', qf_), *opt('e_un_d1', dqs[-1]))
    t = opt('e_in_qf', qf_) + opt('e_in_dp', *downs) + opt('e_in_cd', come_down) + opt('e_in_un', un)

    lows, gas, g_kn, g_norm_one = [None] * 2, [None] * 2, [], []
    for n in (1, 0):
        lows[n], gas[n], gain_part, norm_part = in_back(
            dkvs, raws[n], dq_low, x_all, base_tiles[n], cosine, sine, after(row(key_norm), *t),
            w_query, w_key, w_value, tm,
        )
        g_kn.append(gain_part)
        g_norm_one.append(norm_part)
    kv_cut = heads_kv * HD
    own_half = lambda: lax.axis_index("tensor")
    half_of = lambda n: chunk(n) if nt != 2 else own_half if n == 0 else lambda: 1 - own_half()
    kv_w = shrink([(attn_in, half_of(n), lows[n], zero) for n in range(2)], True, query_w, bool(O('p_kv',1)))
    ks_ = kv_w.send()
    kf_ = kv_w.far(*opt('e_kf_un', un))
    on_ = out_w.near(*opt('e_on_kf', kf_))
    qn_ = query_w.near(*opt('e_qn_on', on_))
    gain_last = after(row(norm_attn), *opt('e_fin_qn', qn_), *opt('e_fin_kf', kf_), *opt('e_fin_on', on_))

    up32 = lambda v: v.astype(F32)
    if nt == 2:
        result = up32(tokens) + up32(pick(downs[0], downs[1])) + up32(come_down)
        for n in range(2):
            result = result + up32(pick(parts[0][n], parts[1][n]))
        grad_tokens = final(tokens, gas[0], swap(gas[1]), gh[0], gh[1], gain_last, y, tm)
    else:
        scatter = lambda v: lax.psum_scatter(v, "tensor", scatter_dimension=0, tiled=True)
        mine = lambda pair: lax.dynamic_slice_in_dim(
            jnp.concatenate(pair, axis=0), y * own_rows, own_rows
        )
        result = up32(tokens) + up32(scatter(jnp.concatenate(downs, axis=0)))
        result = result + up32(mine([parts[0][0], parts[1][0]]))
        x32 = up32(tokens)
        inv = rms(x32)
        n1 = x32 * inv
        g1 = up32(scatter(jnp.concatenate(gas, axis=0))) * row(norm_attn)
        moved = inv * (g1 - n1 * jnp.mean(g1 * n1, axis=1, keepdims=True))
        grad_tokens = (up32(mine(gh)) + moved).astype(BF)
    kn_ = kv_w.near(*opt('e_kn_fin', grad_tokens))
    g_down, g_gate, g_up, g_out, g_query, g_kv = [
        v.finish() for v in (down, gate, up, out_w, query_w, kv_w)
    ]

    share = 1.0 / nt
    fold = lambda pair: jnp.sum(pair[0] + pair[1], axis=0)
    axes = (("dp", nd), ("seq", ns), ("tensor", nt))
    packed = jnp.concatenate(
        [fold(g_norm_one), fold(g_norm_two) * share, jnp.sum(g_qn, axis=0), fold(g_kn)]
    )
    packed = total_sum(after(packed, *opt('e_pk_fin', grad_tokens), *opt('e_pk_kn', kn_), *opt('e_pk_kc', kv_w.come)), axes)
    return (
        result.astype(BF)[None], grad_tokens[None], g_query, g_kv[:, :kv_cut], g_kv[:, kv_cut:],
        g_out, g_gate, g_up, g_down,
        packed[:d], packed[d : 2 * d], packed[2 * d : 2 * d + HD], packed[2 * d + HD :],
    )


def total_sum(v, sizes):
    for name, size in sizes:
        step = 1
        while step < size:
            v = v + lax.ppermute(v, name, [(k, k ^ step) for k in range(size)])
            step *= 2
    return v


def solution(mesh):
    sizes = dict(nd=mesh.shape["dp"], ns=mesh.shape["seq"], nt=mesh.shape["tensor"])
    rows, cols, both = P("dp", ("seq", "tensor"), None), P(None, "tensor"), ("dp", "seq")
    return jax.shard_map(
        functools.partial(per_device, **sizes),
        mesh=mesh,
        in_specs=(
            rows, P("dp", None), cols, cols, cols, P("tensor", None), cols, cols, P("tensor", None),
            P(), P(), P(), P(), rows,
        ),
        out_specs=(
            rows, rows, P(both, "tensor"), P(both, "tensor"), P(both, "tensor"), P("tensor", both),
            P(both, "tensor"), P(both, "tensor"), P("tensor", both), P(), P(), P(), P(),
        ),
        check_vma=False,
    )
```

```python
import functools
import math

import jax
import jax.numpy as jnp
from jax import lax
from jax.experimental import pallas as pl
from jax.experimental.pallas import tpu as pltpu
from jax.sharding import PartitionSpec as P

HD = 128
LONGEST = 2048
eps_norm = 1e-06
rope_base = 1000000.0
score_scale = HD ** (-0.5)
log2e = math.log2(math.e)
exp_scale = score_scale * log2e
BF = jnp.bfloat16
F32 = jnp.float32
MIB = 1 << 20
PLAN = {
    "c_fin": 0.3,
    "c_in": 0.3,
    "c_mid": 1.0,
    "c_wg": 1.6,
    "e_dp_q": 1,
    "e_fb0_gf": 1,
    "e_fb1_gf": 1,
    "e_fb1_uf": 1,
    "e_fb1_us": 1,
    "e_fin_qn": 1,
    "e_gf_early": 1,
    "e_gs_m0": 1,
    "e_in_cd": 1,
    "e_in_dp": 1,
    "e_in_qf": 1,
    "e_in_un": 1,
    "e_kf_un": 1,
    "e_kv_hop": 1,
    "e_m1_gf": 1,
    "e_m1_gs": 1,
    "e_on_kf": 1,
    "e_pk_fin": 1,
    "e_pk_kc": 1,
    "e_pk_kn": 1,
    "e_qb_gn": 1,
    "e_qb_uf": 1,
    "e_qf_of": 1,
    "e_qn_on": 1,
    "e_qs_os": 1,
    "e_un_qf": 1,
    "scale": 0.7,
    "serial": 3,
}


def O(key, default=0):
    return PLAN.get(key, default)


cost_scale = O("scale", 0.4)


def params(limit=56, **kw):
    return pltpu.CompilerParams(vmem_limit_bytes=limit * MIB, **kw)


def cost(us):
    return pl.CostEstimate(flops=int(us * cost_scale * 1e9), bytes_accessed=0, transcendentals=0)


def dot(a, b, ca=1, cb=0):
    return lax.dot_general(a, b, (((ca,), (cb,)), ((), ())), preferred_element_type=F32)


def fixed(shape):
    zeros = (0,) * len(shape)
    return pl.BlockSpec(shape, lambda *_: zeros, pipeline_mode=pl.Buffered(1))


def grid_spec(scalars, grid, ins, outs, scratch=()):
    return pltpu.PrefetchScalarGridSpec(
        num_scalar_prefetch=scalars, grid=grid, in_specs=ins, out_specs=outs, scratch_shapes=scratch
    )


def sds(shape, dtype):
    return jax.ShapeDtypeStruct(shape, dtype)


def rms(x):
    return lax.rsqrt(jnp.mean(x * x, axis=-1, keepdims=True) + eps_norm)


def fold_rows(v):
    return jnp.sum(v.reshape(v.shape[0] // 8, 8, v.shape[1]), axis=0)


def kv_kernel(s_ref, x_ref, gain_ref, wk_ref, wv_ref, cos_ref, sin_ref, hg_ref, kv_ref, raw_ref):
    x = x_ref[...].astype(F32)
    a = (x * rms(x) * gain_ref[...]).astype(BF)
    k = dot(a, wk_ref[...])
    v = dot(a, wv_ref[...]).astype(BF)
    raw_ref[...] = k
    cosine, sine, hg = cos_ref[...], sin_ref[...], hg_ref[...]
    for h in range(k.shape[1] // HD):
        kh = k[:, h * HD : (h + 1) * HD]
        u = kh * rms(kh) * hg
        r = u * cosine + pltpu.roll(u, HD // 2, 1) * sine
        kv_ref[:, 2 * h * HD : (2 * h + 1) * HD] = r.astype(BF)
        kv_ref[:, (2 * h + 1) * HD : (2 * h + 2) * HD] = v[:, h * HD : (h + 1) * HD]


def project_kv(x, base_tile, gain, wk, wv, cosine, sine, hg, tm):
    rows, d = x.shape
    n = wk.shape[1]
    return pl.pallas_call(
        kv_kernel,
        grid_spec=grid_spec(
            1,
            (rows // tm,),
            [
                pl.BlockSpec((tm, d), lambda i, s: (i, 0)),
                fixed((1, d)),
                fixed((d, n)),
                fixed((d, n)),
                pl.BlockSpec((tm, HD), lambda i, s: (s[0] + i, 0)),
                pl.BlockSpec((tm, HD), lambda i, s: (s[0] + i, 0)),
                fixed((1, HD)),
            ],
            [
                pl.BlockSpec((tm, 2 * n), lambda i, s: (i, 0)),
                pl.BlockSpec((tm, n), lambda i, s: (i, 0)),
            ],
        ),
        out_shape=[sds((rows, 2 * n), BF), sds((rows, n), F32)],
        compiler_params=params(),
        cost_estimate=cost(6.5),
        name="project_kv",
    )(jnp.reshape(base_tile, (1,)), x, gain, wk, wv, cosine, sine, hg)


def q_kernel(
    s_ref, xa_ref, xb_ref, gain_ref, w_ref, cos_ref, sin_ref, hg_ref, x_ref, a_ref, q_ref, raw_ref,
    *, half,
):
    xin = jnp.where(pl.program_id(0) < half, xa_ref[...].astype(F32), xb_ref[...].astype(F32))
    x_ref[...] = xin.astype(BF)
    a = (xin * rms(xin) * gain_ref[...]).astype(BF)
    a_ref[...] = a
    q = dot(a, w_ref[...])
    raw_ref[...] = q
    cosine, sine, hg = cos_ref[...], sin_ref[...], hg_ref[...]
    for h in range(q.shape[1] // HD):
        qh = q[:, h * HD : (h + 1) * HD]
        u = qh * rms(qh) * hg
        r = u * cosine + pltpu.roll(u, HD // 2, 1) * sine
        q_ref[:, h * HD : (h + 1) * HD] = (r * exp_scale).astype(BF)


def project_q(xa, xb, bases, gain, w, cosine, sine, hg, tm):
    rows, d = xa.shape
    n = w.shape[1]
    half = rows // tm
    out_at = lambda i, s: (s[i // half] + i % half, 0)
    total = 2 * rows
    return pl.pallas_call(
        functools.partial(q_kernel, half=half),
        grid_spec=grid_spec(
            1,
            (2 * half,),
            [
                pl.BlockSpec((tm, d), lambda i, s: (jnp.minimum(i, half - 1), 0)),
                pl.BlockSpec((tm, d), lambda i, s: (jnp.maximum(i - half, 0), 0)),
                fixed((1, d)),
                fixed((d, n)),
                pl.BlockSpec((tm, HD), out_at),
                pl.BlockSpec((tm, HD), out_at),
                fixed((1, HD)),
            ],
            [
                pl.BlockSpec((tm, d), out_at),
                pl.BlockSpec((tm, d), out_at),
                pl.BlockSpec((tm, n), out_at),
                pl.BlockSpec((tm, n), out_at),
            ],
        ),
        out_shape=[
            sds((total, d), BF), sds((total, d), BF), sds((total, n), BF), sds((total, n), F32)
        ],
        compiler_params=params(),
        cost_estimate=cost(13),
        name="project_q",
    )(bases, xa, xb, gain, w, cosine, sine, hg)


def fill_window(s_ref, at, segs, kwin, vwin):
    for n, seg in enumerate(segs):
        rows = seg.shape[0]
        base = pl.multiple_of(s_ref[at + n], math.gcd(rows, 256))
        kwin[pl.ds(base, rows), :HD] = seg[:, :HD]
        vwin[pl.ds(base, rows), :HD] = seg[:, HD:]


def spread(value, gs, tq):
    step = HD // gs
    return jnp.concatenate([value[:, g * step : g * step + 1] for g in range(gs)], axis=0)


def flash_fwd_kernel(s_ref, q_ref, st_ref, *rest, nseg, prior, last, nq, tq, tk, gs, w0, row0):
    segs, rest = rest[:nseg], rest[nseg:]
    acc_in, rest = rest[: 2 * prior], rest[2 * prior :]
    o_ref, l_ref, kwin, vwin, acc = rest
    i = pl.program_id(1)

    @pl.when(i == 0)
    def _():
        fill_window(s_ref, 4 * nq, segs, kwin, vwin)
        vwin[:, HD:] = jnp.ones(vwin[:, HD:].shape, BF)

    heads = [slice(g * HD, (g + 1) * HD) for g in range(gs)]
    q2 = jnp.concatenate([q_ref[:, hh] for hh in heads], axis=0)
    if prior:
        acc[:, :HD] = jnp.concatenate([acc_in[0][:, hh] for hh in heads], axis=0)
        acc[:, HD:] = jnp.broadcast_to(spread(acc_in[1], gs, tq), (gs * tq, HD))
    else:
        acc[...] = jnp.zeros_like(acc)
    lo, hi, flo, fhi = [s_ref[n * nq + i] for n in range(4)]

    def step(kt, masked):
        at = pl.multiple_of(kt * tk, tk)
        p = jnp.exp2(dot(q2, kwin[pl.ds(at, tk), :], 1, 1))
        if masked:
            st = st_ref[:, :1]
            j = w0 + at + lax.broadcasted_iota(jnp.int32, (tq, tk), 1)
            t = row0 + i * tq + lax.broadcasted_iota(jnp.int32, (tq, tk), 0)
            keep = (j >= st) & (j <= t)
            p = jnp.where(jnp.concatenate([keep] * gs, axis=0), p, 0.0)
        acc[...] += dot(p.astype(BF), vwin[pl.ds(at, tk), :])

    def body(kt, carry):
        inside = (kt >= flo) & (kt < fhi)

        @pl.when(inside)
        def _():
            step(kt, False)

        @pl.when(jnp.logical_not(inside))
        def _():
            step(kt, True)

        return carry

    lax.fori_loop(lo, hi, body, 0)
    total, out = acc[:, HD:], acc[:, :HD]
    if last:
        total = 1.0 / total
        out = (out * total).astype(BF)
    lane = lax.broadcasted_iota(jnp.int32, (tq, HD), 1)
    packed = total[:tq]
    for g in range(gs):
        o_ref[:, heads[g]] = out[g * tq : (g + 1) * tq]
        packed = jnp.where(lane >= g * (HD // gs), total[g * tq : (g + 1) * tq], packed)
    l_ref[...] = packed


def flash_fwd(bounds, bases, q, starts_col, segs, prior, window, part, row_at, rows, last, gs, tq, tk):
    width = gs * HD
    heads = q.shape[1] // width
    nq = rows // tq
    off = row_at // tq
    w0, w1 = part
    scalars = jnp.concatenate([*bounds(row_at, rows, w0, w1), jnp.stack([b - w0 for b in bases])])
    seg_specs = [pl.BlockSpec((seg.shape[0], 2 * HD), lambda h, i, s: (0, h)) for seg in segs]
    pairs = rows * (w1 - w0) // 2
    moved = lambda w: pl.BlockSpec((tq, w), lambda h, i, s: (off + i, h))
    tile = lambda w: pl.BlockSpec((tq, w), lambda h, i, s: (i, h))
    return pl.pallas_call(
        functools.partial(
            flash_fwd_kernel, nseg=len(segs), prior=len(prior) // 2, last=last, nq=nq, tq=tq,
            tk=tk, gs=gs, w0=w0, row0=window - q.shape[0] + row_at,
        ),
        grid_spec=grid_spec(
            1,
            (heads, nq),
            [
                moved(width),
                pl.BlockSpec((tq, HD), lambda h, i, s: (off + i, 0)),
                *seg_specs,
                *([moved(width), moved(HD)] if prior else []),
            ],
            [tile(width), tile(HD)],
            [
                pltpu.VMEM((w1 - w0, HD), BF),
                pltpu.VMEM((w1 - w0, 2 * HD), BF),
                pltpu.VMEM((gs * tq, 2 * HD), F32),
            ],
        ),
        out_shape=[sds((rows, q.shape[1]), BF if last else F32), sds((rows, heads * HD), F32)],
        compiler_params=params(),
        cost_estimate=cost(7 * last + 19 * (1 - last)),
        name="flash_fwd",
    )(scalars, q, starts_col, *segs, *prior)


def flash_bwd_kernel(s_ref, q_ref, st_ref, *rest, nc, ns, nb, nq, tq, tk, gs, row0):
    das, outs, sums = rest[:nc], rest[nc : 2 * nc], rest[2 * nc : 3 * nc]
    segs = rest[3 * nc : 3 * nc + ns]
    dq_ref = rest[3 * nc + ns]
    dkvs = rest[3 * nc + ns + 1 : 3 * nc + ns + 1 + nb]
    kwin, vwin, dk, dv, dqs = rest[3 * nc + ns + 1 + nb :]
    span = dkvs[0].shape[0]

    fill_window(s_ref, 4 * nq, segs, kwin, vwin)
    lane = lax.broadcasted_iota(jnp.int32, (vwin.shape[0], HD), 1)
    vwin[:, HD:] = jnp.where(lane < 2, 1.0, 0.0).astype(BF)
    dk[...] = jnp.zeros_like(dk)
    dv[...] = jnp.zeros_like(dv)

    for i in range(nq):
        per = nq // nc
        c, r = i // per, i % per
        rows = slice(r * tq, (r + 1) * tq)
        heads = [slice(g * HD, (g + 1) * HD) for g in range(gs)]
        pile = lambda ref, rr: jnp.concatenate([ref[rr, hh] for hh in heads], axis=0)
        q2 = pile(q_ref, slice(i * tq, (i + 1) * tq))
        scaled = pile(das[c], rows).astype(F32) * spread(sums[c][rows, :], gs, tq)
        neg = -jnp.sum(scaled * pile(outs[c], rows).astype(F32), axis=1, keepdims=True)
        do2 = scaled.astype(BF)
        first = neg.astype(BF).astype(F32)
        ln = lax.broadcasted_iota(jnp.int32, (gs * tq, HD), 1)
        daug = jnp.where(ln == 0, first, jnp.where(ln == 1, neg - first, 0.0)).astype(BF)
        da = jnp.concatenate([do2, daug], axis=1)
        dqs[...] = jnp.zeros_like(dqs)
        lo, hi, flo, fhi = [s_ref[n * nq + i] for n in range(4)]

        def step(kt, masked, i=i, q2=q2, do2=do2, da=da):
            at = pl.multiple_of(kt * tk, tk)
            ka = kwin[pl.ds(at, tk), :]
            p = jnp.exp2(dot(ka, q2, 1, 1))
            if masked:
                st = st_ref[:1, i * tq : (i + 1) * tq]
                j = at + lax.broadcasted_iota(jnp.int32, (tk, tq), 0)
                t = row0 + i * tq + lax.broadcasted_iota(jnp.int32, (tk, tq), 1)
                keep = (j >= st) & (j <= t)
                p = jnp.where(jnp.concatenate([keep] * gs, axis=1), p, 0.0)
            grad = (p * dot(vwin[pl.ds(at, tk), :], da, 1, 1)).astype(BF)
            dv[pl.ds(at, tk), :] += dot(p.astype(BF), do2)
            dk[pl.ds(at, tk), :] += dot(grad, q2)
            dqs[...] += dot(grad, ka, 0, 0)

        def body(kt, carry, step=step, flo=flo, fhi=fhi):
            inside = (kt >= flo) & (kt < fhi)

            @pl.when(inside)
            def _():
                step(kt, False)

            @pl.when(jnp.logical_not(inside))
            def _():
                step(kt, True)

            return carry

        lax.fori_loop(lo, hi, body, 0)
        for g in range(gs):
            dq_ref[i * tq : (i + 1) * tq, heads[g]] = dqs[g * tq : (g + 1) * tq] * score_scale

    for b in range(nb):
        part = slice(b * span, (b + 1) * span)
        dkvs[b][:, :HD] = (dk[part, :] * (1.0 / log2e)).astype(BF)
        dkvs[b][:, HD:] = dv[part, :].astype(BF)


def flash_bwd(scalars, q, starts_row, das, outs, sums, segs, window, gs, tq, tk, heads):
    span, total = q.shape
    width = gs * HD
    h0, count = heads
    nc, nb, nq = len(das), window // span, span // tq
    rows = das[0].shape[0]
    chunk = lambda w: pl.BlockSpec((rows, w), lambda h, s: (0, h0 + h))
    seg_specs = [pl.BlockSpec((seg.shape[0], 2 * HD), lambda h, s: (0, h0 + h)) for seg in segs]
    pairs = span * (window // 2)
    return pl.pallas_call(
        functools.partial(
            flash_bwd_kernel, nc=nc, ns=len(segs), nb=nb, nq=nq, tq=tq, tk=tk, gs=gs,
            row0=window - span,
        ),
        grid_spec=grid_spec(
            1,
            (count,),
            [
                pl.BlockSpec((span, width), lambda h, s: (0, h0 + h)),
                pl.BlockSpec((8, span), lambda h, s: (0, 0)),
                *([chunk(width)] * (2 * nc)),
                *([chunk(HD)] * nc),
                *seg_specs,
            ],
            [
                pl.BlockSpec((span, width), lambda h, s: (0, h)),
                *([pl.BlockSpec((span, 2 * HD), lambda h, s: (0, h))] * nb),
            ],
            [
                pltpu.VMEM((window, HD), BF),
                pltpu.VMEM((window, 2 * HD), BF),
                pltpu.VMEM((window, HD), F32),
                pltpu.VMEM((window, HD), F32),
                pltpu.VMEM((gs * tq, HD), F32),
            ],
        ),
        out_shape=[sds((span, count * width), F32)] + [sds((span, count * 2 * HD), BF)] * nb,
        compiler_params=params(),
        cost_estimate=cost(O('c_fb', 1.0) * 72 * count * width // total),
        name="flash_bwd",
    )(scalars, q, starts_row, *das, *outs, *sums, *segs)


def mlp_kernel(*refs, np_):
    x_ref, parts = refs[0], refs[1 : 1 + np_]
    gain_ref, gh_ref, wg_ref, wu_ref, m_ref, h_ref, dg_ref, du_ref, gm_ref, acc = refs[1 + np_ :]
    j = pl.program_id(0)

    @pl.when(j == 0)
    def _():
        rows = x_ref.shape[0]
        for r in range(0, rows, 128):
            at = slice(r, r + 128)
            h1 = x_ref[at, :].astype(F32)
            for part in parts:
                h1 = h1 + part[at, :].astype(F32)
            m_ref[at, :] = (h1 * rms(h1) * gain_ref[...]).astype(BF)
        acc[...] = jnp.zeros_like(acc)

    m = m_ref[...]
    gate = dot(m, wg_ref[...])
    up = dot(m, wu_ref[...])
    gh = gh_ref[...].astype(F32)
    sig = jax.nn.sigmoid(gate)
    silu = gate * sig
    h_ref[...] = (silu * up).astype(BF)
    dg = (gh * up * (sig * (1.0 + gate * (1.0 - sig)))).astype(BF)
    du = (gh * silu).astype(BF)
    dg_ref[...] = dg
    du_ref[...] = du
    acc[...] += dot(dg, wg_ref[...], 1, 1) + dot(du, wu_ref[...], 1, 1)

    @pl.when(j == pl.num_programs(0) - 1)
    def _():
        gm_ref[...] = acc[...].astype(BF)


def mlp(x, parts, gh, gain, wg, wu, chunk, tf):
    rows, d = parts[0].shape
    ff = wg.shape[1]
    once = pl.Buffered(1)
    at_chunk = pl.BlockSpec((rows, d), lambda j: (chunk, 0), pipeline_mode=once)
    whole = pl.BlockSpec((rows, d), lambda j: (0, 0), pipeline_mode=once)
    tile = pl.BlockSpec((rows, tf), lambda j: (0, j))
    return pl.pallas_call(
        functools.partial(mlp_kernel, np_=len(parts)),
        grid=(ff // tf,),
        in_specs=[
            at_chunk,
            *([whole] * len(parts)),
            pl.BlockSpec((1, d), lambda j: (0, 0)),
            pl.BlockSpec((rows, tf), lambda j: (chunk, j)),
            pl.BlockSpec((d, tf), lambda j: (0, j)),
            pl.BlockSpec((d, tf), lambda j: (0, j)),
        ],
        out_specs=[
            pl.BlockSpec((rows, d), lambda j: (0, 0)), tile, tile, tile,
            pl.BlockSpec((rows, d), lambda j: (0, 0)),
        ],
        scratch_shapes=[pltpu.VMEM((rows, d), F32)],
        out_shape=[
            sds((rows, d), BF), sds((rows, ff), BF), sds((rows, ff), BF), sds((rows, ff), BF),
            sds((rows, d), BF),
        ],
        compiler_params=params(),
        cost_estimate=cost(O('c_mlp', 1.0) * 38),
        name="mlp",
    )(x, *parts, gain, gh, wg, wu)


def mid_kernel(*refs, np_, ng):
    x_ref, parts, grads = refs[0], refs[1 : 1 + np_], refs[1 + np_ : 1 + np_ + ng]
    gain_ref, cot_ref, w_ref, gh_ref, ga_ref, gn_ref = refs[1 + np_ + ng :]
    h1 = x_ref[...].astype(F32)
    for part in parts:
        h1 = h1 + part[...].astype(F32)
    inv = rms(h1)
    n2 = h1 * inv
    gm = grads[0][...].astype(F32)
    for grad in grads[1:]:
        gm = gm + grad[...].astype(F32)
    g2 = gm * gain_ref[...]
    gh = cot_ref[...].astype(F32) + inv * (g2 - n2 * jnp.mean(g2 * n2, axis=1, keepdims=True))
    low = gh.astype(BF)
    gh_ref[...] = low
    ga_ref[...] = dot(low, w_ref[...], 1, 1).astype(BF)
    add = fold_rows(gm * n2)

    @pl.when(pl.program_id(0) == 0)
    def _():
        gn_ref[...] = add

    @pl.when(pl.program_id(0) > 0)
    def _():
        gn_ref[...] += add


def mid_backward(x, parts, grads, cot, gain, w_out, chunk, tm):
    rows, d = parts[0].shape
    n = w_out.shape[0]
    tiles = rows // tm
    at_chunk = pl.BlockSpec((tm, d), lambda i: (chunk * tiles + i, 0))
    tile = pl.BlockSpec((tm, d), lambda i: (i, 0))
    return pl.pallas_call(
        functools.partial(mid_kernel, np_=len(parts), ng=len(grads)),
        grid=(tiles,),
        in_specs=[
            at_chunk, *([tile] * (len(parts) + len(grads))), fixed((1, d)), at_chunk, fixed((n, d))
        ],
        out_specs=[tile, pl.BlockSpec((tm, n), lambda i: (i, 0)), pl.BlockSpec((8, d), lambda i: (0, 0))],
        out_shape=[sds((rows, d), BF), sds((rows, n), BF), sds((8, d), F32)],
        compiler_params=params(),
        cost_estimate=cost(O('c_mid', 1.0) * 11),
        name="mid_backward",
    )(x, *parts, *grads, gain, cot, w_out)


def head_back(grad, raw, hg, cosine, sine):
    inv = rms(raw)
    n = raw * inv
    du = grad * cosine + pltpu.roll(grad * sine, HD // 2, 1)
    dn = du * hg
    return inv * (dn - n * jnp.mean(dn * n, axis=1, keepdims=True)), fold_rows(du * n)


def add_out(ref, value):
    @pl.when(pl.program_id(0) == 0)
    def _():
        ref[...] = value

    @pl.when(pl.program_id(0) > 0)
    def _():
        ref[...] += value


def q_back_kernel(*refs, ng):
    dqs = refs[:ng]
    raw_ref, cos_ref, sin_ref, hg_ref, low_ref, gain_ref = refs[ng:]
    total = jnp.zeros(gain_ref.shape, F32)
    per = dqs[0].shape[1] // HD
    for h in range(raw_ref.shape[1] // HD):
        at, sub = slice(h * HD, (h + 1) * HD), slice(h % per * HD, (h % per + 1) * HD)
        back, part = head_back(
            dqs[h // per][:, sub], raw_ref[:, at], hg_ref[...], cos_ref[...], sin_ref[...]
        )
        low_ref[:, at] = back.astype(BF)
        total = total + part
    add_out(gain_ref, total)


def q_back(dqs, raw, cosine, sine, hg, tm):
    rows, n = raw.shape
    tile = pl.BlockSpec((tm, n), lambda i: (i, 0))
    part = pl.BlockSpec((tm, n // len(dqs)), lambda i: (i, 0))
    table = pl.BlockSpec((tm, HD), lambda i: (i, 0))
    return pl.pallas_call(
        functools.partial(q_back_kernel, ng=len(dqs)),
        grid=(rows // tm,),
        in_specs=[*([part] * len(dqs)), tile, table, table, fixed((1, HD))],
        out_specs=[tile, pl.BlockSpec((8, HD), lambda i: (0, 0))],
        out_shape=[sds((rows, n), BF), sds((8, HD), F32)],
        compiler_params=params(),
        cost_estimate=cost(O('c_qb', 1.0) * 8.5),
        name="q_back",
    )(*dqs, raw, cosine, sine, hg)


def in_kernel(s_ref, *refs, ng, nk):
    groups = [refs[g * nk : (g + 1) * nk] for g in range(ng)]
    (raw_ref, dq_ref, x_ref, cos_ref, sin_ref, hg_ref, wq_ref, wk_ref, wv_ref,
     low_ref, ga_ref, gain_ref, gn_ref) = refs[ng * nk :]
    heads = raw_ref.shape[1] // HD
    per = heads // ng
    total = jnp.zeros(gain_ref.shape, F32)
    for h in range(heads):
        k_at = slice(2 * (h % per) * HD, (2 * (h % per) + 1) * HD)
        v_at = slice((2 * (h % per) + 1) * HD, (2 * (h % per) + 2) * HD)
        dk, dv = 0.0, 0.0
        for ref in groups[h // per]:
            dk = dk + ref[:, k_at].astype(F32)
            dv = dv + ref[:, v_at].astype(F32)
        at = slice(h * HD, (h + 1) * HD)
        back, part = head_back(dk, raw_ref[:, at], hg_ref[...], cos_ref[...], sin_ref[...])
        low_ref[:, at] = back.astype(BF)
        low_ref[:, (heads + h) * HD : (heads + h + 1) * HD] = dv.astype(BF)
        total = total + part
    add_out(gain_ref, total)
    low = low_ref[...]
    ga = (
        dot(dq_ref[...], wq_ref[...], 1, 1)
        + dot(low[:, : heads * HD], wk_ref[...], 1, 1)
        + dot(low[:, heads * HD :], wv_ref[...], 1, 1)
    )
    ga_ref[...] = ga.astype(BF)
    x = x_ref[...].astype(F32)
    add_out(gn_ref, fold_rows(ga * (x * rms(x))))


def in_back(groups, raw, dq_low, x, base_tile, cosine, sine, hg, wq, wk, wv, tm):
    rows, n = raw.shape
    d = x.shape[1]
    nq = wq.shape[1]
    ng, nk = len(groups), len(groups[0])
    moved = lambda width: pl.BlockSpec((tm, width), lambda i, s: (s[0] + i, 0))
    tile = lambda width: pl.BlockSpec((tm, width), lambda i, s: (i, 0))
    return pl.pallas_call(
        functools.partial(in_kernel, ng=ng, nk=nk),
        grid_spec=grid_spec(
            1,
            (rows // tm,),
            [
                *([moved(2 * n // ng)] * (ng * nk)),
                tile(n), moved(nq), moved(d), moved(HD), moved(HD),
                fixed((1, HD)), fixed((d, nq)), fixed((d, n)), fixed((d, n)),
            ],
            [
                tile(2 * n), tile(d),
                pl.BlockSpec((8, HD), lambda i, s: (0, 0)), pl.BlockSpec((8, d), lambda i, s: (0, 0)),
            ],
        ),
        out_shape=[sds((rows, 2 * n), BF), sds((rows, d), BF), sds((8, HD), F32), sds((8, d), F32)],
        compiler_params=params(),
        cost_estimate=cost(O('c_in', 1.0) * 12.5),
        name="in_back",
    )(
        jnp.reshape(base_tile, (1,)), *[v for g in groups for v in g], raw, dq_low, x, cosine,
        sine, hg, wq, wk, wv,
    )


def pick_tile(n):
    for tile in (1536, 1024, 768, 512, 384, 256, 128):
        if n % tile == 0 and n > tile:
            return tile
    return n


def product(refs, nt):
    stack = lambda ks: jnp.concatenate([refs[k][...] for k in ks], axis=0)
    return dot(stack(range(0, 2 * nt, 2)), stack(range(1, 2 * nt, 2)), 0, 0)


def pieces_of(total, row_type, ns):
    size = total.shape[0 if row_type else 1] // ns
    for n in range(ns):
        yield total[n * size : (n + 1) * size] if row_type else total[:, n * size : (n + 1) * size]


def wgrad_kernel(s_ref, *refs, nt, na, row_type, ns, seq_first):
    adds, out_ref = refs[2 * nt : 2 * nt + na], refs[2 * nt + na]
    for n, piece in enumerate(pieces_of(product(refs, nt), row_type, ns)):
        for add in adds:
            piece = piece + add[0, n].astype(F32)
        out_ref[(n, 0) if seq_first else (0, n)] = piece.astype(BF)


def after(value, *others):
    return lax.optimization_barrier((value, *others))[0]


def nought(value):
    return jnp.minimum(jnp.abs(value[:1, :1].astype(F32)), 0.0)


def wgrad(terms, blocks, addends, row_type, nd, ns, rows, behind, seq_first=False):
    nb, nt = len(blocks), len(terms)
    scalars = jnp.stack(
        [jnp.asarray(v, jnp.int32) for v in blocks]
        + [jnp.asarray(v(), jnp.int32) for t in terms for v in (t[1], t[3])]
    )
    scalars = after(scalars, *behind)
    left, right = terms[0][0].shape[1], terms[0][2].shape[1]
    ins = []
    if row_type:
        bw = left // nd
        tile = pick_tile(right)
        steps = right // tile
        for n in range(nt):
            ins.append(pl.BlockSpec((rows, bw), lambda b, t, s, n=n: (s[nb + 2 * n], s[b])))
            ins.append(pl.BlockSpec((rows, tile), lambda b, t, s, n=n: (s[nb + 2 * n + 1], t)))
        out_dims = (ns, bw // ns, right)
        block = (1, ns, bw // ns, tile)
        at = lambda b, t, s: (b, 0, 0, t)
        add_at = lambda k: lambda b, t, s: (k, 0, 0, t)
    else:
        bw = right // nd
        tile = pick_tile(left)
        steps = left // tile
        for n in range(nt):
            ins.append(pl.BlockSpec((rows, tile), lambda b, t, s, n=n: (s[nb + 2 * n], t)))
            ins.append(pl.BlockSpec((rows, bw), lambda b, t, s, n=n: (s[nb + 2 * n + 1], s[b])))
        out_dims = (ns, left, bw // ns)
        block = (1, ns, tile, bw // ns)
        at = lambda b, t, s: (b, 0, t, 0)
        add_at = lambda k: lambda b, t, s: (k, 0, t, 0)
    work = 2e-9 * nt * rows * left * right / nd
    operands = [v for t in terms for v in (t[0], t[2])]
    for arr, k in addends:
        ins.append(pl.BlockSpec(block, at if k is None else add_at(k)))
        operands.append(arr)
    out_dims = (ns, nb, *out_dims[1:]) if seq_first else (nb, *out_dims)
    out_block, out_at = block, at
    if seq_first:
        out_block = (block[1], 1, *block[2:])
        out_at = lambda *a: (0, at(*a)[0], *at(*a)[2:])
    return pl.pallas_call(
        functools.partial(
            wgrad_kernel, nt=nt, na=len(addends), row_type=row_type, ns=ns, seq_first=seq_first
        ),
        grid_spec=grid_spec(1, (nb, steps), ins, pl.BlockSpec(out_block, out_at)),
        out_shape=sds(out_dims, BF),
        compiler_params=params(),
        cost_estimate=cost(O('c_wg', 1.0) * (1 + 2.3 * work * nb)),
        name="wgrad",
    )(scalars, *operands)


def flip(d, bits):
    return {1: d + 1 - 2 * (d % 2), 2: d + 2 - 4 * (d // 2), 3: 3 - d}[bits]


def wgrad_send_kernel(*refs, nt, row_type, ns, steps, tile):
    ins, out_ref = refs[: 2 * nt], refs[2 * nt]
    slots, send_sem, recv_sem = refs[2 * nt + 1 : 2 * nt + 4]
    b, t = pl.program_id(0), pl.program_id(1)
    k = b * steps + t
    last = 2 * steps - 1
    partner = {"dp": flip(lax.axis_index("dp"), 1)}

    @pl.when(k == 0)
    def _():
        barrier = pltpu.get_barrier_semaphore()
        pl.semaphore_signal(
            barrier, inc=1, device_id=partner, device_id_type=pl.DeviceIdType.MESH
        )
        pl.semaphore_wait(barrier, 1)

    def copy(src, dst, slot):
        return pltpu.make_async_remote_copy(
            src_ref=src, dst_ref=dst, send_sem=send_sem.at[slot], recv_sem=recv_sem,
            device_id=partner, device_id_type=pl.DeviceIdType.MESH,
        )

    def place(b, t):
        at = pl.ds(pl.multiple_of(t * tile, tile), tile)
        return out_ref.at[b, :, :, at] if row_type else out_ref.at[b, :, at, :]

    slot = k % 2

    @pl.when(k >= 2)
    def _():
        copy(slots.at[slot], place(b, t), slot).wait_send()

    for n, piece in enumerate(pieces_of(product(ins, nt), row_type, ns)):
        slots[slot, n] = piece.astype(BF)
    copy(slots.at[slot], place(b, t), slot).start()

    @pl.when(k == last)
    def _():
        copy(slots.at[1 - slot], place(b, t), 1 - slot).wait_send()
        copy(slots.at[slot], place(b, t), slot).wait_send()
        copy(out_ref, out_ref, slot).wait_recv()


def wgrad_send(terms, row_type, nd, ns, rows, ident, behind):
    nt = len(terms)
    left, right = terms[0][0].shape[1], terms[0][2].shape[1]
    block = lambda b: jnp.where(
        b == 0, flip(lax.axis_index("dp"), 1), flip(lax.axis_index("dp"), 3)
    )
    ins = []
    if row_type:
        bw = left // nd
        tile = pick_tile(right)
        steps = right // tile
        for t in terms:
            ins.append(pl.BlockSpec((rows, bw), lambda b, s, r=t[1]: (r(), block(b))))
            ins.append(pl.BlockSpec((rows, tile), lambda b, s, r=t[3]: (r(), s)))
        out_dims, slot = (ns, bw // ns, right), (ns, bw // ns, tile)
    else:
        bw = right // nd
        tile = pick_tile(left)
        steps = left // tile
        for t in terms:
            ins.append(pl.BlockSpec((rows, tile), lambda b, s, r=t[1]: (r(), s)))
            ins.append(pl.BlockSpec((rows, bw), lambda b, s, r=t[3]: (r(), block(b))))
        out_dims, slot = (ns, left, bw // ns), (ns, tile, bw // ns)
    work = 2e-9 * nt * rows * left * right / nd
    operands = [v for t in terms for v in (t[0], t[2])]
    operands[0] = after(operands[0], *behind)
    return pl.pallas_call(
        functools.partial(
            wgrad_send_kernel, nt=nt, row_type=row_type, ns=ns, steps=steps, tile=tile
        ),
        grid=(2, steps),
        in_specs=ins,
        out_specs=pl.BlockSpec(memory_space=pl.ANY),
        scratch_shapes=[
            pltpu.VMEM((2, *slot), BF), pltpu.SemaphoreType.DMA((2,)), pltpu.SemaphoreType.DMA,
        ],
        out_shape=sds((2, *out_dims), BF),
        compiler_params=params(collective_id=ident, has_side_effects=True),
        cost_estimate=cost(O('c_ws', 1.0) * (2 + 3.4 * work)),
        name="wgrad_send",
    )(*operands)


class Shrink:
    def __init__(self, terms, row_type, ahead=None, small=False, *, nd, ns, rows):
        self.small, self.pair = small, None
        self.args, self.nd = (terms, row_type), nd
        self.ahead = ahead
        self.ident = ahead.ident + 1 if ahead else 0
        self.sizes = (nd, ns, rows)
        self.d = lax.axis_index("dp")

    def make(self, blocks, adds, behind, **more):
        terms, row_type = self.args
        return wgrad(terms, blocks, adds, row_type, *self.sizes, behind, **more)

    def send(self, *behind):
        terms, row_type = self.args
        self.got = wgrad_send(terms, row_type, *self.sizes, self.ident, behind)
        return self.got

    def far(self, *behind):
        out = self.make([self.d ^ 2], [(self.got, 1)], behind)
        first = self.ahead
        for _ in range(O('serial', 1)):
            first = first.ahead if first else None
        first = [first.come] if first and first.pair is None and O('serial', 1) < 3 else []
        self.come = lax.ppermute(
            after(out, *first), "dp", [(k, k ^ 2) for k in range(self.nd)]
        )
        return out

    def both(self, *behind):
        out = self.make([self.d, self.d ^ 2], [(self.got, None)], behind, seq_first=True)
        self.pair = lax.psum_scatter(out, "seq", scatter_dimension=0)
        return out

    def near(self, *behind):
        self.here = self.make([self.d], [(self.got, 0), (self.come, 0)], behind)
        if not self.small:
            self.share = lax.psum_scatter(self.here[0], "seq", scatter_dimension=0)
        return self.here

    def finish(self):
        if self.pair is not None:
            come = lax.ppermute(self.pair[1], "dp", [(k, k ^ 2) for k in range(self.nd)])
            return self.pair[0].astype(F32) + come.astype(F32)
        if not self.small:
            return self.share.astype(F32)
        z, ns = lax.axis_index("seq"), self.sizes[1]
        piece = lambda j: lax.dynamic_index_in_dim(self.here[0], j, 0, keepdims=False)
        first = jnp.stack([piece(z ^ 1), piece(z ^ 3)])
        first = lax.ppermute(first, "seq", [(k, k ^ 1) for k in range(ns)]).astype(F32)
        second = (piece(z ^ 2).astype(F32) + first[1]).astype(BF)
        second = lax.ppermute(second, "seq", [(k, k ^ 2) for k in range(ns)])
        return piece(z).astype(F32) + first[0] + second.astype(F32)


def final_kernel(x_ref, ga_ref, gb_ref, h0_ref, h1_ref, gain_ref, s_ref, out_ref):
    x = x_ref[...].astype(F32)
    inv = rms(x)
    n1 = x * inv
    g1 = (ga_ref[...].astype(F32) + gb_ref[...].astype(F32)) * gain_ref[...]
    gh = jnp.where(s_ref[0] == 0, h0_ref[...].astype(F32), h1_ref[...].astype(F32))
    out_ref[...] = (gh + inv * (g1 - n1 * jnp.mean(g1 * n1, axis=1, keepdims=True))).astype(BF)


def final(x, ga, gb, h0, h1, gain, y, tm):
    rows, d = x.shape
    tile = pl.BlockSpec((tm, d), lambda i: (i, 0))
    return pl.pallas_call(
        final_kernel,
        grid=(rows // tm,),
        in_specs=[tile] * 5 + [fixed((1, d)), pl.BlockSpec(memory_space=pltpu.SMEM)],
        out_specs=tile,
        out_shape=sds((rows, d), BF),
        compiler_params=params(),
        cost_estimate=cost(O('c_fin', 1.0) * 8),
        name="final",
    )(x, ga, gb, h0, h1, gain, jnp.reshape(y, (1,)))


def per_device(
    tokens, doc_lengths, w_query, w_key, w_value, w_out, w_gate, w_up, w_down,
    norm_attn, norm_mlp, query_norm, key_norm, cotangent, *, nd, ns, nt,
):
    tokens, cotangent = tokens[0], cotangent[0]
    own_rows, d = tokens.shape
    span = own_rows * nt
    rows = span // 2
    heads_kv = w_key.shape[1] // HD
    gs = w_query.shape[1] // w_key.shape[1]
    z, y = lax.axis_index("seq"), lax.axis_index("tensor")
    row = lambda v: v[None, :]
    tm = 256
    tq = tk = 512
    swap = lambda v: lax.ppermute(v, "tensor", [(0, 1), (1, 0)])
    pick = lambda a, b: jnp.where(y == 0, a, b)

    back = min(ns - 1, -(-(LONGEST - 1) // span))
    window = (back + 1) * span
    ends = jnp.cumsum(doc_lengths[0])
    positions = z * span + jnp.arange(span, dtype=jnp.int32)
    starts = jnp.max(jnp.where(ends[None, :] <= positions[:, None], ends[None, :], 0), axis=1)
    half = HD // 2
    inverse = rope_base ** (-(jnp.arange(half, dtype=F32) * 2.0 / HD))
    angles = (positions - starts).astype(F32)[:, None] * inverse[None, :]
    cosine = jnp.tile(jnp.cos(angles), (1, 2))
    sine = jnp.sin(angles)
    sine = jnp.concatenate([-sine, sine], axis=1)
    rel = jnp.clip(starts - (z - back) * span, 0, window - 1)
    starts_col = jnp.broadcast_to(rel[:, None], (span, HD))
    starts_row = jnp.broadcast_to(rel[None, :], (8, span))

    def bounds(first_row, count, w0, w1):
        heads = rel[first_row : first_row + count : tq]
        tails = rel[first_row + tq - 1 : first_row + count : tq]
        at = window - span + first_row + tq * jnp.arange(count // tq, dtype=jnp.int32)
        inside = lambda v: jnp.clip(v - w0, 0, w1 - w0)
        up = lambda v: (v + tk - 1) // tk
        return [inside(heads) // tk, up(inside(at + tq)), up(inside(tails)), inside(at + 1) // tk]

    if nt == 2:
        other = swap(tokens)
        cot_in, other = lax.optimization_barrier((cotangent, other))
        cot_other = swap(cot_in)
        pieces, bases = [tokens, other], [y * rows, (1 - y) * rows]
        cot = jnp.concatenate([pick(cotangent, cot_other), pick(cot_other, cotangent)], axis=0)
    else:
        everything = lax.all_gather(tokens, "tensor", axis=0, tiled=True)
        cot = lax.all_gather(cotangent, "tensor", axis=0, tiled=True)
        pieces, bases = [everything[:rows], everything[rows:]], [0, rows]
    bases = [jnp.asarray(b, jnp.int32) for b in bases]
    base_tiles = [b // tm for b in bases]

    segs, seg_bases = [[] for _ in range(back + 1)], [[] for _ in range(back + 1)]
    raws = []
    ahead = [(k, k + 1) for k in range(ns - 1)]
    for x_piece, base, base_tile in zip(pieces, bases, base_tiles):
        if raws and O('e_kv_hop'):
            base_tile = after(base_tile, segs[1][0])
        kv, raw = project_kv(
            x_piece, base_tile, row(norm_attn), w_key, w_value, cosine, sine, row(key_norm), tm
        )
        raws.append(raw)
        for hop in range(back + 1):
            segs[hop].append(kv)
            seg_bases[hop].append((back - hop) * span + base)
            if hop < back:
                kv = lax.ppermute(kv, "seq", ahead)
    x_all, attn_in, query, q_raw = project_q(
        pieces[0], pieces[1], jnp.stack(base_tiles), row(norm_attn), w_query, cosine, sine,
        row(query_norm), tm,
    )

    attend = functools.partial(flash_fwd, bounds, gs=gs, tq=tq, tk=tk, window=window)
    prior = []
    for hop in range(back):
        part = ((back - hop) * span, (back - hop + 1) * span)
        prior = attend(
            seg_bases[hop], query, starts_col, segs[hop], prior, part=part, row_at=0, rows=span,
            last=False,
        )
    outs, sums, parts = [], [], []
    for c in range(2):
        out, total = attend(
            seg_bases[back], query, after(starts_col, *[v[0] for v in parts]), segs[back], prior, part=(0, span),
            row_at=c * rows, rows=rows, last=True,
        )
        outs.append(out)
        sums.append(total)
        partial = dot(out, w_out).astype(BF)
        parts.append([partial, swap(partial)] if nt == 2 else [lax.psum(partial, "tensor")])

    grad_hidden = dot(after(cot, partial), w_down, 1, 1).astype(BF)
    low_mlp, hidden, d_gate, d_up, grads = [], [], [], [], []
    tf = min(512, w_gate.shape[1] // 2)
    for c in range(2):
        m, h, dg, du, gm = mlp(
            x_all, parts[c], grad_hidden, after(row(norm_mlp), *low_mlp), w_gate, w_up, c, tf
        )
        low_mlp.append(m)
        hidden.append(h)
        d_gate.append(dg)
        d_up.append(du)
        grads.append([gm, swap(gm)] if nt == 2 else [lax.psum(gm, "tensor")])

    shrink = functools.partial(Shrink, nd=nd, ns=ns, rows=rows)
    zero = lambda: 0
    chunk = lambda c: lambda: c
    down = shrink([(hidden[c], zero, cot, chunk(c)) for c in range(2)], False, None, bool(O('p_down')))
    gate = shrink([(low_mlp[c], zero, d_gate[c], zero) for c in range(2)], True, down, bool(O('p_gate')))
    up = shrink([(low_mlp[c], zero, d_up[c], zero) for c in range(2)], True, gate, bool(O('p_up')))
    gh, g_att, g_norm_two = [], [], []

    def middle(c, *behind):
        low, ga, gn = mid_backward(
            x_all, parts[c], grads[c], cot, after(row(norm_mlp), *behind), w_out, c, tm
        )
        gh.append(low)
        g_att.append(ga)
        g_norm_two.append(gn)
        return low

    opt = lambda k, *v: list(v) if O(k) else []
    down.send()
    middle(0, *opt('e_m0_ds', down.got))
    zf = bool(O('zf'))
    df = down.both(*opt('e_df_m0', gh[0])) if zf else down.far(*opt('e_df_m0', gh[0]))
    gs_out = gate.send(*opt('e_gs_df', df), *opt('e_gs_m0', gh[0]))
    gf = gate.far() if O('e_gf_early') else None
    middle(1, *opt('e_m1_m0', gh[0]), *opt('e_m1_gs', gs_out), *opt('e_m1_gf', *([gf] if gf is not None else [])))
    if gf is None:
        gf = gate.far(gh[1])
    t = opt('e_fb0_gf', gf)
    hop_segs = [v for seg in segs for v in seg]
    hop_bases = jnp.stack([v for b in seg_bases for v in b])
    scalars = jnp.concatenate([*bounds(0, span, 0, window), hop_bases])
    halves = [(0, heads_kv)] if heads_kv == 1 else [(0, heads_kv // 2), (heads_kv // 2, heads_kv // 2)]
    behind = [(k + 1, k) for k in range(ns - 1)]
    dqs, dkvs, first_hops = [], [], []
    for part, heads in enumerate(halves):
        dq, *dkv = flash_bwd(
            after(scalars, *t), query, starts_row, g_att, outs, sums, hop_segs, window, gs, tq, tk,
            heads,
        )
        come = None
        for b in range(back):
            send = dkv[b]
            if come is not None:
                send = (send.astype(F32) + come.astype(F32)).astype(BF)
            come = lax.ppermute(send, "seq", behind)
            first_hops += [come] if b == 0 else []
        dqs.append(dq)
        dkvs.append([dkv[back]] + ([come] if come is not None else []))
        if part == 0:
            dn = dq if zf else down.near(*opt('e_dn_d0', dq))
            us = up.send(dq)
            t = opt('e_fb1_dn', dn) + opt('e_fb1_us', us) + opt('e_fb1_gf', gf)
            if O('e_fb1_uf'):
                uf = up.far()
                t += [uf]
    out_w = shrink([(outs[c], zero, gh[c], zero) for c in range(2)], False, up, bool(O('p_out',1)))
    if not O('e_fb1_uf'):
        uf = up.far(dqs[-1], *opt('e_uf_h0', first_hops[0] if first_hops else dqs[0]))
    gn_ = gate.near(*opt('e_gn_d1', dqs[-1]), *opt('e_gn_uf', uf), *opt('e_gn_hop', *first_hops), *opt('e_gn_h0', first_hops[0] if first_hops else dqs[0]))
    dq_low, g_qn = q_back(
        dqs, q_raw, cosine, sine,
        after(row(query_norm), *opt('e_qb_uf', uf), *opt('e_qb_gn', gn_), *opt('e_qb_hop', *first_hops), *opt('e_qb_h0', first_hops[0] if first_hops else dqs[0])), tm,
    )
    query_w = shrink([(attn_in, chunk(c), dq_low, chunk(c)) for c in range(2)], True, out_w, bool(O('p_q',1)))
    os_ = out_w.send(dq_low, *opt('e_os_gn', gn_))
    qs_ = query_w.send(*opt('e_qs_os', os_))
    of_ = out_w.far(*opt('e_of_qs', qs_))
    qf_ = query_w.far(*opt('e_qf_of', of_))
    w_down_later = after(w_down, dq_low) if O('e_dp_q') else after(w_down, gh[1]) if O('e_dp_m') else w_down
    downs = [dot(hidden[c], w_down_later).astype(BF) for c in range(2)]
    come_down = swap(pick(downs[1], downs[0])) if nt == 2 else downs[0]
    un = up.near(*opt('e_un_qf', qf_), *opt('e_un_d1', dqs[-1]), *opt('e_un_dp', *downs), *opt('e_un_of', of_))
    t = opt('e_in_qf', qf_) + opt('e_in_dp', *downs) + opt('e_in_cd', come_down) + opt('e_in_un', un)

    lows, gas, g_kn, g_norm_one = [None] * 2, [None] * 2, [], []
    for n in (1, 0):
        lows[n], gas[n], gain_part, norm_part = in_back(
            dkvs, raws[n], dq_low, x_all, base_tiles[n], cosine, sine, after(row(key_norm), *t),
            w_query, w_key, w_value, tm,
        )
        g_kn.append(gain_part)
        g_norm_one.append(norm_part)
    kv_cut = heads_kv * HD
    own_half = lambda: lax.axis_index("tensor")
    half_of = lambda n: chunk(n) if nt != 2 else own_half if n == 0 else lambda: 1 - own_half()
    kv_w = shrink([(attn_in, half_of(n), lows[n], zero) for n in range(2)], True, query_w, bool(O('p_kv',1)))
    ks_ = kv_w.send(*opt('e_ks_un', un))
    kf_ = kv_w.far(*opt('e_kf_un', un))
    on_ = out_w.near(*opt('e_on_kf', kf_))
    qn_ = query_w.near(*opt('e_qn_on', on_))
    gain_last = after(row(norm_attn), *opt('e_fin_qn', qn_), *opt('e_fin_kf', kf_), *opt('e_fin_on', on_))

    up32 = lambda v: v.astype(F32)
    if nt == 2:
        result = up32(tokens) + up32(pick(downs[0], downs[1])) + up32(come_down)
        for n in range(2):
            result = result + up32(pick(parts[0][n], parts[1][n]))
        grad_tokens = final(tokens, gas[0], swap(gas[1]), gh[0], gh[1], gain_last, y, tm)
    else:
        scatter = lambda v: lax.psum_scatter(v, "tensor", scatter_dimension=0, tiled=True)
        mine = lambda pair: lax.dynamic_slice_in_dim(
            jnp.concatenate(pair, axis=0), y * own_rows, own_rows
        )
        result = up32(tokens) + up32(scatter(jnp.concatenate(downs, axis=0)))
        result = result + up32(mine([parts[0][0], parts[1][0]]))
        x32 = up32(tokens)
        inv = rms(x32)
        n1 = x32 * inv
        g1 = up32(scatter(jnp.concatenate(gas, axis=0))) * row(norm_attn)
        moved = inv * (g1 - n1 * jnp.mean(g1 * n1, axis=1, keepdims=True))
        grad_tokens = (up32(mine(gh)) + moved).astype(BF)
    kn_ = kv_w.near(*opt('e_kn_fin', grad_tokens))
    g_down, g_gate, g_up, g_out, g_query, g_kv = [
        v.finish() for v in (down, gate, up, out_w, query_w, kv_w)
    ]

    share = 1.0 / nt
    fold = lambda pair: jnp.sum(pair[0] + pair[1], axis=0)
    axes = (("dp", nd), ("seq", ns), ("tensor", nt))
    packed = jnp.concatenate(
        [fold(g_norm_one), fold(g_norm_two) * share, jnp.sum(g_qn, axis=0), fold(g_kn)]
    )
    packed = total_sum(after(packed, *opt('e_pk_fin', grad_tokens), *opt('e_pk_kf', kf_), *opt('e_pk_kn', kn_), *opt('e_pk_kc', kv_w.come)), axes)
    return (
        result.astype(BF)[None], grad_tokens[None], g_query, g_kv[:, :kv_cut], g_kv[:, kv_cut:],
        g_out, g_gate, g_up, g_down,
        packed[:d], packed[d : 2 * d], packed[2 * d : 2 * d + HD], packed[2 * d + HD :],
    )


def total_sum(v, sizes):
    for name, size in sizes:
        step = 1
        while step < size:
            come = lambda k: lax.ppermute(v, name, [(i, i ^ k * step) for i in range(size)])
            if 4 * step <= size:
                v = (v + come(1)) + (come(2) + come(3))
                step *= 4
            else:
                v = v + come(1)
                step *= 2
    return v


def solution(mesh):
    sizes = dict(nd=mesh.shape["dp"], ns=mesh.shape["seq"], nt=mesh.shape["tensor"])
    rows, cols, both = P("dp", ("seq", "tensor"), None), P(None, "tensor"), ("dp", "seq")
    return jax.shard_map(
        functools.partial(per_device, **sizes),
        mesh=mesh,
        in_specs=(
            rows, P("dp", None), cols, cols, cols, P("tensor", None), cols, cols, P("tensor", None),
            P(), P(), P(), P(), rows,
        ),
        out_specs=(
            rows, rows, P(both, "tensor"), P(both, "tensor"), P(both, "tensor"), P("tensor", both),
            P(both, "tensor"), P(both, "tensor"), P("tensor", both), P(), P(), P(), P(),
        ),
        check_vma=False,
    )
```

```python
import functools
import math

import jax
import jax.numpy as jnp
from jax import lax
from jax.experimental import pallas as pl
from jax.experimental.pallas import tpu as pltpu
from jax.sharding import PartitionSpec as P

HD = 128
LONGEST = 2048
eps_norm = 1e-06
rope_base = 1000000.0
score_scale = HD ** (-0.5)
log2e = math.log2(math.e)
exp_scale = score_scale * log2e
BF = jnp.bfloat16
F32 = jnp.float32
MIB = 1 << 20
PLAN = {
    "c_fin": 0.3,
    "c_in": 0.3,
    "c_mid": 1.0,
    "c_wg": 1.6,
    "e_dp_q": 1,
    "e_fb0_gf": 1,
    "e_fb1_gf": 1,
    "e_fb1_uf": 1,
    "e_fb1_us": 1,
    "e_fin_qn": 1,
    "e_gf_early": 1,
    "e_gs_m0": 1,
    "e_in_cd": 1,
    "e_in_dp": 1,
    "e_in_qf": 1,
    "e_in_un": 1,
    "e_kf_un": 1,
    "e_kv_hop": 1,
    "e_m1_gf": 1,
    "e_m1_gs": 1,
    "e_on_kf": 1,
    "e_pk_fin": 1,
    "e_pk_kc": 1,
    "e_pk_kn": 1,
    "e_qb_gn": 1,
    "e_qb_uf": 1,
    "e_qf_of": 1,
    "e_qn_on": 1,
    "e_qs_os": 1,
    "e_un_qf": 1,
    "scale": 0.7,
    "serial": 3,
}


def O(key, default=0):
    return PLAN.get(key, default)


cost_scale = O("scale", 0.4)


def params(limit=56, **kw):
    return pltpu.CompilerParams(vmem_limit_bytes=limit * MIB, **kw)


def cost(us):
    return pl.CostEstimate(flops=int(us * cost_scale * 1e9), bytes_accessed=0, transcendentals=0)


def dot(a, b, ca=1, cb=0):
    return lax.dot_general(a, b, (((ca,), (cb,)), ((), ())), preferred_element_type=F32)


def fixed(shape):
    zeros = (0,) * len(shape)
    return pl.BlockSpec(shape, lambda *_: zeros, pipeline_mode=pl.Buffered(1))


def grid_spec(scalars, grid, ins, outs, scratch=()):
    return pltpu.PrefetchScalarGridSpec(
        num_scalar_prefetch=scalars, grid=grid, in_specs=ins, out_specs=outs, scratch_shapes=scratch
    )


def sds(shape, dtype):
    return jax.ShapeDtypeStruct(shape, dtype)


def rms(x):
    return lax.rsqrt(jnp.mean(x * x, axis=-1, keepdims=True) + eps_norm)


def fold_rows(v):
    return jnp.sum(v.reshape(v.shape[0] // 8, 8, v.shape[1]), axis=0)


def kv_kernel(s_ref, x_ref, gain_ref, wk_ref, wv_ref, cos_ref, sin_ref, hg_ref, kv_ref, raw_ref):
    x = x_ref[...].astype(F32)
    a = (x * rms(x) * gain_ref[...]).astype(BF)
    k = dot(a, wk_ref[...])
    v = dot(a, wv_ref[...]).astype(BF)
    raw_ref[...] = k
    cosine, sine, hg = cos_ref[...], sin_ref[...], hg_ref[...]
    for h in range(k.shape[1] // HD):
        kh = k[:, h * HD : (h + 1) * HD]
        u = kh * rms(kh) * hg
        r = u * cosine + pltpu.roll(u, HD // 2, 1) * sine
        kv_ref[:, 2 * h * HD : (2 * h + 1) * HD] = r.astype(BF)
        kv_ref[:, (2 * h + 1) * HD : (2 * h + 2) * HD] = v[:, h * HD : (h + 1) * HD]


def project_kv(x, base_tile, gain, wk, wv, cosine, sine, hg, tm):
    rows, d = x.shape
    n = wk.shape[1]
    return pl.pallas_call(
        kv_kernel,
        grid_spec=grid_spec(
            1,
            (rows // tm,),
            [
                pl.BlockSpec((tm, d), lambda i, s: (i, 0)),
                fixed((1, d)),
                fixed((d, n)),
                fixed((d, n)),
                pl.BlockSpec((tm, HD), lambda i, s: (s[0] + i, 0)),
                pl.BlockSpec((tm, HD), lambda i, s: (s[0] + i, 0)),
                fixed((1, HD)),
            ],
            [
                pl.BlockSpec((tm, 2 * n), lambda i, s: (i, 0)),
                pl.BlockSpec((tm, n), lambda i, s: (i, 0)),
            ],
        ),
        out_shape=[sds((rows, 2 * n), BF), sds((rows, n), F32)],
        compiler_params=params(),
        cost_estimate=cost(6.5),
        name="project_kv",
    )(jnp.reshape(base_tile, (1,)), x, gain, wk, wv, cosine, sine, hg)


def q_kernel(
    s_ref, xa_ref, xb_ref, gain_ref, w_ref, cos_ref, sin_ref, hg_ref, x_ref, a_ref, q_ref, raw_ref,
    *, half,
):
    xin = jnp.where(pl.program_id(0) < half, xa_ref[...].astype(F32), xb_ref[...].astype(F32))
    x_ref[...] = xin.astype(BF)
    a = (xin * rms(xin) * gain_ref[...]).astype(BF)
    a_ref[...] = a
    q = dot(a, w_ref[...])
    raw_ref[...] = q
    cosine, sine, hg = cos_ref[...], sin_ref[...], hg_ref[...]
    for h in range(q.shape[1] // HD):
        qh = q[:, h * HD : (h + 1) * HD]
        u = qh * rms(qh) * hg
        r = u * cosine + pltpu.roll(u, HD // 2, 1) * sine
        q_ref[:, h * HD : (h + 1) * HD] = (r * exp_scale).astype(BF)


def project_q(xa, xb, bases, gain, w, cosine, sine, hg, tm):
    rows, d = xa.shape
    n = w.shape[1]
    half = rows // tm
    out_at = lambda i, s: (s[i // half] + i % half, 0)
    total = 2 * rows
    return pl.pallas_call(
        functools.partial(q_kernel, half=half),
        grid_spec=grid_spec(
            1,
            (2 * half,),
            [
                pl.BlockSpec((tm, d), lambda i, s: (jnp.minimum(i, half - 1), 0)),
                pl.BlockSpec((tm, d), lambda i, s: (jnp.maximum(i - half, 0), 0)),
                fixed((1, d)),
                fixed((d, n)),
                pl.BlockSpec((tm, HD), out_at),
                pl.BlockSpec((tm, HD), out_at),
                fixed((1, HD)),
            ],
            [
                pl.BlockSpec((tm, d), out_at),
                pl.BlockSpec((tm, d), out_at),
                pl.BlockSpec((tm, n), out_at),
                pl.BlockSpec((tm, n), out_at),
            ],
        ),
        out_shape=[
            sds((total, d), BF), sds((total, d), BF), sds((total, n), BF), sds((total, n), F32)
        ],
        compiler_params=params(),
        cost_estimate=cost(13),
        name="project_q",
    )(bases, xa, xb, gain, w, cosine, sine, hg)


def fill_window(s_ref, at, segs, kwin, vwin):
    for n, seg in enumerate(segs):
        rows = seg.shape[0]
        base = pl.multiple_of(s_ref[at + n], math.gcd(rows, 256))
        kwin[pl.ds(base, rows), :HD] = seg[:, :HD]
        vwin[pl.ds(base, rows), :HD] = seg[:, HD:]


def spread(value, gs, tq):
    step = HD // gs
    return jnp.concatenate([value[:, g * step : g * step + 1] for g in range(gs)], axis=0)


def flash_fwd_kernel(s_ref, q_ref, st_ref, *rest, nseg, prior, last, nq, tq, tk, gs, w0, row0):
    segs, rest = rest[:nseg], rest[nseg:]
    acc_in, rest = rest[: 2 * prior], rest[2 * prior :]
    o_ref, l_ref, kwin, vwin, acc = rest
    i = pl.program_id(1)

    @pl.when(i == 0)
    def _():
        fill_window(s_ref, 4 * nq, segs, kwin, vwin)
        vwin[:, HD:] = jnp.ones(vwin[:, HD:].shape, BF)

    heads = [slice(g * HD, (g + 1) * HD) for g in range(gs)]
    q2 = jnp.concatenate([q_ref[:, hh] for hh in heads], axis=0)
    if prior:
        acc[:, :HD] = jnp.concatenate([acc_in[0][:, hh] for hh in heads], axis=0)
        acc[:, HD:] = jnp.broadcast_to(spread(acc_in[1], gs, tq), (gs * tq, HD))
    else:
        acc[...] = jnp.zeros_like(acc)
    lo, hi, flo, fhi = [s_ref[n * nq + i] for n in range(4)]

    def step(kt, masked):
        at = pl.multiple_of(kt * tk, tk)
        p = jnp.exp2(dot(q2, kwin[pl.ds(at, tk), :], 1, 1))
        if masked:
            st = st_ref[:, :1]
            j = w0 + at + lax.broadcasted_iota(jnp.int32, (tq, tk), 1)
            t = row0 + i * tq + lax.broadcasted_iota(jnp.int32, (tq, tk), 0)
            keep = (j >= st) & (j <= t)
            p = jnp.where(jnp.concatenate([keep] * gs, axis=0), p, 0.0)
        acc[...] += dot(p.astype(BF), vwin[pl.ds(at, tk), :])

    def body(kt, carry):
        inside = (kt >= flo) & (kt < fhi)

        @pl.when(inside)
        def _():
            step(kt, False)

        @pl.when(jnp.logical_not(inside))
        def _():
            step(kt, True)

        return carry

    lax.fori_loop(lo, hi, body, 0)
    total, out = acc[:, HD:], acc[:, :HD]
    if last:
        total = 1.0 / total
        out = (out * total).astype(BF)
    lane = lax.broadcasted_iota(jnp.int32, (tq, HD), 1)
    packed = total[:tq]
    for g in range(gs):
        o_ref[:, heads[g]] = out[g * tq : (g + 1) * tq]
        packed = jnp.where(lane >= g * (HD // gs), total[g * tq : (g + 1) * tq], packed)
    l_ref[...] = packed


def flash_fwd(bounds, bases, q, starts_col, segs, prior, window, part, row_at, rows, last, gs, tq, tk):
    width = gs * HD
    heads = q.shape[1] // width
    nq = rows // tq
    off = row_at // tq
    w0, w1 = part
    scalars = jnp.concatenate([*bounds(row_at, rows, w0, w1, tk), jnp.stack([b - w0 for b in bases])])
    seg_specs = [pl.BlockSpec((seg.shape[0], 2 * HD), lambda h, i, s: (0, h)) for seg in segs]
    pairs = rows * (w1 - w0) // 2
    moved = lambda w: pl.BlockSpec((tq, w), lambda h, i, s: (off + i, h))
    tile = lambda w: pl.BlockSpec((tq, w), lambda h, i, s: (i, h))
    return pl.pallas_call(
        functools.partial(
            flash_fwd_kernel, nseg=len(segs), prior=len(prior) // 2, last=last, nq=nq, tq=tq,
            tk=tk, gs=gs, w0=w0, row0=window - q.shape[0] + row_at,
        ),
        grid_spec=grid_spec(
            1,
            (heads, nq),
            [
                moved(width),
                pl.BlockSpec((tq, HD), lambda h, i, s: (off + i, 0)),
                *seg_specs,
                *([moved(width), moved(HD)] if prior else []),
            ],
            [tile(width), tile(HD)],
            [
                pltpu.VMEM((w1 - w0, HD), BF),
                pltpu.VMEM((w1 - w0, 2 * HD), BF),
                pltpu.VMEM((gs * tq, 2 * HD), F32),
            ],
        ),
        out_shape=[sds((rows, q.shape[1]), BF if last else F32), sds((rows, heads * HD), F32)],
        compiler_params=params(),
        cost_estimate=cost(7 * last + 19 * (1 - last)),
        name="flash_fwd",
    )(scalars, q, starts_col, *segs, *prior)


def flash_bwd_kernel(s_ref, q_ref, st_ref, *rest, nc, ns, nb, nq, tq, tk, gs, row0):
    das, outs, sums = rest[:nc], rest[nc : 2 * nc], rest[2 * nc : 3 * nc]
    segs = rest[3 * nc : 3 * nc + ns]
    dq_ref = rest[3 * nc + ns]
    dkvs = rest[3 * nc + ns + 1 : 3 * nc + ns + 1 + nb]
    kwin, vwin, dk, dv, dqs = rest[3 * nc + ns + 1 + nb :]
    span = dkvs[0].shape[0]

    fill_window(s_ref, 4 * nq, segs, kwin, vwin)
    lane = lax.broadcasted_iota(jnp.int32, (vwin.shape[0], HD), 1)
    vwin[:, HD:] = jnp.where(lane < 2, 1.0, 0.0).astype(BF)
    dk[...] = jnp.zeros_like(dk)
    dv[...] = jnp.zeros_like(dv)

    for i in range(nq):
        per = nq // nc
        c, r = i // per, i % per
        rows = slice(r * tq, (r + 1) * tq)
        heads = [slice(g * HD, (g + 1) * HD) for g in range(gs)]
        pile = lambda ref, rr: jnp.concatenate([ref[rr, hh] for hh in heads], axis=0)
        q2 = pile(q_ref, slice(i * tq, (i + 1) * tq))
        scaled = pile(das[c], rows).astype(F32) * spread(sums[c][rows, :], gs, tq)
        neg = -jnp.sum(scaled * pile(outs[c], rows).astype(F32), axis=1, keepdims=True)
        do2 = scaled.astype(BF)
        first = neg.astype(BF).astype(F32)
        ln = lax.broadcasted_iota(jnp.int32, (gs * tq, HD), 1)
        daug = jnp.where(ln == 0, first, jnp.where(ln == 1, neg - first, 0.0)).astype(BF)
        da = jnp.concatenate([do2, daug], axis=1)
        dqs[...] = jnp.zeros_like(dqs)
        lo, hi, flo, fhi = [s_ref[n * nq + i] for n in range(4)]

        def step(kt, masked, i=i, q2=q2, do2=do2, da=da):
            at = pl.multiple_of(kt * tk, tk)
            ka = kwin[pl.ds(at, tk), :]
            p = jnp.exp2(dot(ka, q2, 1, 1))
            if masked:
                st = st_ref[:1, i * tq : (i + 1) * tq]
                j = at + lax.broadcasted_iota(jnp.int32, (tk, tq), 0)
                t = row0 + i * tq + lax.broadcasted_iota(jnp.int32, (tk, tq), 1)
                keep = (j >= st) & (j <= t)
                p = jnp.where(jnp.concatenate([keep] * gs, axis=1), p, 0.0)
            grad = (p * dot(vwin[pl.ds(at, tk), :], da, 1, 1)).astype(BF)
            dv[pl.ds(at, tk), :] += dot(p.astype(BF), do2)
            dk[pl.ds(at, tk), :] += dot(grad, q2)
            dqs[...] += dot(grad, ka, 0, 0)

        def body(kt, carry, step=step, flo=flo, fhi=fhi):
            inside = (kt >= flo) & (kt < fhi)

            @pl.when(inside)
            def _():
                step(kt, False)

            @pl.when(jnp.logical_not(inside))
            def _():
                step(kt, True)

            return carry

        lax.fori_loop(lo, hi, body, 0)
        for g in range(gs):
            dq_ref[i * tq : (i + 1) * tq, heads[g]] = dqs[g * tq : (g + 1) * tq] * score_scale

    for b in range(nb):
        part = slice(b * span, (b + 1) * span)
        dkvs[b][:, :HD] = (dk[part, :] * (1.0 / log2e)).astype(BF)
        dkvs[b][:, HD:] = dv[part, :].astype(BF)


def flash_bwd(scalars, q, starts_row, das, outs, sums, segs, window, gs, tq, tk, heads):
    span, total = q.shape
    width = gs * HD
    h0, count = heads
    nc, nb, nq = len(das), window // span, span // tq
    rows = das[0].shape[0]
    chunk = lambda w: pl.BlockSpec((rows, w), lambda h, s: (0, h0 + h))
    seg_specs = [pl.BlockSpec((seg.shape[0], 2 * HD), lambda h, s: (0, h0 + h)) for seg in segs]
    pairs = span * (window // 2)
    return pl.pallas_call(
        functools.partial(
            flash_bwd_kernel, nc=nc, ns=len(segs), nb=nb, nq=nq, tq=tq, tk=tk, gs=gs,
            row0=window - span,
        ),
        grid_spec=grid_spec(
            1,
            (count,),
            [
                pl.BlockSpec((span, width), lambda h, s: (0, h0 + h)),
                pl.BlockSpec((8, span), lambda h, s: (0, 0)),
                *([chunk(width)] * (2 * nc)),
                *([chunk(HD)] * nc),
                *seg_specs,
            ],
            [
                pl.BlockSpec((span, width), lambda h, s: (0, h)),
                *([pl.BlockSpec((span, 2 * HD), lambda h, s: (0, h))] * nb),
            ],
            [
                pltpu.VMEM((window, HD), BF),
                pltpu.VMEM((window, 2 * HD), BF),
                pltpu.VMEM((window, HD), F32),
                pltpu.VMEM((window, HD), F32),
                pltpu.VMEM((gs * tq, HD), F32),
            ],
        ),
        out_shape=[sds((span, count * width), F32)] + [sds((span, count * 2 * HD), BF)] * nb,
        compiler_params=params(),
        cost_estimate=cost(O('c_fb', 1.0) * 72 * count * width // total),
        name="flash_bwd",
    )(scalars, q, starts_row, *das, *outs, *sums, *segs)


def mlp_kernel(*refs, np_):
    x_ref, parts = refs[0], refs[1 : 1 + np_]
    gain_ref, gh_ref, wg_ref, wu_ref, m_ref, h_ref, dg_ref, du_ref, gm_ref, acc = refs[1 + np_ :]
    j = pl.program_id(0)

    @pl.when(j == 0)
    def _():
        rows = x_ref.shape[0]
        for r in range(0, rows, 128):
            at = slice(r, r + 128)
            h1 = x_ref[at, :].astype(F32)
            for part in parts:
                h1 = h1 + part[at, :].astype(F32)
            m_ref[at, :] = (h1 * rms(h1) * gain_ref[...]).astype(BF)
        acc[...] = jnp.zeros_like(acc)

    m = m_ref[...]
    gate = dot(m, wg_ref[...])
    up = dot(m, wu_ref[...])
    gh = gh_ref[...].astype(F32)
    sig = jax.nn.sigmoid(gate)
    silu = gate * sig
    h_ref[...] = (silu * up).astype(BF)
    dg = (gh * up * (sig * (1.0 + gate * (1.0 - sig)))).astype(BF)
    du = (gh * silu).astype(BF)
    dg_ref[...] = dg
    du_ref[...] = du
    acc[...] += dot(dg, wg_ref[...], 1, 1) + dot(du, wu_ref[...], 1, 1)

    @pl.when(j == pl.num_programs(0) - 1)
    def _():
        gm_ref[...] = acc[...].astype(BF)


def mlp(x, parts, gh, gain, wg, wu, chunk, tf):
    rows, d = parts[0].shape
    ff = wg.shape[1]
    once = pl.Buffered(1)
    at_chunk = pl.BlockSpec((rows, d), lambda j: (chunk, 0), pipeline_mode=once)
    whole = pl.BlockSpec((rows, d), lambda j: (0, 0), pipeline_mode=once)
    tile = pl.BlockSpec((rows, tf), lambda j: (0, j))
    return pl.pallas_call(
        functools.partial(mlp_kernel, np_=len(parts)),
        grid=(ff // tf,),
        in_specs=[
            at_chunk,
            *([whole] * len(parts)),
            pl.BlockSpec((1, d), lambda j: (0, 0)),
            pl.BlockSpec((rows, tf), lambda j: (chunk, j)),
            pl.BlockSpec((d, tf), lambda j: (0, j)),
            pl.BlockSpec((d, tf), lambda j: (0, j)),
        ],
        out_specs=[
            pl.BlockSpec((rows, d), lambda j: (0, 0)), tile, tile, tile,
            pl.BlockSpec((rows, d), lambda j: (0, 0)),
        ],
        scratch_shapes=[pltpu.VMEM((rows, d), F32)],
        out_shape=[
            sds((rows, d), BF), sds((rows, ff), BF), sds((rows, ff), BF), sds((rows, ff), BF),
            sds((rows, d), BF),
        ],
        compiler_params=params(),
        cost_estimate=cost(O('c_mlp', 1.0) * 38),
        name="mlp",
    )(x, *parts, gain, gh, wg, wu)


def mid_kernel(*refs, np_, ng):
    x_ref, parts, grads = refs[0], refs[1 : 1 + np_], refs[1 + np_ : 1 + np_ + ng]
    gain_ref, cot_ref, w_ref, gh_ref, ga_ref, gn_ref = refs[1 + np_ + ng :]
    h1 = x_ref[...].astype(F32)
    for part in parts:
        h1 = h1 + part[...].astype(F32)
    inv = rms(h1)
    n2 = h1 * inv
    gm = grads[0][...].astype(F32)
    for grad in grads[1:]:
        gm = gm + grad[...].astype(F32)
    g2 = gm * gain_ref[...]
    gh = cot_ref[...].astype(F32) + inv * (g2 - n2 * jnp.mean(g2 * n2, axis=1, keepdims=True))
    low = gh.astype(BF)
    gh_ref[...] = low
    ga_ref[...] = dot(low, w_ref[...], 1, 1).astype(BF)
    add = fold_rows(gm * n2)

    @pl.when(pl.program_id(0) == 0)
    def _():
        gn_ref[...] = add

    @pl.when(pl.program_id(0) > 0)
    def _():
        gn_ref[...] += add


def mid_backward(x, parts, grads, cot, gain, w_out, chunk, tm):
    rows, d = parts[0].shape
    n = w_out.shape[0]
    tiles = rows // tm
    at_chunk = pl.BlockSpec((tm, d), lambda i: (chunk * tiles + i, 0))
    tile = pl.BlockSpec((tm, d), lambda i: (i, 0))
    return pl.pallas_call(
        functools.partial(mid_kernel, np_=len(parts), ng=len(grads)),
        grid=(tiles,),
        in_specs=[
            at_chunk, *([tile] * (len(parts) + len(grads))), fixed((1, d)), at_chunk, fixed((n, d))
        ],
        out_specs=[tile, pl.BlockSpec((tm, n), lambda i: (i, 0)), pl.BlockSpec((8, d), lambda i: (0, 0))],
        out_shape=[sds((rows, d), BF), sds((rows, n), BF), sds((8, d), F32)],
        compiler_params=params(),
        cost_estimate=cost(O('c_mid', 1.0) * 11),
        name="mid_backward",
    )(x, *parts, *grads, gain, cot, w_out)


def head_back(grad, raw, hg, cosine, sine):
    inv = rms(raw)
    n = raw * inv
    du = grad * cosine + pltpu.roll(grad * sine, HD // 2, 1)
    dn = du * hg
    return inv * (dn - n * jnp.mean(dn * n, axis=1, keepdims=True)), fold_rows(du * n)


def add_out(ref, value):
    @pl.when(pl.program_id(0) == 0)
    def _():
        ref[...] = value

    @pl.when(pl.program_id(0) > 0)
    def _():
        ref[...] += value


def q_back_kernel(*refs, ng):
    dqs = refs[:ng]
    raw_ref, cos_ref, sin_ref, hg_ref, low_ref, gain_ref = refs[ng:]
    total = jnp.zeros(gain_ref.shape, F32)
    per = dqs[0].shape[1] // HD
    for h in range(raw_ref.shape[1] // HD):
        at, sub = slice(h * HD, (h + 1) * HD), slice(h % per * HD, (h % per + 1) * HD)
        back, part = head_back(
            dqs[h // per][:, sub], raw_ref[:, at], hg_ref[...], cos_ref[...], sin_ref[...]
        )
        low_ref[:, at] = back.astype(BF)
        total = total + part
    add_out(gain_ref, total)


def q_back(dqs, raw, cosine, sine, hg, tm):
    rows, n = raw.shape
    tile = pl.BlockSpec((tm, n), lambda i: (i, 0))
    part = pl.BlockSpec((tm, n // len(dqs)), lambda i: (i, 0))
    table = pl.BlockSpec((tm, HD), lambda i: (i, 0))
    return pl.pallas_call(
        functools.partial(q_back_kernel, ng=len(dqs)),
        grid=(rows // tm,),
        in_specs=[*([part] * len(dqs)), tile, table, table, fixed((1, HD))],
        out_specs=[tile, pl.BlockSpec((8, HD), lambda i: (0, 0))],
        out_shape=[sds((rows, n), BF), sds((8, HD), F32)],
        compiler_params=params(),
        cost_estimate=cost(O('c_qb', 1.0) * 8.5),
        name="q_back",
    )(*dqs, raw, cosine, sine, hg)


def in_kernel(s_ref, *refs, ng, nk):
    groups = [refs[g * nk : (g + 1) * nk] for g in range(ng)]
    (raw_ref, dq_ref, x_ref, cos_ref, sin_ref, hg_ref, wq_ref, wk_ref, wv_ref,
     low_ref, ga_ref, gain_ref, gn_ref) = refs[ng * nk :]
    heads = raw_ref.shape[1] // HD
    per = heads // ng
    total = jnp.zeros(gain_ref.shape, F32)
    for h in range(heads):
        k_at = slice(2 * (h % per) * HD, (2 * (h % per) + 1) * HD)
        v_at = slice((2 * (h % per) + 1) * HD, (2 * (h % per) + 2) * HD)
        dk, dv = 0.0, 0.0
        for ref in groups[h // per]:
            dk = dk + ref[:, k_at].astype(F32)
            dv = dv + ref[:, v_at].astype(F32)
        at = slice(h * HD, (h + 1) * HD)
        back, part = head_back(dk, raw_ref[:, at], hg_ref[...], cos_ref[...], sin_ref[...])
        low_ref[:, at] = back.astype(BF)
        low_ref[:, (heads + h) * HD : (heads + h + 1) * HD] = dv.astype(BF)
        total = total + part
    add_out(gain_ref, total)
    low = low_ref[...]
    ga = (
        dot(dq_ref[...], wq_ref[...], 1, 1)
        + dot(low[:, : heads * HD], wk_ref[...], 1, 1)
        + dot(low[:, heads * HD :], wv_ref[...], 1, 1)
    )
    ga_ref[...] = ga.astype(BF)
    x = x_ref[...].astype(F32)
    add_out(gn_ref, fold_rows(ga * (x * rms(x))))


def in_back(groups, raw, dq_low, x, base_tile, cosine, sine, hg, wq, wk, wv, tm):
    rows, n = raw.shape
    d = x.shape[1]
    nq = wq.shape[1]
    ng, nk = len(groups), len(groups[0])
    moved = lambda width: pl.BlockSpec((tm, width), lambda i, s: (s[0] + i, 0))
    tile = lambda width: pl.BlockSpec((tm, width), lambda i, s: (i, 0))
    return pl.pallas_call(
        functools.partial(in_kernel, ng=ng, nk=nk),
        grid_spec=grid_spec(
            1,
            (rows // tm,),
            [
                *([moved(2 * n // ng)] * (ng * nk)),
                tile(n), moved(nq), moved(d), moved(HD), moved(HD),
                fixed((1, HD)), fixed((d, nq)), fixed((d, n)), fixed((d, n)),
            ],
            [
                tile(2 * n), tile(d),
                pl.BlockSpec((8, HD), lambda i, s: (0, 0)), pl.BlockSpec((8, d), lambda i, s: (0, 0)),
            ],
        ),
        out_shape=[sds((rows, 2 * n), BF), sds((rows, d), BF), sds((8, HD), F32), sds((8, d), F32)],
        compiler_params=params(),
        cost_estimate=cost(O('c_in', 1.0) * 12.5),
        name="in_back",
    )(
        jnp.reshape(base_tile, (1,)), *[v for g in groups for v in g], raw, dq_low, x, cosine,
        sine, hg, wq, wk, wv,
    )


def pick_tile(n):
    for tile in (1536, 1024, 768, 512, 384, 256, 128):
        if n % tile == 0 and n > tile:
            return tile
    return n


def product(refs, nt):
    stack = lambda ks: jnp.concatenate([refs[k][...] for k in ks], axis=0)
    return dot(stack(range(0, 2 * nt, 2)), stack(range(1, 2 * nt, 2)), 0, 0)


def pieces_of(total, row_type, ns):
    size = total.shape[0 if row_type else 1] // ns
    for n in range(ns):
        yield total[n * size : (n + 1) * size] if row_type else total[:, n * size : (n + 1) * size]


def wgrad_kernel(s_ref, *refs, nt, na, row_type, ns, seq_first):
    adds, out_ref = refs[2 * nt : 2 * nt + na], refs[2 * nt + na]
    for n, piece in enumerate(pieces_of(product(refs, nt), row_type, ns)):
        for add in adds:
            piece = piece + add[0, n].astype(F32)
        out_ref[(n, 0) if seq_first else (0, n)] = piece.astype(BF)


def after(value, *others):
    return lax.optimization_barrier((value, *others))[0]


def nought(value):
    return jnp.minimum(jnp.abs(value[:1, :1].astype(F32)), 0.0)


def wgrad(terms, blocks, addends, row_type, nd, ns, rows, behind, seq_first=False):
    nb, nt = len(blocks), len(terms)
    scalars = jnp.stack(
        [jnp.asarray(v, jnp.int32) for v in blocks]
        + [jnp.asarray(v(), jnp.int32) for t in terms for v in (t[1], t[3])]
    )
    scalars = after(scalars, *behind)
    left, right = terms[0][0].shape[1], terms[0][2].shape[1]
    ins = []
    if row_type:
        bw = left // nd
        tile = pick_tile(right)
        steps = right // tile
        for n in range(nt):
            ins.append(pl.BlockSpec((rows, bw), lambda b, t, s, n=n: (s[nb + 2 * n], s[b])))
            ins.append(pl.BlockSpec((rows, tile), lambda b, t, s, n=n: (s[nb + 2 * n + 1], t)))
        out_dims = (ns, bw // ns, right)
        block = (1, ns, bw // ns, tile)
        at = lambda b, t, s: (b, 0, 0, t)
        add_at = lambda k: lambda b, t, s: (k, 0, 0, t)
    else:
        bw = right // nd
        tile = pick_tile(left)
        steps = left // tile
        for n in range(nt):
            ins.append(pl.BlockSpec((rows, tile), lambda b, t, s, n=n: (s[nb + 2 * n], t)))
            ins.append(pl.BlockSpec((rows, bw), lambda b, t, s, n=n: (s[nb + 2 * n + 1], s[b])))
        out_dims = (ns, left, bw // ns)
        block = (1, ns, tile, bw // ns)
        at = lambda b, t, s: (b, 0, t, 0)
        add_at = lambda k: lambda b, t, s: (k, 0, t, 0)
    work = 2e-9 * nt * rows * left * right / nd
    operands = [v for t in terms for v in (t[0], t[2])]
    for arr, k in addends:
        ins.append(pl.BlockSpec(block, at if k is None else add_at(k)))
        operands.append(arr)
    out_dims = (ns, nb, *out_dims[1:]) if seq_first else (nb, *out_dims)
    out_block, out_at = block, at
    if seq_first:
        out_block = (block[1], 1, *block[2:])
        out_at = lambda *a: (0, at(*a)[0], *at(*a)[2:])
    return pl.pallas_call(
        functools.partial(
            wgrad_kernel, nt=nt, na=len(addends), row_type=row_type, ns=ns, seq_first=seq_first
        ),
        grid_spec=grid_spec(1, (nb, steps), ins, pl.BlockSpec(out_block, out_at)),
        out_shape=sds(out_dims, BF),
        compiler_params=params(),
        cost_estimate=cost(O('c_wg', 1.0) * (1 + 2.3 * work * nb)),
        name="wgrad",
    )(scalars, *operands)


def flip(d, bits):
    return {1: d + 1 - 2 * (d % 2), 2: d + 2 - 4 * (d // 2), 3: 3 - d}[bits]


def wgrad_send_kernel(*refs, nt, row_type, ns, steps, tile):
    ins, out_ref = refs[: 2 * nt], refs[2 * nt]
    slots, send_sem, recv_sem = refs[2 * nt + 1 : 2 * nt + 4]
    b, t = pl.program_id(0), pl.program_id(1)
    k = b * steps + t
    last = 2 * steps - 1
    partner = {"dp": flip(lax.axis_index("dp"), 1)}

    @pl.when(k == 0)
    def _():
        barrier = pltpu.get_barrier_semaphore()
        pl.semaphore_signal(
            barrier, inc=1, device_id=partner, device_id_type=pl.DeviceIdType.MESH
        )
        pl.semaphore_wait(barrier, 1)

    def copy(src, dst, slot):
        return pltpu.make_async_remote_copy(
            src_ref=src, dst_ref=dst, send_sem=send_sem.at[slot], recv_sem=recv_sem,
            device_id=partner, device_id_type=pl.DeviceIdType.MESH,
        )

    def place(b, t):
        at = pl.ds(pl.multiple_of(t * tile, tile), tile)
        return out_ref.at[b, :, :, at] if row_type else out_ref.at[b, :, at, :]

    slot = k % 2

    @pl.when(k >= 2)
    def _():
        copy(slots.at[slot], place(b, t), slot).wait_send()

    for n, piece in enumerate(pieces_of(product(ins, nt), row_type, ns)):
        slots[slot, n] = piece.astype(BF)
    copy(slots.at[slot], place(b, t), slot).start()

    @pl.when(k == last)
    def _():
        copy(slots.at[1 - slot], place(b, t), 1 - slot).wait_send()
        copy(slots.at[slot], place(b, t), slot).wait_send()
        copy(out_ref, out_ref, slot).wait_recv()


def wgrad_send(terms, row_type, nd, ns, rows, ident, behind):
    nt = len(terms)
    left, right = terms[0][0].shape[1], terms[0][2].shape[1]
    block = lambda b: jnp.where(
        b == 0, flip(lax.axis_index("dp"), 1), flip(lax.axis_index("dp"), 3)
    )
    ins = []
    if row_type:
        bw = left // nd
        tile = pick_tile(right)
        steps = right // tile
        for t in terms:
            ins.append(pl.BlockSpec((rows, bw), lambda b, s, r=t[1]: (r(), block(b))))
            ins.append(pl.BlockSpec((rows, tile), lambda b, s, r=t[3]: (r(), s)))
        out_dims, slot = (ns, bw // ns, right), (ns, bw // ns, tile)
    else:
        bw = right // nd
        tile = pick_tile(left)
        steps = left // tile
        for t in terms:
            ins.append(pl.BlockSpec((rows, tile), lambda b, s, r=t[1]: (r(), s)))
            ins.append(pl.BlockSpec((rows, bw), lambda b, s, r=t[3]: (r(), block(b))))
        out_dims, slot = (ns, left, bw // ns), (ns, tile, bw // ns)
    work = 2e-9 * nt * rows * left * right / nd
    operands = [v for t in terms for v in (t[0], t[2])]
    operands[0] = after(operands[0], *behind)
    return pl.pallas_call(
        functools.partial(
            wgrad_send_kernel, nt=nt, row_type=row_type, ns=ns, steps=steps, tile=tile
        ),
        grid=(2, steps),
        in_specs=ins,
        out_specs=pl.BlockSpec(memory_space=pl.ANY),
        scratch_shapes=[
            pltpu.VMEM((2, *slot), BF), pltpu.SemaphoreType.DMA((2,)), pltpu.SemaphoreType.DMA,
        ],
        out_shape=sds((2, *out_dims), BF),
        compiler_params=params(collective_id=ident, has_side_effects=True),
        cost_estimate=cost(O('c_ws', 1.0) * (2 + 3.4 * work)),
        name="wgrad_send",
    )(*operands)


class Shrink:
    def __init__(self, terms, row_type, ahead=None, small=False, *, nd, ns, rows):
        self.small, self.pair = small, None
        self.args, self.nd = (terms, row_type), nd
        self.ahead = ahead
        self.ident = ahead.ident + 1 if ahead else 0
        self.sizes = (nd, ns, rows)
        self.d = lax.axis_index("dp")

    def make(self, blocks, adds, behind, **more):
        terms, row_type = self.args
        return wgrad(terms, blocks, adds, row_type, *self.sizes, behind, **more)

    def send(self, *behind):
        terms, row_type = self.args
        self.got = wgrad_send(terms, row_type, *self.sizes, self.ident, behind)
        return self.got

    def far(self, *behind):
        out = self.make([self.d ^ 2], [(self.got, 1)], behind)
        first = self.ahead
        for _ in range(O('serial', 1)):
            first = first.ahead if first else None
        first = [first.come] if first and first.pair is None and O('serial', 1) < 3 else []
        self.come = lax.ppermute(
            after(out, *first), "dp", [(k, k ^ 2) for k in range(self.nd)]
        )
        return out

    def both(self, *behind):
        out = self.make([self.d, self.d ^ 2], [(self.got, None)], behind, seq_first=True)
        self.pair = lax.psum_scatter(out, "seq", scatter_dimension=0)
        return out

    def near(self, *behind):
        self.here = self.make([self.d], [(self.got, 0), (self.come, 0)], behind)
        if not self.small:
            self.share = lax.psum_scatter(self.here[0], "seq", scatter_dimension=0)
        return self.here

    def finish(self):
        if self.pair is not None:
            come = lax.ppermute(self.pair[1], "dp", [(k, k ^ 2) for k in range(self.nd)])
            return self.pair[0].astype(F32) + come.astype(F32)
        if not self.small:
            return self.share.astype(F32)
        z, ns = lax.axis_index("seq"), self.sizes[1]
        piece = lambda j: lax.dynamic_index_in_dim(self.here[0], j, 0, keepdims=False)
        first = jnp.stack([piece(z ^ 1), piece(z ^ 3)])
        first = lax.ppermute(first, "seq", [(k, k ^ 1) for k in range(ns)]).astype(F32)
        second = (piece(z ^ 2).astype(F32) + first[1]).astype(BF)
        second = lax.ppermute(second, "seq", [(k, k ^ 2) for k in range(ns)])
        return piece(z).astype(F32) + first[0] + second.astype(F32)


def final_kernel(x_ref, ga_ref, gb_ref, h0_ref, h1_ref, gain_ref, s_ref, out_ref):
    x = x_ref[...].astype(F32)
    inv = rms(x)
    n1 = x * inv
    g1 = (ga_ref[...].astype(F32) + gb_ref[...].astype(F32)) * gain_ref[...]
    gh = jnp.where(s_ref[0] == 0, h0_ref[...].astype(F32), h1_ref[...].astype(F32))
    out_ref[...] = (gh + inv * (g1 - n1 * jnp.mean(g1 * n1, axis=1, keepdims=True))).astype(BF)


def final(x, ga, gb, h0, h1, gain, y, tm):
    rows, d = x.shape
    tile = pl.BlockSpec((tm, d), lambda i: (i, 0))
    return pl.pallas_call(
        final_kernel,
        grid=(rows // tm,),
        in_specs=[tile] * 5 + [fixed((1, d)), pl.BlockSpec(memory_space=pltpu.SMEM)],
        out_specs=tile,
        out_shape=sds((rows, d), BF),
        compiler_params=params(),
        cost_estimate=cost(O('c_fin', 1.0) * 8),
        name="final",
    )(x, ga, gb, h0, h1, gain, jnp.reshape(y, (1,)))


def per_device(
    tokens, doc_lengths, w_query, w_key, w_value, w_out, w_gate, w_up, w_down,
    norm_attn, norm_mlp, query_norm, key_norm, cotangent, *, nd, ns, nt,
):
    tokens, cotangent = tokens[0], cotangent[0]
    own_rows, d = tokens.shape
    span = own_rows * nt
    rows = span // 2
    heads_kv = w_key.shape[1] // HD
    gs = w_query.shape[1] // w_key.shape[1]
    z, y = lax.axis_index("seq"), lax.axis_index("tensor")
    row = lambda v: v[None, :]
    tm = 256
    tq = tk = 512
    swap = lambda v: lax.ppermute(v, "tensor", [(0, 1), (1, 0)])
    pick = lambda a, b: jnp.where(y == 0, a, b)

    back = min(ns - 1, -(-(LONGEST - 1) // span))
    window = (back + 1) * span
    ends = jnp.cumsum(doc_lengths[0])
    positions = z * span + jnp.arange(span, dtype=jnp.int32)
    starts = jnp.max(jnp.where(ends[None, :] <= positions[:, None], ends[None, :], 0), axis=1)
    half = HD // 2
    inverse = rope_base ** (-(jnp.arange(half, dtype=F32) * 2.0 / HD))
    angles = (positions - starts).astype(F32)[:, None] * inverse[None, :]
    cosine = jnp.tile(jnp.cos(angles), (1, 2))
    sine = jnp.sin(angles)
    sine = jnp.concatenate([-sine, sine], axis=1)
    rel = jnp.clip(starts - (z - back) * span, 0, window - 1)
    starts_col = jnp.broadcast_to(rel[:, None], (span, HD))
    starts_row = jnp.broadcast_to(rel[None, :], (8, span))

    def bounds(first_row, count, w0, w1, tk=tk):
        heads = rel[first_row : first_row + count : tq]
        tails = rel[first_row + tq - 1 : first_row + count : tq]
        at = window - span + first_row + tq * jnp.arange(count // tq, dtype=jnp.int32)
        inside = lambda v: jnp.clip(v - w0, 0, w1 - w0)
        up = lambda v: (v + tk - 1) // tk
        return [inside(heads) // tk, up(inside(at + tq)), up(inside(tails)), inside(at + 1) // tk]

    if nt == 2:
        other = swap(tokens)
        cot_in, other = lax.optimization_barrier((cotangent, other))
        cot_other = swap(cot_in)
        pieces, bases = [tokens, other], [y * rows, (1 - y) * rows]
        cot = jnp.concatenate([pick(cotangent, cot_other), pick(cot_other, cotangent)], axis=0)
    else:
        everything = lax.all_gather(tokens, "tensor", axis=0, tiled=True)
        cot = lax.all_gather(cotangent, "tensor", axis=0, tiled=True)
        pieces, bases = [everything[:rows], everything[rows:]], [0, rows]
    bases = [jnp.asarray(b, jnp.int32) for b in bases]
    base_tiles = [b // tm for b in bases]

    segs, seg_bases = [[] for _ in range(back + 1)], [[] for _ in range(back + 1)]
    raws = []
    ahead = [(k, k + 1) for k in range(ns - 1)]
    for x_piece, base, base_tile in zip(pieces, bases, base_tiles):
        if raws and O('e_kv_hop'):
            base_tile = after(base_tile, segs[1][0])
        kv, raw = project_kv(
            x_piece, base_tile, row(norm_attn), w_key, w_value, cosine, sine, row(key_norm), tm
        )
        raws.append(raw)
        for hop in range(back + 1):
            segs[hop].append(kv)
            seg_bases[hop].append((back - hop) * span + base)
            if hop < back:
                kv = lax.ppermute(kv, "seq", ahead)
    x_all, attn_in, query, q_raw = project_q(
        pieces[0], pieces[1], jnp.stack(base_tiles), row(norm_attn), w_query, cosine, sine,
        row(query_norm), tm,
    )

    attend = functools.partial(flash_fwd, bounds, gs=gs, tq=tq, window=window)
    prior = []
    for hop in range(back):
        part = ((back - hop) * span, (back - hop + 1) * span)
        prior = attend(
            seg_bases[hop], query, starts_col, segs[hop], prior, part=part, row_at=0, rows=span,
            last=False, tk=tk if hop == 0 else min(span, 2 * tk),
        )
    outs, sums, parts = [], [], []
    for c in range(2):
        out, total = attend(
            seg_bases[back], query, after(starts_col, *[v[0] for v in parts]), segs[back], prior, part=(0, span),
            row_at=c * rows, rows=rows, last=True, tk=tk,
        )
        outs.append(out)
        sums.append(total)
        partial = dot(out, w_out).astype(BF)
        parts.append([partial, swap(partial)] if nt == 2 else [lax.psum(partial, "tensor")])

    grad_hidden = dot(after(cot, partial), w_down, 1, 1).astype(BF)
    low_mlp, hidden, d_gate, d_up, grads = [], [], [], [], []
    tf = min(512, w_gate.shape[1] // 2)
    for c in range(2):
        m, h, dg, du, gm = mlp(
            x_all, parts[c], grad_hidden, after(row(norm_mlp), *low_mlp), w_gate, w_up, c, tf
        )
        low_mlp.append(m)
        hidden.append(h)
        d_gate.append(dg)
        d_up.append(du)
        grads.append([gm, swap(gm)] if nt == 2 else [lax.psum(gm, "tensor")])

    shrink = functools.partial(Shrink, nd=nd, ns=ns, rows=rows)
    zero = lambda: 0
    chunk = lambda c: lambda: c
    down = shrink([(hidden[c], zero, cot, chunk(c)) for c in range(2)], False, None, bool(O('p_down')))
    gate = shrink([(low_mlp[c], zero, d_gate[c], zero) for c in range(2)], True, down, bool(O('p_gate')))
    up = shrink([(low_mlp[c], zero, d_up[c], zero) for c in range(2)], True, gate, bool(O('p_up')))
    gh, g_att, g_norm_two = [], [], []

    def middle(c, *behind):
        low, ga, gn = mid_backward(
            x_all, parts[c], grads[c], cot, after(row(norm_mlp), *behind), w_out, c, tm
        )
        gh.append(low)
        g_att.append(ga)
        g_norm_two.append(gn)
        return low

    opt = lambda k, *v: list(v) if O(k) else []
    down.send()
    middle(0, *opt('e_m0_ds', down.got))
    zf = bool(O('zf'))
    df = down.both(*opt('e_df_m0', gh[0])) if zf else down.far(*opt('e_df_m0', gh[0]))
    gs_out = gate.send(*opt('e_gs_df', df), *opt('e_gs_m0', gh[0]))
    gf = gate.far() if O('e_gf_early') else None
    middle(1, *opt('e_m1_m0', gh[0]), *opt('e_m1_gs', gs_out), *opt('e_m1_gf', *([gf] if gf is not None else [])))
    if gf is None:
        gf = gate.far(gh[1])
    t = opt('e_fb0_gf', gf)
    hop_segs = [v for seg in segs for v in seg]
    hop_bases = jnp.stack([v for b in seg_bases for v in b])
    scalars = jnp.concatenate([*bounds(0, span, 0, window), hop_bases])
    halves = [(0, heads_kv)] if heads_kv == 1 else [(0, heads_kv // 2), (heads_kv // 2, heads_kv // 2)]
    behind = [(k + 1, k) for k in range(ns - 1)]
    dqs, dkvs, first_hops = [], [], []
    for part, heads in enumerate(halves):
        dq, *dkv = flash_bwd(
            after(scalars, *t), query, starts_row, g_att, outs, sums, hop_segs, window, gs, tq, tk,
            heads,
        )
        come = None
        for b in range(back):
            send = dkv[b]
            if come is not None:
                send = (send.astype(F32) + come.astype(F32)).astype(BF)
            come = lax.ppermute(send, "seq", behind)
            first_hops += [come] if b == 0 else []
        dqs.append(dq)
        dkvs.append([dkv[back]] + ([come] if come is not None else []))
        if part == 0:
            dn = dq if zf else down.near(*opt('e_dn_d0', dq))
            us = up.send(dq)
            t = opt('e_fb1_dn', dn) + opt('e_fb1_us', us) + opt('e_fb1_gf', gf)
            if O('e_fb1_uf'):
                uf = up.far()
                t += [uf]
    out_w = shrink([(outs[c], zero, gh[c], zero) for c in range(2)], False, up, bool(O('p_out',1)))
    if not O('e_fb1_uf'):
        uf = up.far(dqs[-1], *opt('e_uf_h0', first_hops[0] if first_hops else dqs[0]))
    gn_ = gate.near(*opt('e_gn_d1', dqs[-1]), *opt('e_gn_uf', uf), *opt('e_gn_hop', *first_hops), *opt('e_gn_h0', first_hops[0] if first_hops else dqs[0]))
    dq_low, g_qn = q_back(
        dqs, q_raw, cosine, sine,
        after(row(query_norm), *opt('e_qb_uf', uf), *opt('e_qb_gn', gn_), *opt('e_qb_hop', *first_hops), *opt('e_qb_h0', first_hops[0] if first_hops else dqs[0])), tm,
    )
    query_w = shrink([(attn_in, chunk(c), dq_low, chunk(c)) for c in range(2)], True, out_w, bool(O('p_q',1)))
    os_ = out_w.send(dq_low, *opt('e_os_gn', gn_))
    qs_ = query_w.send(*opt('e_qs_os', os_))
    of_ = out_w.far(*opt('e_of_qs', qs_))
    qf_ = query_w.far(*opt('e_qf_of', of_))
    w_down_later = after(w_down, dq_low) if O('e_dp_q') else after(w_down, gh[1]) if O('e_dp_m') else w_down
    downs = [dot(hidden[c], w_down_later).astype(BF) for c in range(2)]
    come_down = swap(pick(downs[1], downs[0])) if nt == 2 else downs[0]
    un = up.near(*opt('e_un_qf', qf_), *opt('e_un_d1', dqs[-1]), *opt('e_un_dp', *downs), *opt('e_un_of', of_))
    t = opt('e_in_qf', qf_) + opt('e_in_dp', *downs) + opt('e_in_cd', come_down) + opt('e_in_un', un)

    lows, gas, g_kn, g_norm_one = [None] * 2, [None] * 2, [], []
    for n in (1, 0):
        lows[n], gas[n], gain_part, norm_part = in_back(
            dkvs, raws[n], dq_low, x_all, base_tiles[n], cosine, sine, after(row(key_norm), *t),
            w_query, w_key, w_value, tm,
        )
        g_kn.append(gain_part)
        g_norm_one.append(norm_part)
    kv_cut = heads_kv * HD
    own_half = lambda: lax.axis_index("tensor")
    half_of = lambda n: chunk(n) if nt != 2 else own_half if n == 0 else lambda: 1 - own_half()
    kv_w = shrink([(attn_in, half_of(n), lows[n], zero) for n in range(2)], True, query_w, bool(O('p_kv',1)))
    ks_ = kv_w.send(*opt('e_ks_un', un))
    kf_ = kv_w.far(*opt('e_kf_un', un))
    on_ = out_w.near(*opt('e_on_kf', kf_))
    qn_ = query_w.near(*opt('e_qn_on', on_))
    gain_last = after(row(norm_attn), *opt('e_fin_qn', qn_), *opt('e_fin_kf', kf_), *opt('e_fin_on', on_))

    up32 = lambda v: v.astype(F32)
    if nt == 2:
        result = up32(tokens) + up32(pick(downs[0], downs[1])) + up32(come_down)
        for n in range(2):
            result = result + up32(pick(parts[0][n], parts[1][n]))
        grad_tokens = final(tokens, gas[0], swap(gas[1]), gh[0], gh[1], gain_last, y, tm)
    else:
        scatter = lambda v: lax.psum_scatter(v, "tensor", scatter_dimension=0, tiled=True)
        mine = lambda pair: lax.dynamic_slice_in_dim(
            jnp.concatenate(pair, axis=0), y * own_rows, own_rows
        )
        result = up32(tokens) + up32(scatter(jnp.concatenate(downs, axis=0)))
        result = result + up32(mine([parts[0][0], parts[1][0]]))
        x32 = up32(tokens)
        inv = rms(x32)
        n1 = x32 * inv
        g1 = up32(scatter(jnp.concatenate(gas, axis=0))) * row(norm_attn)
        moved = inv * (g1 - n1 * jnp.mean(g1 * n1, axis=1, keepdims=True))
        grad_tokens = (up32(mine(gh)) + moved).astype(BF)
    kn_ = kv_w.near(*opt('e_kn_fin', grad_tokens))
    g_down, g_gate, g_up, g_out, g_query, g_kv = [
        v.finish() for v in (down, gate, up, out_w, query_w, kv_w)
    ]

    share = 1.0 / nt
    fold = lambda pair: jnp.sum(pair[0] + pair[1], axis=0)
    axes = (("dp", nd), ("seq", ns), ("tensor", nt))
    packed = jnp.concatenate(
        [fold(g_norm_one), fold(g_norm_two) * share, jnp.sum(g_qn, axis=0), fold(g_kn)]
    )
    packed = total_sum(after(packed, *opt('e_pk_fin', grad_tokens), *opt('e_pk_kf', kf_), *opt('e_pk_kn', kn_), *opt('e_pk_kc', kv_w.come)), axes)
    return (
        result.astype(BF)[None], grad_tokens[None], g_query, g_kv[:, :kv_cut], g_kv[:, kv_cut:],
        g_out, g_gate, g_up, g_down,
        packed[:d], packed[d : 2 * d], packed[2 * d : 2 * d + HD], packed[2 * d + HD :],
    )


def total_sum(v, sizes):
    for name, size in sizes:
        step = 1
        while step < size:
            come = lambda k: lax.ppermute(v, name, [(i, i ^ k * step) for i in range(size)])
            if 4 * step <= size:
                v = (v + come(1)) + (come(2) + come(3))
                step *= 4
            else:
                v = v + come(1)
                step *= 2
    return v


def solution(mesh):
    sizes = dict(nd=mesh.shape["dp"], ns=mesh.shape["seq"], nt=mesh.shape["tensor"])
    rows, cols, both = P("dp", ("seq", "tensor"), None), P(None, "tensor"), ("dp", "seq")
    return jax.shard_map(
        functools.partial(per_device, **sizes),
        mesh=mesh,
        in_specs=(
            rows, P("dp", None), cols, cols, cols, P("tensor", None), cols, cols, P("tensor", None),
            P(), P(), P(), P(), rows,
        ),
        out_specs=(
            rows, rows, P(both, "tensor"), P(both, "tensor"), P(both, "tensor"), P("tensor", both),
            P(both, "tensor"), P(both, "tensor"), P("tensor", both), P(), P(), P(), P(),
        ),
        check_vma=False,
    )
```
